32 devices in a mesh: img: 2 (over core), pix: 16 (over z, y, x).
Axes of the slice: x: 2, y: 2, z: 4, core: 2. Of those that a mesh axis runs over, the one named last changes fastest.
Arguments:
- latents: bfloat16 [2, 256, 1024], P('img'), may hold values from -6 to 6
- pixels: float32 [2, 3, 6144], P('img', None, 'pix'), may hold values from -5 to 5
- coords: int32 [2, 2, 6144], P('img', None, 'pix'), may hold values from 0 to 223, as said below
- kept_mask: int32 [2, 6144], P('img', 'pix'), may hold values from 0 to 1, as said below
- lat_gain: float32 [1024], replicated, may hold values from 0.1 to 1.9
- lat_shift: float32 [1024], replicated, may hold values from -3 to 3
- query_weight: bfloat16 [1024, 1024], replicated, may hold values from -0.1875 to 0.1875
- query_bias: float32 [1024], replicated, may hold values from -3 to 3
- in_gain: float32 [261], replicated, may hold values from 0.1 to 1.9
- in_shift: float32 [261], replicated, may hold values from -3 to 3
- key_weight: bfloat16 [261, 1024], replicated, may hold values from -0.75 to 0.75
- value_weight: bfloat16 [261, 1024], replicated, may hold values from -2.023352 to 2.023352
- value_bias: float32 [1024], replicated, may hold values from -4 to 4
- mlp_gain: float32 [1024], replicated, may hold values from 0.1 to 1.9
- mlp_shift: float32 [1024], replicated, may hold values from -3 to 3
- up_weight: bfloat16 [1024, 1024], replicated, may hold values from -0.1875 to 0.1875
- up_bias: float32 [1024], replicated, may hold values from -3 to 3
- down_weight: bfloat16 [1024, 1024], replicated, may hold values from -0.1875 to 0.1875
- down_bias: float32 [1024], replicated, may hold values from -3 to 3
- cotangent: bfloat16 [2, 256, 1024], P('img'), may hold values from -6 to 6
Outputs:
- encoded: bfloat16 [2, 256, 1024], P('img')
- latent_grad: float32 [2, 256, 1024], P('img')
- pixel_grad: float32 [2, 3, 6144], P('img', None, 'pix')
- lat_gain_grad: float32 [1024], replicated
- lat_shift_grad: float32 [1024], replicated
- query_weight_grad: float32 [1024, 1024], replicated
- query_bias_grad: float32 [1024], replicated
- in_gain_grad: float32 [261], replicated
- in_shift_grad: float32 [261], replicated
- key_weight_grad: float32 [261, 1024], replicated
- value_weight_grad: float32 [261, 1024], replicated
- value_bias_grad: float32 [1024], replicated
- mlp_gain_grad: float32 [1024], replicated
- mlp_shift_grad: float32 [1024], replicated
- up_weight_grad: float32 [1024, 1024], replicated
- up_bias_grad: float32 [1024], replicated
- down_weight_grad: float32 [1024, 1024], replicated
- down_bias_grad: float32 [1024], replicated
The draws below stay inside these ranges and needn't reach their ends.
Inputs may be any that keep to these rules, and one draw needn't show every extreme that they name: `coords`: for each image the pixels are distinct cells of a 224 x 224 grid in row-major order, given as (row, column); the first and the last cell of the grid are always among them. `kept_mask`: exactly half of each image's pixels are kept; dropped keys cluster in square patches of 16 x 16 grid cells, with a share that varies by patch row.
All inputs are finite; a program needn't handle non-finite values.
Results may differ from the reference program's by a relative error of at most 0.017.
The reference program's roundings to bfloat16 on the way count: a program that leaves them out, or rounds other values in their place, can miss the bound.
Values may be sent and summed in bfloat16 or wider, within the bound.
No kernel may reach another device: no remote copies, remote signals or barrier semaphores. Data moves between devices by JAX's collectives and lax.ppermute only.
A program may use at most 128 MiB of HBM per device.

```python
import math
import jax
import jax.numpy as jnp
from jax import lax

D = 1024
BANDS = 64
CIN = 261
NLAT = 256
GRID = 224
IMGS = 2
PIXELS = 6144


def grid_flat(key):
    chosen = []
    for picture in range(IMGS):
        image_key = jax.random.fold_in(jax.random.fold_in(key, 7301), picture)
        middle = jax.random.permutation(image_key, GRID * GRID - 2)[:PIXELS - 2] + 1
        all_cells = jnp.concatenate([jnp.zeros((1,), jnp.int32), middle.astype(jnp.int32), jnp.full((1,), GRID * GRID - 1, jnp.int32)])
        chosen.append(jnp.sort(all_cells))
    return jnp.stack(chosen)


def draw_coords(key, part):
    flat_cells = grid_flat(key)
    return jnp.stack([flat_cells // GRID, flat_cells % GRID], axis=1).astype(jnp.int32)


def draw_kept_mask(key, part):
    flat_cells = grid_flat(key)
    rows_at = flat_cells // GRID
    cols_at = flat_cells % GRID
    patches = (GRID + 15) // 16
    mask_rows = []
    for picture in range(IMGS):
        image_key = jax.random.fold_in(jax.random.fold_in(key, 7302), picture)
        level_key, patch_key, pixel_key, tie_key = jax.random.split(image_key, 4)
        drop_level = jax.random.randint(level_key, (patches,), 0, 8)
        patch_draw = jax.random.randint(patch_key, (patches * patches,), 0, 10)
        pixel_draw = jax.random.randint(pixel_key, (PIXELS,), 0, 4)
        tie_rank = jax.random.permutation(tie_key, PIXELS).astype(jnp.int32)
        patch_row = rows_at[picture] // 16
        patch_index = patch_row * patches + cols_at[picture] // 16
        coarse = patch_draw[patch_index] - drop_level[patch_row] + 8
        priority = (coarse * 4 + pixel_draw) * PIXELS + tie_rank
        ordering = jnp.argsort(-priority)
        rank_of = jnp.zeros((PIXELS,), jnp.int32).at[ordering].set(jnp.arange(PIXELS, dtype=jnp.int32))
        mask_rows.append(jnp.where(rank_of < PIXELS // 2, 1, 0).astype(jnp.int32))
    return jnp.stack(mask_rows)


def draw_value_weight(key, part):
    own_key = jax.random.fold_in(key, 7303)
    raw_draw = jnp.clip(jax.random.normal(own_key, (CIN, D), jnp.float32), -4.0, 4.0)
    return (raw_draw * math.sqrt(PIXELS / (92.0 * CIN))).astype(jnp.bfloat16)


def block_scale(stream_key, shape, shards, smallest, top_value):
    loudness, own = 1.0, jax.random.fold_in(stream_key, 6)
    for axis_at, shards_of in shards:
        steps = jnp.exp(jax.random.uniform(jax.random.fold_in(own, axis_at), (shards_of,), jnp.float32, smallest / len(shards), top_value / len(shards)))
        loudness = loudness * jnp.repeat(steps, shape[axis_at] // shards_of).reshape([-1 if axis == axis_at else 1 for axis in range(len(shape))])
    return loudness


def gaussian(rng, extent, spread, limit, cuts=(), kind=jnp.bfloat16):
    result = spread * jax.random.normal(rng, extent, jnp.float32)
    if cuts:
        result = result * block_scale(rng, extent, cuts, -0.22, 0.18)
    return jnp.clip(result, -limit, limit).astype(kind)


def setup_inputs(seed: int = 0) -> dict:
    streams_of = jax.random.split(jax.random.key(seed), 21)
    latents = gaussian(streams_of[0], (IMGS, NLAT, D), 1.0, 6.0, ((0, 2),))
    pixels = gaussian(streams_of[1], (IMGS, 3, PIXELS), 1.0, 5.0, ((0, 2), (2, 16)), jnp.float32)
    coords = draw_coords(jax.random.fold_in(streams_of[20], 71), 0)
    kept_mask = draw_kept_mask(jax.random.fold_in(streams_of[20], 71), 0)
    lat_gain = jnp.clip(1.0 + 0.18 * jax.random.normal(streams_of[4], (D,), jnp.float32), 0.1, 1.9)
    lat_shift = gaussian(streams_of[5], (D,), 0.5, 3.0, (), jnp.float32)
    query_weight = gaussian(streams_of[6], (D, D), D ** -0.5, 0.1875)
    query_bias = gaussian(streams_of[7], (D,), 0.5, 3.0, (), jnp.float32)
    in_gain = jnp.clip(1.0 + 0.18 * jax.random.normal(streams_of[8], (CIN,), jnp.float32), 0.1, 1.9)
    in_shift = gaussian(streams_of[9], (CIN,), 0.5, 3.0, (), jnp.float32)
    key_weight = gaussian(streams_of[10], (CIN, D), (CIN // 4) ** -0.5, 0.75)
    value_weight = draw_value_weight(jax.random.fold_in(streams_of[20], 71), 0)
    value_bias = gaussian(streams_of[12], (D,), 1.0, 4.0, (), jnp.float32)
    mlp_gain = jnp.clip(1.0 + 0.18 * jax.random.normal(streams_of[13], (D,), jnp.float32), 0.1, 1.9)
    mlp_shift = gaussian(streams_of[14], (D,), 0.5, 3.0, (), jnp.float32)
    up_weight = gaussian(streams_of[15], (D, D), D ** -0.5, 0.1875)
    up_bias = gaussian(streams_of[16], (D,), 0.5, 3.0, (), jnp.float32)
    down_weight = gaussian(streams_of[17], (D, D), D ** -0.5, 0.1875)
    down_bias = gaussian(streams_of[18], (D,), 0.5, 3.0, (), jnp.float32)
    cotangent = gaussian(streams_of[19], (IMGS, NLAT, D), 1.0, 6.0, ((0, 2),))
    return {"latents": latents, "pixels": pixels, "coords": coords, "kept_mask": kept_mask, "lat_gain": lat_gain, "lat_shift": lat_shift, "query_weight": query_weight, "query_bias": query_bias, "in_gain": in_gain, "in_shift": in_shift, "key_weight": key_weight, "value_weight": value_weight, "value_bias": value_bias, "mlp_gain": mlp_gain, "mlp_shift": mlp_shift, "up_weight": up_weight, "up_bias": up_bias, "down_weight": down_weight, "down_bias": down_bias, "cotangent": cotangent}


@jax.custom_vjp
def low(v):
    return lax.optimization_barrier(v.astype(jnp.bfloat16)).astype(jnp.float32)

@jax.custom_vjp
def low_back(v):
    return v

def low_keep(v):
    return (low(v), None)

def low_pass(kept, grad):
    return (grad,)

def back_keep(v):
    return (v, None)

def back_low(kept, grad):
    return (low(grad),)
low.defvjp(low_keep, low_pass)
low_back.defvjp(back_keep, back_low)
EPSILON = 1e-05
HIGHEST = lax.Precision.HIGHEST

def norm_axis(values, gain_vec, shift_vec, axis_pos):
    centre = values - lax.optimization_barrier(jnp.mean(values, axis=axis_pos, keepdims=True))
    spread_sq = lax.optimization_barrier(jnp.mean(centre * centre, axis=axis_pos, keepdims=True))
    return centre * lax.rsqrt(spread_sq + EPSILON) * gain_vec + shift_vec

def fourier_table(colors, grid_pos):
    position = grid_pos.astype(jnp.float32) * (2.0 / (GRID - 1)) - 1.0
    frequency = 1.0 + jnp.arange(BANDS, dtype=jnp.float32) * ((GRID / 2.0 - 1.0) / (BANDS - 1))
    phases = (position[:, None, :] * (math.pi * frequency)[None, :, None]).reshape(2 * BANDS, position.shape[1])
    return jnp.concatenate([colors, position, jnp.sin(phases), jnp.cos(phases)], axis=0)

def image_forward(latent, colors, grid_pos, kept, weights):
    lat_gain, lat_shift, query_weight, query_bias, in_gain, in_shift, key_weight, value_weight, value_bias, mlp_gain, mlp_shift, up_weight, up_bias, down_weight, down_bias = weights
    norm_one = low(norm_axis(latent, lat_gain, lat_shift, 1))
    query = low(low_back(jnp.dot(norm_one, query_weight, precision=HIGHEST) + query_bias))
    table = low(fourier_table(colors, grid_pos))
    x_in = low(norm_axis(table, in_gain[:, None], in_shift[:, None], 0))
    keys = low(low_back(jnp.dot(x_in.T, key_weight, precision=HIGHEST)))
    values = low(low_back(jnp.dot(x_in.T, value_weight, precision=HIGHEST) + value_bias))
    score = low_back(jnp.dot(query, keys.T, precision=HIGHEST) * (1.0 / math.sqrt(D)))
    live_mask = (kept > 0)[None, :]
    row_top = lax.optimization_barrier(jnp.max(jnp.where(live_mask, score, -1e+30), axis=1, keepdims=True))
    weight = jnp.where(live_mask, jnp.exp(score - row_top), 0.0)
    attn = jnp.dot(weight, values, precision=HIGHEST) / lax.optimization_barrier(jnp.sum(weight, axis=1, keepdims=True))
    mixed = latent + low_back(attn)
    norm_two = low(norm_axis(mixed, mlp_gain, mlp_shift, 1))
    pre_act = low_back(jnp.dot(norm_two, up_weight, precision=HIGHEST) + up_bias)
    hidden = low(jax.nn.gelu(pre_act, approximate=False))
    return mixed + jnp.dot(hidden, down_weight, precision=HIGHEST) + down_bias

def reference(latents, pixels, coords, kept_mask, lat_gain, lat_shift, query_weight, query_bias, in_gain, in_shift, key_weight, value_weight, value_bias, mlp_gain, mlp_shift, up_weight, up_bias, down_weight, down_bias, cotangent):
    weights = tuple((member.astype(jnp.float32) for member in (lat_gain, lat_shift, query_weight, query_bias, in_gain, in_shift, key_weight, value_weight, value_bias, mlp_gain, mlp_shift, up_weight, up_bias, down_weight, down_bias)))

    def forward(latent_all, pixel_all, params):
        return jnp.stack([image_forward(latent_all[picture], pixel_all[picture], coords[picture], kept_mask[picture], params) for picture in range(IMGS)])
    encoded, pullback = jax.vjp(forward, latents.astype(jnp.float32), pixels, weights)
    latent_grad, pixel_grad, grads = pullback(cotangent.astype(jnp.float32))
    return (encoded.astype(jnp.bfloat16), latent_grad, pixel_grad, grads[0], grads[1], grads[2], grads[3], grads[4], grads[5], grads[6], grads[7], grads[8], grads[9], grads[10], grads[11], grads[12], grads[13], grads[14])
```

```python
import math

import jax
import jax.numpy as jnp
import numpy as np
from jax import lax
from jax.sharding import PartitionSpec as P

BANDS = 64
GRID = 224
EPSILON = 1e-05
FLOOR = -1e30
BLOCK = 16
BF = jnp.bfloat16
F32 = jnp.float32


def fourier_lookup():
    position = np.arange(GRID, dtype=np.float32) * np.float32(2.0 / (GRID - 1)) - np.float32(1.0)
    frequency = np.float32(1.0) + np.arange(BANDS, dtype=np.float32) * np.float32(
        (GRID / 2.0 - 1.0) / (BANDS - 1)
    )
    phases = position[None, :] * (np.float32(math.pi) * frequency)[:, None]
    waves = np.concatenate([np.sin(phases.astype(np.float64)), np.cos(phases.astype(np.float64))])
    return waves.astype(np.float32)


def contract(left, right, left_dim, right_dim):
    return lax.dot_general(
        left, right, (((left_dim,), (right_dim,)), ((), ())), preferred_element_type=F32
    )


def norm_stats(values, axis):
    centre = values - jnp.mean(values, axis=axis, keepdims=True)
    spread = lax.rsqrt(jnp.mean(centre * centre, axis=axis, keepdims=True) + EPSILON)
    return centre * spread, spread


def norm_back(upstream, gain, unit, spread, axis):
    inner = upstream * gain
    return spread * (
        inner
        - jnp.mean(inner, axis=axis, keepdims=True)
        - unit * jnp.mean(inner * unit, axis=axis, keepdims=True)
    )


def shards(
    latents,
    pixels,
    coords,
    kept_mask,
    lat_gain,
    lat_shift,
    query_weight,
    query_bias,
    in_gain,
    in_shift,
    key_weight,
    value_weight,
    value_bias,
    mlp_gain,
    mlp_shift,
    up_weight,
    up_bias,
    down_weight,
    down_bias,
    cotangent,
):
    pix = lax.axis_size("pix")
    mine = lax.axis_index("pix")
    own = pixels.shape[2]
    packed = jnp.concatenate(
        [
            pixels[0].astype(BF),
            coords[0].astype(BF),
            kept_mask.astype(BF),
            jnp.zeros((2, own), BF),
        ],
        axis=0,
    )
    gathered = lax.all_to_all(jnp.broadcast_to(packed[None], (pix,) + packed.shape), "pix", 0, 0)
    every = gathered.transpose(1, 0, 2).reshape(packed.shape[0], pix * own)
    swap = [(0, 1), (1, 0)]

    def other(value):
        return lax.ppermute(value, "img", swap)

    root = math.sqrt(latents.shape[2])
    latent = latents[0].astype(F32)
    lat_unit, lat_spread = norm_stats(latent, 1)
    norm_one = (lat_unit * lat_gain + lat_shift).astype(BF)
    query = (jnp.dot(norm_one, query_weight, preferred_element_type=F32) + query_bias).astype(BF)
    absorbed = (contract(query, key_weight, 1, 1) * (1.0 / root)).astype(BF)

    waves = jnp.asarray(fourier_lookup(), BF)
    places = jnp.arange(GRID, dtype=F32)[:, None]

    def features(part):
        cells = part[3:5].astype(F32)
        position = (cells * (2.0 / (GRID - 1)) - 1.0).astype(BF)
        row_waves = jnp.dot(waves, (cells[0:1] == places).astype(BF), preferred_element_type=F32).astype(BF)
        col_waves = jnp.dot(waves, (cells[1:2] == places).astype(BF), preferred_element_type=F32).astype(BF)
        table = jnp.concatenate(
            [part[0:3], position, row_waves[:BANDS], col_waves[:BANDS], row_waves[BANDS:], col_waves[BANDS:]],
            axis=0,
        ).astype(F32)
        unit, spread = norm_stats(table, 0)
        x_in = (unit * in_gain[:, None] + in_shift[:, None]).astype(BF)
        score = jnp.dot(absorbed, x_in, preferred_element_type=F32)
        return unit, spread, x_in, jnp.where(part[5:6] > 0, score, FLOOR), part[5:6] > 0

    def pool(part, feats):
        unit, spread, x_in, score, live = feats
        top = jnp.max(score, axis=1, keepdims=True)
        weight = jnp.where(live, jnp.exp(score - top), 0.0)
        return top, jnp.sum(weight, axis=1, keepdims=True), contract(weight.astype(BF), x_in, 1, 1)

    blocks = max(1, pix // BLOCK)
    parts = every.reshape(packed.shape[0], blocks, -1).transpose(1, 0, 2)
    if blocks == 1:
        feats = features(parts[0])
        row_top, row_total, pooled = pool(parts[0], feats)
    else:

        def merge(carry, part):
            top, total, sums = pool(part, features(part))
            new_top = jnp.maximum(carry[0], top)
            old_scale, new_scale = jnp.exp(carry[0] - new_top), jnp.exp(top - new_top)
            return (
                new_top,
                carry[1] * old_scale + total * new_scale,
                carry[2] * old_scale + sums * new_scale,
            ), None

        start = (
            jnp.full((latent.shape[0], 1), FLOOR, F32),
            jnp.zeros((latent.shape[0], 1), F32),
            jnp.zeros((latent.shape[0], in_gain.shape[0]), F32),
        )
        row_top, row_total, pooled = lax.scan(merge, start, parts)[0]
    pooled = pooled / row_total
    pooled_low = pooled.astype(BF)
    attn = jnp.dot(pooled_low, value_weight, preferred_element_type=F32) + value_bias
    mixed = latent + attn
    mix_unit, mix_spread = norm_stats(mixed, 1)
    norm_two = (mix_unit * mlp_gain + mlp_shift).astype(BF)
    pre_act = jnp.dot(norm_two, up_weight, preferred_element_type=F32) + up_bias
    half_erf = 0.5 * (1.0 + lax.erf(pre_act * (1.0 / math.sqrt(2.0))))
    hidden = (pre_act * half_erf).astype(BF)
    encoded = (
        mixed + jnp.dot(hidden, down_weight, preferred_element_type=F32) + down_bias
    ).astype(BF)

    out_grad = cotangent[0]
    out_grad_full = out_grad.astype(F32)
    hidden_grad = contract(out_grad, down_weight, 1, 1)
    slope = half_erf + pre_act * jnp.exp(-0.5 * pre_act * pre_act) * (1.0 / math.sqrt(2.0 * math.pi))
    pre_grad = (hidden_grad * slope).astype(BF)
    norm_two_grad = contract(pre_grad, up_weight, 1, 1)
    mixed_grad = out_grad_full + norm_back(norm_two_grad, mlp_gain, mix_unit, mix_spread, 1)
    attn_grad = mixed_grad.astype(BF)

    lifted = contract(attn_grad, value_weight, 1, 1).astype(BF)
    row_delta = jnp.sum(lifted.astype(F32) * pooled, axis=1, keepdims=True)

    def pull(part, feats):
        unit, spread, x_in, score, live = feats
        prob = jnp.where(live, jnp.exp(score - row_top), 0.0) / row_total
        score_grad = (prob * (jnp.dot(lifted, x_in, preferred_element_type=F32) - row_delta)).astype(BF)
        score_pool = contract(score_grad, x_in, 1, 1)
        x_in_grad = contract(absorbed, score_grad, 0, 0) + contract(lifted, prob.astype(BF), 0, 0)
        gain_part = jnp.sum(x_in_grad * unit, axis=1)
        shift_part = jnp.sum(x_in_grad, axis=1)
        colour_part = norm_back(x_in_grad, in_gain[:, None], unit, spread, 0)[:3]
        return score_pool, gain_part, shift_part, colour_part

    if blocks == 1:
        score_pool, in_gain_grad, in_shift_grad, all_colors = pull(parts[0], feats)
    else:

        def gather_up(carry, part):
            found = pull(part, features(part))
            return tuple(kept + new for kept, new in zip(carry, found[:3])), found[3]

        start = (
            jnp.zeros((latent.shape[0], in_gain.shape[0]), F32),
            jnp.zeros_like(in_gain),
            jnp.zeros_like(in_shift),
        )
        (score_pool, in_gain_grad, in_shift_grad), stacked = lax.scan(gather_up, start, parts)
        all_colors = stacked.transpose(1, 0, 2).reshape(3, -1)
    color_grad = lax.dynamic_slice(all_colors, (0, mine * own), (3, own))
    score_pool_low = score_pool.astype(BF)
    query_grad = (
        jnp.dot(score_pool_low, key_weight, preferred_element_type=F32) * (1.0 / root)
    ).astype(BF)
    norm_one_grad = contract(query_grad, query_weight, 1, 1)
    latent_grad = mixed_grad + norm_back(norm_one_grad, lat_gain, lat_unit, lat_spread, 1)

    def both(value):
        return jnp.concatenate([value, other(value)], axis=0)

    out_both = both(out_grad)
    hidden_both = both(hidden)
    two_both = both(norm_two)
    pre_both = both(pre_grad)
    attn_both = both(attn_grad)
    one_both = both(norm_one)
    query_both = both(query)
    query_grad_both = both(query_grad)
    pool_both = both(pooled_low)
    score_both = both(score_pool_low)
    wide = jnp.stack(
        [
            jnp.sum(norm_one_grad * lat_unit, axis=0),
            jnp.sum(norm_one_grad, axis=0),
            jnp.sum(norm_two_grad * mix_unit, axis=0),
            jnp.sum(norm_two_grad, axis=0),
        ]
    )
    narrow = jnp.stack([in_gain_grad, in_shift_grad])
    wide = wide + other(wide)
    narrow = narrow + other(narrow)
    return (
        encoded[None],
        latent_grad[None],
        color_grad[None],
        wide[0],
        wide[1],
        contract(one_both, query_grad_both, 0, 0),
        jnp.sum(query_grad_both.astype(F32), axis=0),
        narrow[0],
        narrow[1],
        contract(score_both, query_both, 0, 0) * (1.0 / root),
        contract(pool_both, attn_both, 0, 0),
        jnp.sum(attn_both.astype(F32), axis=0),
        wide[2],
        wide[3],
        contract(two_both, pre_both, 0, 0),
        jnp.sum(pre_both.astype(F32), axis=0),
        contract(hidden_both, out_both, 0, 0),
        jnp.sum(out_both.astype(F32), axis=0),
    )


def solution(mesh):
    lat = P("img", None, None)
    whole = P()
    return jax.shard_map(
        shards,
        mesh=mesh,
        in_specs=(lat, P("img", None, "pix"), P("img", None, "pix"), P("img", "pix"))
        + (whole,) * 15
        + (lat,),
        out_specs=(lat, lat, P("img", None, "pix")) + (whole,) * 15,
        check_vma=False,
    )
```

```python
import math

import jax
import jax.numpy as jnp
import numpy as np
from jax import lax
from jax.experimental import pallas as pl
from jax.experimental.pallas import tpu as pltpu
from jax.sharding import PartitionSpec as P

BANDS = 64
GRID = 224
EPSILON = 1e-05
FLOOR = -1e30
BLOCK = 16
LANES = 128
BF = jnp.bfloat16
F32 = jnp.float32
VM = pl.BlockSpec(memory_space=pltpu.VMEM)
ANY = pl.BlockSpec(memory_space=pl.ANY)
MIB = 1 << 20


def fourier_lookup():
    position = np.arange(GRID, dtype=np.float32) * np.float32(2.0 / (GRID - 1)) - np.float32(1.0)
    frequency = np.float32(1.0) + np.arange(BANDS, dtype=np.float32) * np.float32(
        (GRID / 2.0 - 1.0) / (BANDS - 1)
    )
    phases = position[None, :] * (np.float32(math.pi) * frequency)[:, None]
    waves = np.concatenate([np.sin(phases.astype(np.float64)), np.cos(phases.astype(np.float64))])
    return waves.astype(np.float32)


def contract(left, right, left_dim, right_dim):
    return lax.dot_general(
        left, right, (((left_dim,), (right_dim,)), ((), ())), preferred_element_type=F32
    )


def norm_stats(values, axis):
    centre = values - jnp.mean(values, axis=axis, keepdims=True)
    spread = lax.rsqrt(jnp.mean(centre * centre, axis=axis, keepdims=True) + EPSILON)
    return centre * spread, spread


def norm_back(upstream, gain, unit, spread, axis):
    inner = upstream * gain
    return spread * (
        inner
        - jnp.mean(inner, axis=axis, keepdims=True)
        - unit * jnp.mean(inner * unit, axis=axis, keepdims=True)
    )


def out(shape, dtype):
    return jax.ShapeDtypeStruct(shape, dtype)


def padded(rows, step):
    return -(-rows // step) * step


def lane_ids(shape):
    return lax.broadcasted_iota(jnp.int32, shape, len(shape) - 1)


def waves_first(values, features):
    width = values.shape[1]
    lead = features - 4 * BANDS
    at = lane_ids(values.shape)
    waves = pltpu.roll(values, width - lead, 1)
    rest = pltpu.roll(values, 4 * BANDS, 1)
    return jnp.where(at < 4 * BANDS, waves, jnp.where(at < features, rest, 0.0))


def waves_last(values, features):
    width = values.shape[1]
    lead = features - 4 * BANDS
    at = lane_ids(values.shape)
    rest = pltpu.roll(values, width - 4 * BANDS, 1)
    waves = pltpu.roll(values, lead, 1)
    return jnp.where(at < lead, rest, jnp.where(at < features, waves, 0.0))


def fold(values):
    total = values[:, :LANES]
    for start in range(LANES, values.shape[1], LANES):
        total = total + values[:, start : start + LANES]
    return total


def fold_max(values):
    total = values[:, :LANES]
    for start in range(LANES, values.shape[1], LANES):
        total = jnp.maximum(total, values[:, start : start + LANES])
    return total


def fold_rows(values):
    total = values[:8]
    for start in range(8, values.shape[0], 8):
        total = total + values[start : start + 8]
    return total


def slot_of(kept_row):
    own = kept_row.shape[1]
    shape = (own, own)
    upper = lax.broadcasted_iota(jnp.int32, shape, 0) <= lax.broadcasted_iota(jnp.int32, shape, 1)
    tall = jnp.broadcast_to(kept_row, (8, own)).astype(BF)
    rank = jnp.dot(tall, jnp.where(upper, 1.0, 0.0).astype(BF), preferred_element_type=F32)[:1]
    slot = jnp.where(kept_row > 0, rank - 1.0, -1.0)
    return slot == lax.broadcasted_iota(jnp.int32, shape, 0).astype(F32)


def pack_kernel(pixels, coords, kept, packed, rows):
    rows[...] = jnp.zeros_like(rows)
    rows[0:3, :] = pixels[...]
    rows[3:5, :] = coords[...].astype(F32)
    kept_row = kept[...].astype(F32)
    rows[5:6, :] = kept_row
    slots = jnp.where(slot_of(kept_row), 1.0, 0.0).astype(BF)
    squeezed = contract(rows[...].astype(BF), slots, 1, 1).astype(BF)
    packed[...] = jnp.broadcast_to(squeezed[None], packed.shape)


def pad_rows(target, source):
    rows = source.shape[0]
    whole = rows // LANES * LANES
    target[:whole, :] = source[:whole, :]
    target[whole:, :] = jnp.zeros_like(target[whole:, :])
    target[whole:rows, :] = source[whole:, :]


def query_kernel(
    features, latent, gain, shift, bias, weight_hbm, key_hbm, grad, down_hbm,
    one, query, absorbed, hidden_grad, weight, key_raw, key, down, sems,
):
    copies = [
        pltpu.make_async_copy(weight_hbm, weight, sems.at[0]),
        pltpu.make_async_copy(key_hbm, key_raw, sems.at[1]),
        pltpu.make_async_copy(down_hbm, down, sems.at[2]),
    ]
    for copy in copies:
        copy.start()
    count, dim = latent.shape
    step = 32
    for start in range(0, count, step):
        unit, _ = norm_stats(latent[start : start + step, :].astype(F32), 1)
        one[start : start + step, :] = (unit * gain[...] + shift[...]).astype(BF)
    copies[0].wait()
    step = 256
    for start in range(0, dim, step):
        part = jnp.dot(one[...], weight[:, start : start + step], preferred_element_type=F32)
        query[:, start : start + step] = (part + bias[:, start : start + step]).astype(BF)
    copies[1].wait()
    pad_rows(key, key_raw)
    lifted = contract(query[...], key[...], 1, 1) * (1.0 / math.sqrt(dim))
    absorbed[...] = waves_first(lifted, features).astype(BF)
    copies[2].wait()
    for start in range(0, dim, step):
        hidden_grad[:, start : start + step] = contract(grad[...], down[start : start + step, :], 1, 1)


def as_column(row, width, features):
    wide = jnp.concatenate([row, jnp.zeros((1, width - row.shape[1]), F32)], axis=1)
    tall = jnp.broadcast_to(wide, (LANES, width))
    return jnp.transpose(waves_first(tall, features))


def forward_kernel(
    features, step,
    segments, absorbed, hidden_grad, latent, grad, table, in_gain, in_shift,
    value_hbm, value_bias, gain, shift, up_hbm, up_bias, down_hbm, down_bias,
    encoded, packs, mixed_grad, pool_out, lift_out, x_out, unit_out, spread_out, weight_out, stats, sums,
    placed, gains, shifts, top, total, pooled, mixed, mix_unit, mix_spread,
    value_raw, value, up, down, sems,
):
    copies = [
        pltpu.make_async_copy(value_hbm, value_raw, sems.at[0]),
        pltpu.make_async_copy(up_hbm, up, sems.at[1]),
        pltpu.make_async_copy(down_hbm, down, sems.at[2]),
    ]
    for copy in copies:
        copy.start()
    count, dim = latent.shape
    pix, _, own = segments.shape
    kept = x_out.shape[1]
    tall = x_out.shape[0]
    rows = unit_out.shape[0]
    waves = 4 * BANDS

    placed[...] = jnp.zeros_like(placed)

    def place(index, offset):
        segment = segments[index].astype(F32)
        wide = jnp.concatenate([segment, jnp.zeros((8, LANES), F32)], axis=1)
        inside = lax.rem(offset, LANES)
        base = pl.multiple_of(jnp.minimum(offset - inside, kept), LANES)
        placed[:, pl.ds(base, own + LANES)] += pltpu.roll(wide, inside, 1)
        return offset + jnp.sum(segment[5:6, :]).astype(jnp.int32)

    lax.fori_loop(0, pix, place, jnp.int32(0))
    gains[...] = as_column(in_gain[...], tall, features)
    shifts[...] = as_column(in_shift[...], tall, features)
    top[...] = jnp.full_like(top, FLOOR)

    def make(index, carry):
        lanes = pl.ds(pl.multiple_of(index * step, LANES), step)
        raw = placed[:, lanes]
        places = lax.broadcasted_iota(jnp.int32, (table.shape[1], step), 0).astype(F32)
        row_hot = jnp.where(places == raw[3:4], 1.0, 0.0).astype(BF)
        col_hot = jnp.where(places == raw[4:5], 1.0, 0.0).astype(BF)
        row_waves = jnp.dot(table[...], row_hot, preferred_element_type=F32)
        col_waves = jnp.dot(table[...], col_hot, preferred_element_type=F32)
        at = lax.broadcasted_iota(jnp.int32, raw.shape, 0)
        position = (raw * (2.0 / (GRID - 1)) - 1.0).astype(BF).astype(F32)
        extra = jnp.where(at < 3, raw, jnp.where(at < 5, position, 0.0))
        mean = (
            jnp.sum(row_waves, axis=0, keepdims=True)
            + jnp.sum(col_waves, axis=0, keepdims=True)
            + jnp.sum(extra, axis=0, keepdims=True)
        ) * (1.0 / features)
        row_waves = row_waves - mean
        col_waves = col_waves - mean
        extra = jnp.where(at < features - waves, extra - mean, 0.0)
        square = (
            jnp.sum(row_waves * row_waves, axis=0, keepdims=True)
            + jnp.sum(col_waves * col_waves, axis=0, keepdims=True)
            + jnp.sum(extra * extra, axis=0, keepdims=True)
        ) * (1.0 / features)
        spread = lax.rsqrt(square + EPSILON)
        spread_out[:, lanes] = jnp.broadcast_to(spread, (8, step))
        for piece, start in (
            (row_waves[:BANDS], 0),
            (col_waves[:BANDS], BANDS),
            (row_waves[BANDS:], 2 * BANDS),
            (col_waves[BANDS:], 3 * BANDS),
            (extra, waves),
        ):
            unit = piece * spread
            span = slice(start, start + piece.shape[0])
            unit_out[span, lanes] = unit
            wide = unit * gains[span, :1] + shifts[span, :1]
            if start == waves:
                wide = jnp.concatenate([wide, jnp.zeros((tall - waves - 8, step), F32)], axis=0)
                span = slice(waves, tall)
            x_out[span, lanes] = wide.astype(BF)
        score = jnp.dot(absorbed[...], x_out[:, lanes], preferred_element_type=F32)
        weight_out[:, lanes] = score
        top[...] = jnp.maximum(top[...], fold_max(score))
        return carry

    lax.fori_loop(0, kept // step, make, 0)
    peak = jnp.max(top[...], axis=1, keepdims=True)
    top[...] = jnp.broadcast_to(peak, top.shape)
    total[...] = jnp.zeros_like(total)
    pooled[...] = jnp.zeros_like(pooled)

    def pool(index, carry):
        lanes = pl.ds(pl.multiple_of(index * step, LANES), step)
        weight = jnp.exp(weight_out[:, lanes] - top[:, :1])
        weight_out[:, lanes] = weight
        total[...] += fold(weight)
        pooled[...] += contract(weight.astype(BF), x_out[:, lanes], 1, 1)
        return carry

    lax.fori_loop(0, kept // step, pool, 0)
    share = 1.0 / jnp.sum(total[...], axis=1, keepdims=True)
    pooled[...] = pooled[...] * share
    pool_out[...] = waves_last(pooled[...], features).astype(BF)

    copies[0].wait()
    pad_rows(value, value_raw)
    wide = 256
    for start in range(0, dim, wide):
        span = slice(start, start + wide)
        attn = jnp.dot(pool_out[...], value[:, span], preferred_element_type=F32) + value_bias[:, span]
        mixed[:, span] = latent[:, span].astype(F32) + attn
    low = 32
    hidden, two, pre_grad, attn_grad = packs.at[0], packs.at[1], packs.at[2], packs.at[3]
    for start in range(0, count, low):
        span = slice(start, start + low)
        unit, spread = norm_stats(mixed[span, :], 1)
        mix_unit[span, :] = unit
        mix_spread[span, :] = jnp.broadcast_to(spread, (low, LANES))
        two[span, :] = (unit * gain[...] + shift[...]).astype(BF)
    copies[1].wait()
    for start in range(0, dim, wide):
        span = slice(start, start + wide)
        act = jnp.dot(two[...], up[:, span], preferred_element_type=F32) + up_bias[:, span]
        half = 0.5 * (1.0 + lax.erf(act * (1.0 / math.sqrt(2.0))))
        hidden[:, span] = (act * half).astype(BF)
        slope = half + act * jnp.exp(-0.5 * act * act) * (1.0 / math.sqrt(2.0 * math.pi))
        pre_grad[:, span] = (hidden_grad[:, span] * slope).astype(BF)
    copies[2].wait()
    for start in range(0, dim, wide):
        span = slice(start, start + wide)
        part = jnp.dot(hidden[...], down[:, span], preferred_element_type=F32)
        encoded[:, span] = (mixed[:, span] + part + down_bias[:, span]).astype(BF)
    for start in range(0, dim, wide):
        span = slice(start, start + wide)
        mixed[:, span] = contract(pre_grad[...], up[span, :], 1, 1)
    gain_sum = jnp.zeros((8, dim), F32)
    shift_sum = jnp.zeros((8, dim), F32)
    for start in range(0, count, low):
        span = slice(start, start + low)
        upstream = mixed[span, :]
        unit = mix_unit[span, :]
        full = grad[span, :].astype(F32) + norm_back(upstream, gain[...], unit, mix_spread[span, :1], 1)
        mixed_grad[span, :] = full
        attn_grad[span, :] = full.astype(BF)
        gain_sum = gain_sum + fold_rows(upstream * unit)
        shift_sum = shift_sum + fold_rows(upstream)
    sums[0:1, :] = jnp.sum(gain_sum, axis=0, keepdims=True)
    sums[1:2, :] = jnp.sum(shift_sum, axis=0, keepdims=True)
    lifted = waves_first(contract(attn_grad[...], value[...], 1, 1), features).astype(BF)
    lift_out[...] = lifted
    delta = jnp.sum(lifted.astype(F32) * pooled[...], axis=1, keepdims=True)
    at = lane_ids(stats.shape)
    stats[...] = jnp.where(at == 0, share, delta)


def pull_kernel(
    features, step,
    segments, kept_row, absorbed, lifted, x_in, unit_in, spread_in, weight, stats, in_gain,
    key_hbm, weight_hbm, latent, gain, mixed_grad, sums,
    query_grad, pool_out, latent_grad, color_grad, vectors,
    gains, factors, pooled, gain_sum, shift_sum, colors, back, key_raw, key, query_weight, sems,
):
    copies = [
        pltpu.make_async_copy(key_hbm, key_raw, sems.at[0]),
        pltpu.make_async_copy(weight_hbm, query_weight, sems.at[1]),
    ]
    for copy in copies:
        copy.start()
    count, dim = latent.shape
    own = kept_row.shape[1]
    tall, kept = x_in.shape
    rows = unit_in.shape[0]
    waves = 4 * BANDS
    gains[...] = as_column(in_gain[...], tall, features)
    factors[:, :count] = jnp.transpose(absorbed[...].astype(F32))[:rows].astype(BF)
    factors[:, count:] = jnp.transpose(lifted[...].astype(F32))[:rows].astype(BF)
    pooled[...] = jnp.zeros_like(pooled)
    gain_sum[...] = jnp.zeros_like(gain_sum)
    shift_sum[...] = jnp.zeros_like(shift_sum)

    def pull(index, carry):
        lanes = pl.ds(pl.multiple_of(index * step, LANES), step)
        x_part = x_in[:, lanes]
        prob = weight[:, lanes] * stats[:, :1]
        inner = jnp.dot(lifted[...], x_part, preferred_element_type=F32) - stats[:, 1:2]
        score_grad = (prob * inner).astype(BF)
        pooled[...] += contract(score_grad, x_part, 1, 1)
        both = jnp.concatenate([score_grad, prob.astype(BF)], axis=0)
        upstream = jnp.dot(factors[...], both, preferred_element_type=F32)
        unit = unit_in[:, lanes]
        gain_sum[...] += fold(upstream * unit)
        shift_sum[...] += fold(upstream)
        inner = upstream * gains[:rows, :1]
        mean = jnp.sum(inner, axis=0, keepdims=True) * (1.0 / features)
        tilt = jnp.sum(inner * unit, axis=0, keepdims=True) * (1.0 / features)
        colors[:, lanes] = spread_in[:, lanes] * (inner[waves:] - mean - unit[waves:] * tilt)
        return carry

    lax.fori_loop(0, kept // step, pull, 0)
    colors[:, kept:] = jnp.zeros((8, own + LANES), F32)

    def skip(index, offset):
        return offset + jnp.sum(segments[index][5:6, :].astype(F32)).astype(jnp.int32)

    offset = lax.fori_loop(0, lax.axis_index("pix"), skip, jnp.int32(0))
    inside = lax.rem(offset, LANES)
    base = pl.multiple_of(jnp.minimum(offset - inside, kept), LANES)
    window = pltpu.roll(colors[:, pl.ds(base, own + LANES)], own + LANES - inside, 1)[:, :own]
    slots = jnp.where(slot_of(kept_row[...].astype(F32)), 1.0, 0.0)
    spread_back = jnp.dot(window, slots, precision=lax.Precision.HIGHEST, preferred_element_type=F32)
    color_grad[...] = spread_back[:3]

    pool_out[...] = waves_last(pooled[...], features).astype(BF)
    copies[0].wait()
    pad_rows(key, key_raw)
    wide = 256
    for start in range(0, dim, wide):
        span = slice(start, start + wide)
        part = jnp.dot(pool_out[...], key[:, span], preferred_element_type=F32) * (1.0 / math.sqrt(dim))
        query_grad[:, span] = part.astype(BF)
    copies[1].wait()
    for start in range(0, dim, wide):
        span = slice(start, start + wide)
        back[:, span] = contract(query_grad[...], query_weight[span, :], 1, 1)
    low = 32
    lat_gain_sum = jnp.zeros((8, dim), F32)
    lat_shift_sum = jnp.zeros((8, dim), F32)
    for start in range(0, count, low):
        span = slice(start, start + low)
        unit, spread = norm_stats(latent[span, :].astype(F32), 1)
        upstream = back[span, :]
        latent_grad[span, :] = mixed_grad[span, :] + norm_back(upstream, gain[...], unit, spread, 1)
        lat_gain_sum = lat_gain_sum + fold_rows(upstream * unit)
        lat_shift_sum = lat_shift_sum + fold_rows(upstream)
    vectors[...] = jnp.zeros_like(vectors)
    vectors[0:1, :] = jnp.sum(lat_gain_sum, axis=0, keepdims=True)
    vectors[1:2, :] = jnp.sum(lat_shift_sum, axis=0, keepdims=True)
    vectors[2:4, :] = sums[0:2, :]
    for at, held in ((4, gain_sum), (5, shift_sum)):
        flat = jnp.sum(held[...], axis=1, keepdims=True)
        flat = jnp.concatenate([flat, jnp.zeros((tall - rows, 1), F32)], axis=0)
        turned = jnp.transpose(jnp.broadcast_to(flat, (tall, LANES)))[:8]
        vectors[at : at + 1, :tall] = waves_last(turned, features)[:1]


def outer(left, right, left_other, right_other):
    return contract(left[...], right[...], 0, 0) + contract(left_other[...], right_other[...], 0, 0)


def column_sum(own, far):
    rows = fold_rows(own[...].astype(F32)) + fold_rows(far[...].astype(F32))
    return jnp.sum(rows, axis=0, keepdims=True)


def late_kernel(
    features,
    hidden, hidden_far, grad, grad_far, grad_cols, grad_cols_far, two, two_far, pre, pre_far, pre_cols, pre_cols_far,
    pool, pool_far, attn, attn_far,
    down_grad, down_bias, up_grad, up_bias, value_grad, value_bias,
):
    down_grad[...] = outer(hidden, grad, hidden_far, grad_far)
    up_grad[...] = outer(two, pre, two_far, pre_far)
    value_grad[...] = outer(pool, attn, pool_far, attn_far)[:features]
    down_bias[...] = column_sum(grad_cols, grad_cols_far)
    up_bias[...] = column_sum(pre_cols, pre_cols_far)
    value_bias[...] = column_sum(attn, attn_far)


def last_kernel(
    features,
    one, one_far, back, back_far, back_cols, back_cols_far, pool, pool_far, query, query_far, vectors, vectors_far,
    query_grad, query_bias, key_grad, lat_gain, lat_shift, mlp_gain, mlp_shift, in_gain, in_shift,
):
    query_grad[...] = outer(one, back, one_far, back_far)
    root = 1.0 / math.sqrt(back.shape[1])
    key_grad[...] = outer(pool, query, pool_far, query_far)[:features] * root
    query_bias[...] = column_sum(back_cols, back_cols_far)
    sums = vectors[...] + vectors_far[...]
    lat_gain[...] = sums[0:1]
    lat_shift[...] = sums[1:2]
    mlp_gain[...] = sums[2:3]
    mlp_shift[...] = sums[3:4]
    in_gain[...] = sums[4:5, :features]
    in_shift[...] = sums[5:6, :features]


def call(body, outs, args, specs, scratch, vmem, flops, moved):
    return pl.pallas_call(
        body,
        out_shape=outs,
        in_specs=specs,
        out_specs=jax.tree.map(lambda _: VM, outs),
        scratch_shapes=scratch,
        compiler_params=pltpu.CompilerParams(vmem_limit_bytes=vmem * MIB),
        cost_estimate=pl.CostEstimate(flops=flops, bytes_accessed=moved, transcendentals=0),
    )(*args)


def on_chip(
    latents, pixels, coords, kept_mask, lat_gain, lat_shift, query_weight, query_bias, in_gain, in_shift,
    key_weight, value_weight, value_bias, mlp_gain, mlp_shift, up_weight, up_bias, down_weight, down_bias,
    cotangent,
):
    pix = lax.axis_size("pix")
    own = pixels.shape[2]
    kept = pix * own // 2
    _, count, dim = latents.shape
    features = in_gain.shape[0]
    tall = padded(features, LANES)
    rows = padded(features, 8)
    step = 512 if kept % 512 == 0 else LANES
    latent, out_grad = latents[0], cotangent[0]

    def flat(vector):
        return vector.reshape(1, -1)

    swap = [(0, 1), (1, 0)]

    def other(value):
        return lax.ppermute(value, "img", swap)

    packed = call(
        pack_kernel, out((pix, 8, own), BF), (pixels[0], coords[0], kept_mask), (VM,) * 3,
        [pltpu.VMEM((8, own), F32)], 16, 4 * 8 * own * own, 16 * 8 * own,
    )
    segments = lax.all_to_all(packed, "pix", 0, 0)

    grid_matrix = pltpu.VMEM((dim, dim), BF)
    raw = pltpu.VMEM((features, dim), BF)
    wide = pltpu.VMEM((tall, dim), BF)
    one, query, absorbed, hidden_grad = call(
        lambda *refs: query_kernel(features, *refs),
        (out((count, dim), BF), out((count, dim), BF), out((count, tall), BF), out((count, dim), F32)),
        (latent, flat(lat_gain), flat(lat_shift), flat(query_bias), query_weight, key_weight, out_grad, down_weight),
        (VM, VM, VM, VM, ANY, ANY, VM, ANY),
        [grid_matrix, raw, wide, grid_matrix, pltpu.SemaphoreType.DMA((3,))],
        32, 4 * count * dim * dim + 2 * count * dim * tall, 8 * MIB,
    )

    table = np.zeros((2 * BANDS, padded(GRID, LANES)), np.float32)
    table[:, :GRID] = fourier_lookup()
    column = pltpu.VMEM((tall, LANES), F32)
    narrow = pltpu.VMEM((count, LANES), F32)
    area = pltpu.VMEM((count, dim), F32)
    (
        encoded, packs, mixed_grad, pooled, lifted, x_in, unit_in, spread_in, weight, stats, sums,
    ) = call(
        lambda *refs: forward_kernel(features, step, *refs),
        (
            out((count, dim), BF), out((4, count, dim), BF), out((count, dim), F32), out((count, tall), BF),
            out((count, tall), BF), out((tall, kept), BF), out((rows, kept), F32), out((8, kept), F32),
            out((count, kept), F32), out((count, LANES), F32), out((8, dim), F32),
        ),
        (
            segments, absorbed, hidden_grad, latent, out_grad, jnp.asarray(table, BF), flat(in_gain), flat(in_shift),
            value_weight, flat(value_bias), flat(mlp_gain), flat(mlp_shift), up_weight, flat(up_bias), down_weight,
            flat(down_bias),
        ),
        (VM,) * 8 + (ANY, VM, VM, VM, ANY, VM, ANY, VM),
        [
            pltpu.VMEM((8, kept + own + LANES), F32), column, column, narrow, narrow, pltpu.VMEM((count, tall), F32),
            area, area, narrow, raw, wide, grid_matrix, grid_matrix, pltpu.SemaphoreType.DMA((3,)),
        ],
        52, 6 * count * dim * dim + 4 * count * dim * tall + 6 * kept * count * tall, 8 * MIB,
    )

    query_grad, score_pool, latent_grad, color_grad, vectors = call(
        lambda *refs: pull_kernel(features, step, *refs),
        (
            out((count, dim), BF), out((count, tall), BF), out((count, dim), F32), out((3, own), F32),
            out((8, dim), F32),
        ),
        (
            segments, kept_mask, absorbed, lifted, x_in, unit_in, spread_in, weight, stats, flat(in_gain),
            key_weight, query_weight, latent, flat(lat_gain), mixed_grad, sums,
        ),
        (VM,) * 10 + (ANY, ANY) + (VM,) * 4,
        [
            column, pltpu.VMEM((rows, 2 * count), BF), pltpu.VMEM((count, tall), F32),
            pltpu.VMEM((rows, LANES), F32), pltpu.VMEM((rows, LANES), F32),
            pltpu.VMEM((8, kept + own + LANES), F32), area, raw, wide, grid_matrix, pltpu.SemaphoreType.DMA((2,)),
        ],
        52, 2 * count * dim * dim + 2 * count * dim * tall + 8 * kept * count * tall, 8 * MIB,
    )

    block = 256
    cols = pl.BlockSpec((count, block), lambda i: (0, i))
    full = pl.BlockSpec((count, dim), lambda i: (0, 0))
    pool_spec = pl.BlockSpec((count, tall), lambda i: (0, 0))
    strip = pl.BlockSpec((block, dim), lambda i: (i, 0))
    slab = pl.BlockSpec((features, block), lambda i: (0, i))
    line = pl.BlockSpec((1, block), lambda i: (0, i))
    square = out((dim, dim), F32)
    slab_out = out((features, dim), F32)
    line_out = out((1, dim), F32)
    hidden, two, pre_grad, attn_grad = packs[0], packs[1], packs[2], packs[3]
    packs_far = other(packs)
    hidden_far, two_far, pre_far, attn_far = packs_far[0], packs_far[1], packs_far[2], packs_far[3]
    grad_far = other(out_grad)
    pooled_far = other(pooled)
    down_weight_grad, down_bias_grad, up_weight_grad, up_bias_grad, value_weight_grad, value_bias_grad = pl.pallas_call(
        lambda *refs: late_kernel(features, *refs),
        grid=(dim // block,),
        out_shape=(square, line_out, square, line_out, slab_out, line_out),
        in_specs=(
            cols, cols, full, full, cols, cols, cols, cols, full, full, cols, cols, pool_spec, pool_spec, cols, cols,
        ),
        out_specs=(strip, line, strip, line, slab, line),
        compiler_params=pltpu.CompilerParams(vmem_limit_bytes=40 * MIB),
        cost_estimate=pl.CostEstimate(
            flops=8 * count * dim * dim + 4 * count * dim * tall, bytes_accessed=16 * MIB, transcendentals=0
        ),
    )(
        hidden, hidden_far, out_grad, grad_far, out_grad, grad_far, two, two_far, pre_grad, pre_far, pre_grad, pre_far,
        pooled, pooled_far, attn_grad, attn_far,
    )

    query_grad_far = other(query_grad)
    score_pool_far = other(score_pool)
    vectors_far = other(vectors)
    one_far = other(one)
    query_far = other(query)
    vector_spec = pl.BlockSpec((8, dim), lambda i: (0, 0))
    full_line = pl.BlockSpec((1, dim), lambda i: (0, 0))
    short_line = pl.BlockSpec((1, features), lambda i: (0, 0))
    short_out = out((1, features), F32)
    (
        query_weight_grad, query_bias_grad, key_weight_grad, lat_gain_grad, lat_shift_grad, mlp_gain_grad,
        mlp_shift_grad, in_gain_grad, in_shift_grad,
    ) = pl.pallas_call(
        lambda *refs: last_kernel(features, *refs),
        grid=(dim // block,),
        out_shape=(square, line_out, slab_out) + (line_out,) * 4 + (short_out,) * 2,
        in_specs=(
            cols, cols, full, full, cols, cols, pool_spec, pool_spec, cols, cols, vector_spec, vector_spec,
        ),
        out_specs=(strip, line, slab) + (full_line,) * 4 + (short_line,) * 2,
        compiler_params=pltpu.CompilerParams(vmem_limit_bytes=32 * MIB),
        cost_estimate=pl.CostEstimate(
            flops=4 * count * dim * dim + 4 * count * dim * tall, bytes_accessed=8 * MIB, transcendentals=0
        ),
    )(
        one, one_far, query_grad, query_grad_far, query_grad, query_grad_far, score_pool, score_pool_far, query,
        query_far, vectors, vectors_far,
    )

    return (
        encoded[None], latent_grad[None], color_grad[None], lat_gain_grad[0], lat_shift_grad[0], query_weight_grad,
        query_bias_grad[0], in_gain_grad[0], in_shift_grad[0], key_weight_grad, value_weight_grad, value_bias_grad[0],
        mlp_gain_grad[0], mlp_shift_grad[0], up_weight_grad, up_bias_grad[0], down_weight_grad, down_bias_grad[0],
    )


def in_blocks(
    latents,
    pixels,
    coords,
    kept_mask,
    lat_gain,
    lat_shift,
    query_weight,
    query_bias,
    in_gain,
    in_shift,
    key_weight,
    value_weight,
    value_bias,
    mlp_gain,
    mlp_shift,
    up_weight,
    up_bias,
    down_weight,
    down_bias,
    cotangent,
):
    pix = lax.axis_size("pix")
    mine = lax.axis_index("pix")
    own = pixels.shape[2]
    packed = jnp.concatenate(
        [
            pixels[0].astype(BF),
            coords[0].astype(BF),
            kept_mask.astype(BF),
            jnp.zeros((2, own), BF),
        ],
        axis=0,
    )
    gathered = lax.all_to_all(jnp.broadcast_to(packed[None], (pix,) + packed.shape), "pix", 0, 0)
    every = gathered.transpose(1, 0, 2).reshape(packed.shape[0], pix * own)
    swap = [(0, 1), (1, 0)]

    def other(value):
        return lax.ppermute(value, "img", swap)

    root = math.sqrt(latents.shape[2])
    latent = latents[0].astype(F32)
    lat_unit, lat_spread = norm_stats(latent, 1)
    norm_one = (lat_unit * lat_gain + lat_shift).astype(BF)
    query = (jnp.dot(norm_one, query_weight, preferred_element_type=F32) + query_bias).astype(BF)
    absorbed = (contract(query, key_weight, 1, 1) * (1.0 / root)).astype(BF)

    waves = jnp.asarray(fourier_lookup(), BF)
    places = jnp.arange(GRID, dtype=F32)[:, None]

    def features(part):
        cells = part[3:5].astype(F32)
        position = (cells * (2.0 / (GRID - 1)) - 1.0).astype(BF)
        row_waves = jnp.dot(waves, (cells[0:1] == places).astype(BF), preferred_element_type=F32).astype(BF)
        col_waves = jnp.dot(waves, (cells[1:2] == places).astype(BF), preferred_element_type=F32).astype(BF)
        table = jnp.concatenate(
            [part[0:3], position, row_waves[:BANDS], col_waves[:BANDS], row_waves[BANDS:], col_waves[BANDS:]],
            axis=0,
        ).astype(F32)
        unit, spread = norm_stats(table, 0)
        x_in = (unit * in_gain[:, None] + in_shift[:, None]).astype(BF)
        score = jnp.dot(absorbed, x_in, preferred_element_type=F32)
        return unit, spread, x_in, jnp.where(part[5:6] > 0, score, FLOOR), part[5:6] > 0

    def pool(part, feats):
        unit, spread, x_in, score, live = feats
        top = jnp.max(score, axis=1, keepdims=True)
        weight = jnp.where(live, jnp.exp(score - top), 0.0)
        return top, jnp.sum(weight, axis=1, keepdims=True), contract(weight.astype(BF), x_in, 1, 1)

    blocks = max(1, pix // BLOCK)
    parts = every.reshape(packed.shape[0], blocks, -1).transpose(1, 0, 2)
    if blocks == 1:
        feats = features(parts[0])
        row_top, row_total, pooled = pool(parts[0], feats)
    else:

        def merge(carry, part):
            top, total, sums = pool(part, features(part))
            new_top = jnp.maximum(carry[0], top)
            old_scale, new_scale = jnp.exp(carry[0] - new_top), jnp.exp(top - new_top)
            return (
                new_top,
                carry[1] * old_scale + total * new_scale,
                carry[2] * old_scale + sums * new_scale,
            ), None

        start = (
            jnp.full((latent.shape[0], 1), FLOOR, F32),
            jnp.zeros((latent.shape[0], 1), F32),
            jnp.zeros((latent.shape[0], in_gain.shape[0]), F32),
        )
        row_top, row_total, pooled = lax.scan(merge, start, parts)[0]
    pooled = pooled / row_total
    pooled_low = pooled.astype(BF)
    attn = jnp.dot(pooled_low, value_weight, preferred_element_type=F32) + value_bias
    mixed = latent + attn
    mix_unit, mix_spread = norm_stats(mixed, 1)
    norm_two = (mix_unit * mlp_gain + mlp_shift).astype(BF)
    pre_act = jnp.dot(norm_two, up_weight, preferred_element_type=F32) + up_bias
    half_erf = 0.5 * (1.0 + lax.erf(pre_act * (1.0 / math.sqrt(2.0))))
    hidden = (pre_act * half_erf).astype(BF)
    encoded = (
        mixed + jnp.dot(hidden, down_weight, preferred_element_type=F32) + down_bias
    ).astype(BF)

    out_grad = cotangent[0]
    out_grad_full = out_grad.astype(F32)
    hidden_grad = contract(out_grad, down_weight, 1, 1)
    slope = half_erf + pre_act * jnp.exp(-0.5 * pre_act * pre_act) * (1.0 / math.sqrt(2.0 * math.pi))
    pre_grad = (hidden_grad * slope).astype(BF)
    norm_two_grad = contract(pre_grad, up_weight, 1, 1)
    mixed_grad = out_grad_full + norm_back(norm_two_grad, mlp_gain, mix_unit, mix_spread, 1)
    attn_grad = mixed_grad.astype(BF)

    lifted = contract(attn_grad, value_weight, 1, 1).astype(BF)
    row_delta = jnp.sum(lifted.astype(F32) * pooled, axis=1, keepdims=True)

    def pull(part, feats):
        unit, spread, x_in, score, live = feats
        prob = jnp.where(live, jnp.exp(score - row_top), 0.0) / row_total
        score_grad = (prob * (jnp.dot(lifted, x_in, preferred_element_type=F32) - row_delta)).astype(BF)
        score_pool = contract(score_grad, x_in, 1, 1)
        x_in_grad = contract(absorbed, score_grad, 0, 0) + contract(lifted, prob.astype(BF), 0, 0)
        gain_part = jnp.sum(x_in_grad * unit, axis=1)
        shift_part = jnp.sum(x_in_grad, axis=1)
        colour_part = norm_back(x_in_grad, in_gain[:, None], unit, spread, 0)[:3]
        return score_pool, gain_part, shift_part, colour_part

    if blocks == 1:
        score_pool, in_gain_grad, in_shift_grad, all_colors = pull(parts[0], feats)
    else:

        def gather_up(carry, part):
            found = pull(part, features(part))
            return tuple(kept + new for kept, new in zip(carry, found[:3])), found[3]

        start = (
            jnp.zeros((latent.shape[0], in_gain.shape[0]), F32),
            jnp.zeros_like(in_gain),
            jnp.zeros_like(in_shift),
        )
        (score_pool, in_gain_grad, in_shift_grad), stacked = lax.scan(gather_up, start, parts)
        all_colors = stacked.transpose(1, 0, 2).reshape(3, -1)
    color_grad = lax.dynamic_slice(all_colors, (0, mine * own), (3, own))
    score_pool_low = score_pool.astype(BF)
    query_grad = (
        jnp.dot(score_pool_low, key_weight, preferred_element_type=F32) * (1.0 / root)
    ).astype(BF)
    norm_one_grad = contract(query_grad, query_weight, 1, 1)
    latent_grad = mixed_grad + norm_back(norm_one_grad, lat_gain, lat_unit, lat_spread, 1)

    def both(value):
        return jnp.concatenate([value, other(value)], axis=0)

    out_both = both(out_grad)
    hidden_both = both(hidden)
    two_both = both(norm_two)
    pre_both = both(pre_grad)
    attn_both = both(attn_grad)
    one_both = both(norm_one)
    query_both = both(query)
    query_grad_both = both(query_grad)
    pool_both = both(pooled_low)
    score_both = both(score_pool_low)
    wide = jnp.stack(
        [
            jnp.sum(norm_one_grad * lat_unit, axis=0),
            jnp.sum(norm_one_grad, axis=0),
            jnp.sum(norm_two_grad * mix_unit, axis=0),
            jnp.sum(norm_two_grad, axis=0),
        ]
    )
    narrow = jnp.stack([in_gain_grad, in_shift_grad])
    wide = wide + other(wide)
    narrow = narrow + other(narrow)
    return (
        encoded[None],
        latent_grad[None],
        color_grad[None],
        wide[0],
        wide[1],
        contract(one_both, query_grad_both, 0, 0),
        jnp.sum(query_grad_both.astype(F32), axis=0),
        narrow[0],
        narrow[1],
        contract(score_both, query_both, 0, 0) * (1.0 / root),
        contract(pool_both, attn_both, 0, 0),
        jnp.sum(attn_both.astype(F32), axis=0),
        wide[2],
        wide[3],
        contract(two_both, pre_both, 0, 0),
        jnp.sum(pre_both.astype(F32), axis=0),
        contract(hidden_both, out_both, 0, 0),
        jnp.sum(out_both.astype(F32), axis=0),
    )


def shards(*args):
    pixels = args[1]
    kept = lax.axis_size("pix") * pixels.shape[2] // 2
    fits = kept <= 4096 and pixels.shape[2] % LANES == 0
    return (on_chip if fits else in_blocks)(*args)


def solution(mesh):
    lat = P("img", None, None)
    whole = P()
    return jax.shard_map(
        shards,
        mesh=mesh,
        in_specs=(lat, P("img", None, "pix"), P("img", None, "pix"), P("img", "pix"))
        + (whole,) * 15
        + (lat,),
        out_specs=(lat, lat, P("img", None, "pix")) + (whole,) * 15,
        check_vma=False,
    )
```

```python
import math

import jax
import jax.numpy as jnp
import numpy as np
from jax import lax
from jax.experimental import pallas as pl
from jax.experimental.pallas import tpu as pltpu
from jax.sharding import PartitionSpec as P

BANDS = 64
GRID = 224
EPSILON = 1e-05
FLOOR = -1e30
BLOCK = 16
LANES = 128
BF = jnp.bfloat16
F32 = jnp.float32
VM = pl.BlockSpec(memory_space=pltpu.VMEM)
HBM = pl.BlockSpec(memory_space=pltpu.HBM)
MIB = 1 << 20


def fourier_lookup():
    position = np.arange(GRID, dtype=np.float32) * np.float32(2.0 / (GRID - 1)) - np.float32(1.0)
    frequency = np.float32(1.0) + np.arange(BANDS, dtype=np.float32) * np.float32(
        (GRID / 2.0 - 1.0) / (BANDS - 1)
    )
    phases = position[None, :] * (np.float32(math.pi) * frequency)[:, None]
    waves = np.concatenate([np.sin(phases.astype(np.float64)), np.cos(phases.astype(np.float64))])
    return waves.astype(np.float32)


def contract(left, right, left_dim, right_dim):
    return lax.dot_general(
        left, right, (((left_dim,), (right_dim,)), ((), ())), preferred_element_type=F32
    )


def norm_stats(values, axis):
    centre = values - jnp.mean(values, axis=axis, keepdims=True)
    spread = lax.rsqrt(jnp.mean(centre * centre, axis=axis, keepdims=True) + EPSILON)
    return centre * spread, spread


def norm_back(upstream, gain, unit, spread, axis):
    inner = upstream * gain
    return spread * (
        inner
        - jnp.mean(inner, axis=axis, keepdims=True)
        - unit * jnp.mean(inner * unit, axis=axis, keepdims=True)
    )


def out(shape, dtype):
    return jax.ShapeDtypeStruct(shape, dtype)


def padded(rows, step):
    return -(-rows // step) * step


def lane_ids(shape):
    return lax.broadcasted_iota(jnp.int32, shape, len(shape) - 1)


def waves_first(values, features):
    width = values.shape[1]
    lead = features - 4 * BANDS
    at = lane_ids(values.shape)
    waves = pltpu.roll(values, width - lead, 1)
    rest = pltpu.roll(values, 4 * BANDS, 1)
    return jnp.where(at < 4 * BANDS, waves, jnp.where(at < features, rest, 0.0))


def waves_last(values, features):
    width = values.shape[1]
    lead = features - 4 * BANDS
    at = lane_ids(values.shape)
    rest = pltpu.roll(values, width - 4 * BANDS, 1)
    waves = pltpu.roll(values, lead, 1)
    return jnp.where(at < lead, rest, jnp.where(at < features, waves, 0.0))


def fold(values):
    total = values[:, :LANES]
    for start in range(LANES, values.shape[1], LANES):
        total = total + values[:, start : start + LANES]
    return total


def fold_max(values):
    total = values[:, :LANES]
    for start in range(LANES, values.shape[1], LANES):
        total = jnp.maximum(total, values[:, start : start + LANES])
    return total


def fold_rows(values):
    total = values[:8]
    for start in range(8, values.shape[0], 8):
        total = total + values[start : start + 8]
    return total


def slot_of(kept_row):
    own = kept_row.shape[1]
    shape = (own, own)
    upper = lax.broadcasted_iota(jnp.int32, shape, 0) <= lax.broadcasted_iota(jnp.int32, shape, 1)
    tall = jnp.broadcast_to(kept_row, (8, own)).astype(BF)
    rank = jnp.dot(tall, jnp.where(upper, 1.0, 0.0).astype(BF), preferred_element_type=F32)[:1]
    slot = jnp.where(kept_row > 0, rank - 1.0, -1.0)
    return slot == lax.broadcasted_iota(jnp.int32, shape, 0).astype(F32)


class Fetch:
    def __init__(self, source, target, sem):
        self.copy = pltpu.make_async_copy(source, target, sem)
        self.target = target
        self.waiting = True

    def start(self):
        self.copy.start()

    def get(self):
        if self.waiting:
            self.copy.wait()
            self.waiting = False
        return self.target


def row_of(fetch):
    return fetch.get()[...].reshape(1, -1)


def pack_kernel(pixels, coords, kept, packed, rows):
    rows[...] = jnp.zeros_like(rows)
    rows[0:3, :] = pixels.get()[:, 0, :]
    rows[3:5, :] = coords.get()[...].astype(F32)
    kept_row = kept.get()[...].astype(F32)
    rows[5:6, :] = kept_row
    slots = jnp.where(slot_of(kept_row), 1.0, 0.0).astype(BF)
    squeezed = contract(rows[...].astype(BF), slots, 1, 1).astype(BF)
    packed[...] = jnp.broadcast_to(squeezed[None], packed.shape)


def pad_rows(target, source):
    rows = source.shape[0]
    whole = rows // LANES * LANES
    target[:whole, :] = source[:whole, :]
    target[whole:, :] = jnp.zeros_like(target[whole:, :])
    target[whole:rows, :] = source[whole:, :]


def query_kernel(
    features, latent, gain, shift, bias, weight, key_raw, grad, down,
    early, absorbed, hidden_grad, key,
):
    latent = latent.get()
    count, dim = latent.shape
    one, query, kept_grad = early.at[:, :dim], early.at[:, dim : 2 * dim], early.at[:, 2 * dim :]
    gain, shift = row_of(gain), row_of(shift)
    step = 32
    for start in range(0, count, step):
        unit, _ = norm_stats(latent[start : start + step, :].astype(F32), 1)
        one[start : start + step, :] = (unit * gain + shift).astype(BF)
    bias, weight = row_of(bias), weight.get()
    step = 256
    for start in range(0, dim, step):
        part = jnp.dot(one[...], weight[:, start : start + step], preferred_element_type=F32)
        query[:, start : start + step] = (part + bias[:, start : start + step]).astype(BF)
    pad_rows(key, key_raw.get())
    lifted = contract(query[...], key[...], 1, 1) * (1.0 / math.sqrt(dim))
    absorbed[...] = waves_first(lifted, features).astype(BF)
    grad = grad.get()
    kept_grad[...] = grad[...]
    down = down.get()
    for start in range(0, dim, step):
        hidden_grad[:, start : start + step] = contract(grad[...], down[start : start + step, :], 1, 1)


def as_column(row, width, features):
    wide = jnp.concatenate([row, jnp.zeros((1, width - row.shape[1]), F32)], axis=1)
    tall = jnp.broadcast_to(wide, (LANES, width))
    return jnp.transpose(waves_first(tall, features))


def segment_counts(segments, stop):
    return [jnp.sum(segments[index][5:6, :].astype(F32)).astype(jnp.int32) for index in range(stop)]


def forward_kernel(
    features, step,
    segments, absorbed, hidden_grad, latent, grad, table, in_gain, in_shift,
    value_raw, value_bias, gain, shift, up, up_bias, down, down_bias,
    encoded_out, packs, mixed_grad, lift_out, x_out, unit_out, spread_out, weight_out, stats, sums,
    placed, gains, shifts, top, total, pooled, mixed, mix_unit, mix_spread, value, encoded, out_sem,
):
    pix, _, own = segments.shape
    kept = x_out.shape[1]
    tall = x_out.shape[0]
    waves = 4 * BANDS

    placed[...] = jnp.zeros_like(placed)
    offset = jnp.int32(0)
    for index, found in enumerate(segment_counts(segments, pix)):
        wide = jnp.concatenate([segments[index].astype(F32), jnp.zeros((8, LANES), F32)], axis=1)
        inside = lax.rem(offset, LANES)
        base = pl.multiple_of(jnp.minimum(offset - inside, kept), LANES)
        placed[:, pl.ds(base, own + LANES)] += pltpu.roll(wide, inside, 1)
        offset = offset + found
    gains[...] = as_column(row_of(in_gain), tall, features)
    shifts[...] = as_column(row_of(in_shift), tall, features)
    top[...] = jnp.full_like(top, FLOOR)
    table = table.get()

    def make(index, carry):
        lanes = pl.ds(pl.multiple_of(index * step, LANES), step)
        raw = placed[:, lanes]
        places = lax.broadcasted_iota(jnp.int32, (table.shape[1], step), 0).astype(F32)
        row_hot = jnp.where(places == raw[3:4], 1.0, 0.0).astype(BF)
        col_hot = jnp.where(places == raw[4:5], 1.0, 0.0).astype(BF)
        row_waves = jnp.dot(table[...], row_hot, preferred_element_type=F32)
        col_waves = jnp.dot(table[...], col_hot, preferred_element_type=F32)
        at = lax.broadcasted_iota(jnp.int32, raw.shape, 0)
        position = (raw * (2.0 / (GRID - 1)) - 1.0).astype(BF).astype(F32)
        extra = jnp.where(at < 3, raw, jnp.where(at < 5, position, 0.0))
        mean = (
            jnp.sum(row_waves, axis=0, keepdims=True)
            + jnp.sum(col_waves, axis=0, keepdims=True)
            + jnp.sum(extra, axis=0, keepdims=True)
        ) * (1.0 / features)
        row_waves = row_waves - mean
        col_waves = col_waves - mean
        extra = jnp.where(at < features - waves, extra - mean, 0.0)
        square = (
            jnp.sum(row_waves * row_waves, axis=0, keepdims=True)
            + jnp.sum(col_waves * col_waves, axis=0, keepdims=True)
            + jnp.sum(extra * extra, axis=0, keepdims=True)
        ) * (1.0 / features)
        spread = lax.rsqrt(square + EPSILON)
        spread_out[:, lanes] = jnp.broadcast_to(spread, (8, step))
        for piece, start in (
            (row_waves[:BANDS], 0),
            (col_waves[:BANDS], BANDS),
            (row_waves[BANDS:], 2 * BANDS),
            (col_waves[BANDS:], 3 * BANDS),
            (extra, waves),
        ):
            unit = piece * spread
            span = slice(start, start + piece.shape[0])
            unit_out[span, lanes] = unit
            wide = unit * gains[span, :1] + shifts[span, :1]
            if start == waves:
                wide = jnp.concatenate([wide, jnp.zeros((tall - waves - 8, step), F32)], axis=0)
                span = slice(waves, tall)
            x_out[span, lanes] = wide.astype(BF)
        score = jnp.dot(absorbed[...], x_out[:, lanes], preferred_element_type=F32)
        weight_out[:, lanes] = score
        top[...] = jnp.maximum(top[...], fold_max(score))
        return carry

    lax.fori_loop(0, kept // step, make, 0)
    peak = jnp.max(top[...], axis=1, keepdims=True)
    top[...] = jnp.broadcast_to(peak, top.shape)
    total[...] = jnp.zeros_like(total)
    pooled[...] = jnp.zeros_like(pooled)

    def pool(index, carry):
        lanes = pl.ds(pl.multiple_of(index * step, LANES), step)
        weight = jnp.exp(weight_out[:, lanes] - top[:, :1])
        weight_out[:, lanes] = weight
        total[...] += fold(weight)
        pooled[...] += contract(weight.astype(BF), x_out[:, lanes], 1, 1)
        return carry

    lax.fori_loop(0, kept // step, pool, 0)
    share = 1.0 / jnp.sum(total[...], axis=1, keepdims=True)
    pooled[...] = pooled[...] * share
    latent, grad = latent.get(), grad.get()
    count, dim = latent.shape
    hidden, two, pre_grad, attn_grad = (packs.at[:, at * dim : (at + 1) * dim] for at in range(4))
    pool_out = packs.at[:, 4 * dim : 4 * dim + tall]
    packs[:, 4 * dim + tall :] = jnp.zeros((count, packs.shape[1] - 4 * dim - tall), BF)
    pool_out[...] = waves_last(pooled[...], features).astype(BF)

    pad_rows(value, value_raw.get())
    value_bias = row_of(value_bias)
    wide = 256
    for start in range(0, dim, wide):
        span = slice(start, start + wide)
        attn = jnp.dot(pool_out[...], value[:, span], preferred_element_type=F32) + value_bias[:, span]
        mixed[:, span] = latent[:, span].astype(F32) + attn
    low = 32
    gain, shift = row_of(gain), row_of(shift)
    for start in range(0, count, low):
        span = slice(start, start + low)
        unit, spread = norm_stats(mixed[span, :], 1)
        mix_unit[span, :] = unit
        mix_spread[span, :] = jnp.broadcast_to(spread, (low, LANES))
        two[span, :] = (unit * gain + shift).astype(BF)
    up, up_bias = up.get(), row_of(up_bias)
    for start in range(0, dim, wide):
        span = slice(start, start + wide)
        act = jnp.dot(two[...], up[:, span], preferred_element_type=F32) + up_bias[:, span]
        half = 0.5 * (1.0 + lax.erf(act * (1.0 / math.sqrt(2.0))))
        hidden[:, span] = (act * half).astype(BF)
        slope = half + act * jnp.exp(-0.5 * act * act) * (1.0 / math.sqrt(2.0 * math.pi))
        pre_grad[:, span] = (hidden_grad[:, span] * slope).astype(BF)
    down, down_bias = down.get(), row_of(down_bias)
    for start in range(0, dim, wide):
        span = slice(start, start + wide)
        part = jnp.dot(hidden[...], down[:, span], preferred_element_type=F32)
        encoded[:, span] = (mixed[:, span] + part + down_bias[:, span]).astype(BF)
    leave = pltpu.make_async_copy(encoded, encoded_out, out_sem)
    leave.start()
    for start in range(0, dim, wide):
        span = slice(start, start + wide)
        mixed[:, span] = contract(pre_grad[...], up[span, :], 1, 1)
    gain_sum = jnp.zeros((8, dim), F32)
    shift_sum = jnp.zeros((8, dim), F32)
    for start in range(0, count, low):
        span = slice(start, start + low)
        upstream = mixed[span, :]
        unit = mix_unit[span, :]
        full = grad[span, :].astype(F32) + norm_back(upstream, gain, unit, mix_spread[span, :1], 1)
        mixed_grad[span, :] = full
        attn_grad[span, :] = full.astype(BF)
        gain_sum = gain_sum + fold_rows(upstream * unit)
        shift_sum = shift_sum + fold_rows(upstream)
    sums[0:1, :] = jnp.sum(gain_sum, axis=0, keepdims=True)
    sums[1:2, :] = jnp.sum(shift_sum, axis=0, keepdims=True)
    lifted = waves_first(contract(attn_grad[...], value[...], 1, 1), features).astype(BF)
    lift_out[...] = lifted
    delta = jnp.sum(lifted.astype(F32) * pooled[...], axis=1, keepdims=True)
    at = lane_ids(stats.shape)
    stats[...] = jnp.where(at == 0, share, delta)
    leave.wait()


def pull_kernel(
    features, step,
    segments, kept_row, absorbed, lifted, x_in, unit_in, spread_in, weight, stats, in_gain,
    key_raw, query_weight, latent, gain, mixed_grad, sums,
    late, vectors, latent_out, color_out,
    gains, factors, pooled, gain_sum, shift_sum, colors, back, key, latent_grad, color_grad, out_sems,
):
    count, dim = latent_grad.shape
    own = segments.shape[2]
    tall, kept = x_in.shape
    rows = unit_in.shape[0]
    waves = 4 * BANDS
    query_grad, pool_out = late.at[:, :dim], late.at[:, dim : dim + tall]
    late[:, dim + tall :] = jnp.zeros((count, late.shape[1] - dim - tall), BF)
    gains[...] = as_column(row_of(in_gain), tall, features)
    factors[:, :count] = jnp.transpose(absorbed[...].astype(F32))[:rows].astype(BF)
    factors[:, count:] = jnp.transpose(lifted[...].astype(F32))[:rows].astype(BF)
    pooled[...] = jnp.zeros_like(pooled)
    gain_sum[...] = jnp.zeros_like(gain_sum)
    shift_sum[...] = jnp.zeros_like(shift_sum)

    def pull(index, carry):
        lanes = pl.ds(pl.multiple_of(index * step, LANES), step)
        x_part = x_in[:, lanes]
        prob = weight[:, lanes] * stats[:, :1]
        inner = jnp.dot(lifted[...], x_part, preferred_element_type=F32) - stats[:, 1:2]
        score_grad = (prob * inner).astype(BF)
        pooled[...] += contract(score_grad, x_part, 1, 1)
        both = jnp.concatenate([score_grad, prob.astype(BF)], axis=0)
        upstream = jnp.dot(factors[...], both, preferred_element_type=F32)
        unit = unit_in[:, lanes]
        gain_sum[...] += fold(upstream * unit)
        shift_sum[...] += fold(upstream)
        inner = upstream * gains[:rows, :1]
        mean = jnp.sum(inner, axis=0, keepdims=True) * (1.0 / features)
        tilt = jnp.sum(inner * unit, axis=0, keepdims=True) * (1.0 / features)
        colors[:, lanes] = spread_in[:, lanes] * (inner[waves:] - mean - unit[waves:] * tilt)
        return carry

    lax.fori_loop(0, kept // step, pull, 0)
    colors[:, kept:] = jnp.zeros((8, own + LANES), F32)

    mine = lax.axis_index("pix")
    offset = jnp.int32(0)
    for index, found in enumerate(segment_counts(segments, segments.shape[0])):
        offset = offset + jnp.where(index < mine, found, 0)
    inside = lax.rem(offset, LANES)
    base = pl.multiple_of(jnp.minimum(offset - inside, kept), LANES)
    window = pltpu.roll(colors[:, pl.ds(base, own + LANES)], own + LANES - inside, 1)[:, :own]
    slots = jnp.where(slot_of(kept_row.get()[...].astype(F32)), 1.0, 0.0)
    spread_back = jnp.dot(window, slots, precision=lax.Precision.HIGHEST, preferred_element_type=F32)
    color_grad[:, 0, :] = spread_back[:3]
    leave = [pltpu.make_async_copy(color_grad, color_out, out_sems.at[0])]
    leave[0].start()

    pool_out[...] = waves_last(pooled[...], features).astype(BF)
    pad_rows(key, key_raw.get())
    wide = 256
    for start in range(0, dim, wide):
        span = slice(start, start + wide)
        part = jnp.dot(pool_out[...], key[:, span], preferred_element_type=F32) * (1.0 / math.sqrt(dim))
        query_grad[:, span] = part.astype(BF)
    query_weight = query_weight.get()
    for start in range(0, dim, wide):
        span = slice(start, start + wide)
        back[:, span] = contract(query_grad[...], query_weight[span, :], 1, 1)
    low = 32
    gain, latent = row_of(gain), latent.get()
    lat_gain_sum = jnp.zeros((8, dim), F32)
    lat_shift_sum = jnp.zeros((8, dim), F32)
    parts = 4
    for start in range(0, count, low):
        span = slice(start, start + low)
        unit, spread = norm_stats(latent[span, :].astype(F32), 1)
        upstream = back[span, :]
        latent_grad[span, :] = mixed_grad[span, :] + norm_back(upstream, gain, unit, spread, 1)
        lat_gain_sum = lat_gain_sum + fold_rows(upstream * unit)
        lat_shift_sum = lat_shift_sum + fold_rows(upstream)
        done = start + low
        if done % (count // parts) == 0:
            span = slice(done - count // parts, done)
            at = len(leave)
            leave.append(pltpu.make_async_copy(latent_grad.at[span, :], latent_out.at[span, :], out_sems.at[at]))
            leave[-1].start()
    vectors[...] = jnp.zeros_like(vectors)
    vectors[0:1, :] = jnp.sum(lat_gain_sum, axis=0, keepdims=True)
    vectors[1:2, :] = jnp.sum(lat_shift_sum, axis=0, keepdims=True)
    vectors[2:4, :] = sums[0:2, :]
    for at, held in ((4, gain_sum), (5, shift_sum)):
        flat = jnp.sum(held[...], axis=1, keepdims=True)
        flat = jnp.concatenate([flat, jnp.zeros((tall - rows, 1), F32)], axis=0)
        turned = jnp.transpose(jnp.broadcast_to(flat, (tall, LANES)))[:8]
        vectors[at : at + 1, :tall] = waves_last(turned, features)[:1]
    for copy in leave:
        copy.wait()


def outer(left, right, left_other, right_other):
    return contract(left[...], right[...], 0, 0) + contract(left_other[...], right_other[...], 0, 0)


def column_sum(own, far):
    rows = fold_rows(own[...].astype(F32)) + fold_rows(far[...].astype(F32))
    return jnp.sum(rows, axis=0)


def late_kernel(
    features, width,
    hidden, hidden_far, grad, grad_far, grad_cols, grad_cols_far, two, two_far, pre, pre_far, pre_cols, pre_cols_far,
    pool, pool_far, attn, attn_far,
    down_grad, down_bias, up_grad, up_bias, value_grad, value_bias,
):
    down_grad[...] = outer(hidden, grad, hidden_far, grad_far)
    up_grad[...] = outer(two, pre, two_far, pre_far)
    value_grad[...] = outer(pool, attn, pool_far, attn_far)[:features]
    down_bias[...] = column_sum(grad_cols, grad_cols_far)
    up_bias[...] = column_sum(pre_cols, pre_cols_far)
    value_bias[...] = column_sum(attn, attn_far)


def last_kernel(
    features, width,
    one, one_far, back, back_far, back_cols, back_cols_far, pool, pool_far, query, query_far, vectors, vectors_far, _,
    query_grad, query_bias, key_grad, lat_gain, lat_shift, mlp_gain, mlp_shift, in_gain, in_shift,
):
    query_grad[...] = outer(one, back, one_far, back_far)
    key_grad[...] = outer(pool, query, pool_far, query_far)[:features] * (1.0 / math.sqrt(width))
    query_bias[...] = column_sum(back_cols, back_cols_far)
    sums = vectors[...] + vectors_far[...]
    lat_gain[...] = sums[0]
    lat_shift[...] = sums[1]
    mlp_gain[...] = sums[2]
    mlp_shift[...] = sums[3]
    in_gain[...] = sums[4, :features]
    in_shift[...] = sums[5, :features]


def call(body, outs, args, fetched, scratch, vmem, flops, moved):
    places = [at for at in range(len(args)) if at in fetched]
    buffers = [pltpu.VMEM(args[at].shape, args[at].dtype) for at in places]
    shapes = tuple(out(shape, dtype) for shape, dtype, _ in outs)

    def whole(*refs):
        sources, rest = list(refs[: len(args)]), refs[len(args) :]
        targets, sems, rest = rest[-len(buffers) - 1 : -1], rest[-1], rest[: -len(buffers) - 1]
        for slot, (at, target) in enumerate(zip(places, targets)):
            sources[at] = Fetch(sources[at], target, sems.at[slot])
            sources[at].start()
        body(*sources, *rest)
        for at in places:
            sources[at].get()

    return pl.pallas_call(
        whole,
        out_shape=shapes if len(shapes) > 1 else shapes[0],
        in_specs=tuple(HBM if at in fetched else VM for at in range(len(args))),
        out_specs=tuple(place for _, _, place in outs) if len(outs) > 1 else outs[0][2],
        scratch_shapes=list(scratch) + buffers + [pltpu.SemaphoreType.DMA((len(places),))],
        compiler_params=pltpu.CompilerParams(vmem_limit_bytes=vmem * MIB),
        cost_estimate=pl.CostEstimate(flops=flops, bytes_accessed=moved, transcendentals=0),
    )(*(pltpu.with_memory_space_constraint(arg, pltpu.HBM) if at in fetched else arg for at, arg in enumerate(args)))


def on_chip(
    latents, pixels, coords, kept_mask, lat_gain, lat_shift, query_weight, query_bias, in_gain, in_shift,
    key_weight, value_weight, value_bias, mlp_gain, mlp_shift, up_weight, up_bias, down_weight, down_bias,
    cotangent,
):
    pix = lax.axis_size("pix")
    own = pixels.shape[2]
    kept = pix * own // 2
    _, count, dim = latents.shape
    features = in_gain.shape[0]
    tall = padded(features, LANES)
    rows = padded(features, 8)
    step = 512 if kept % 512 == 0 else LANES
    latent, out_grad = latents[0], cotangent[0]
    swap = [(0, 1), (1, 0)]

    def other(value):
        return lax.ppermute(value, "img", swap)

    packed = call(
        pack_kernel, [((pix, 8, own), BF, VM)], (pixels.transpose(1, 0, 2), coords[0], kept_mask), (0, 1, 2),
        [pltpu.VMEM((8, own), F32)], 8, 4 * 8 * own * own, 16 * 8 * own,
    )
    segments = lax.all_to_all(packed, "pix", 0, 0)

    wide = pltpu.VMEM((tall, dim), BF)
    early, absorbed, hidden_grad = call(
        lambda *refs: query_kernel(features, *refs),
        [((count, 3 * dim), BF, VM), ((count, tall), BF, VM), ((count, dim), F32, VM)],
        (latent, lat_gain, lat_shift, query_bias, query_weight, key_weight, out_grad, down_weight),
        tuple(range(8)), [wide], 14, 4 * count * dim * dim + 2 * count * dim * tall, 8 * MIB,
    )

    table = np.zeros((2 * BANDS, padded(GRID, LANES)), np.float32)
    table[:, :GRID] = fourier_lookup()
    column = pltpu.VMEM((tall, LANES), F32)
    narrow = pltpu.VMEM((count, LANES), F32)
    area = pltpu.VMEM((count, dim), F32)
    spare = 512
    (
        encoded, packs, mixed_grad, lifted, x_in, unit_in, spread_in, weight, stats, sums,
    ) = call(
        lambda *refs: forward_kernel(features, step, *refs),
        [
            ((count, dim), BF, HBM), ((count, 4 * dim + spare), BF, VM), ((count, dim), F32, VM),
            ((count, tall), BF, VM), ((tall, kept), BF, VM), ((rows, kept), F32, VM), ((8, kept), F32, VM),
            ((count, kept), F32, VM), ((count, LANES), F32, VM), ((8, dim), F32, VM),
        ],
        (
            segments, absorbed, hidden_grad, latent, out_grad, jnp.asarray(table, BF), in_gain, in_shift,
            value_weight, value_bias, mlp_gain, mlp_shift, up_weight, up_bias, down_weight, down_bias,
        ),
        tuple(range(3, 16)),
        [
            pltpu.VMEM((8, kept + own + LANES), F32), column, column, narrow, narrow, pltpu.VMEM((count, tall), F32),
            area, area, narrow, wide, pltpu.VMEM((count, dim), BF), pltpu.SemaphoreType.DMA(()),
        ],
        20, 6 * count * dim * dim + 4 * count * dim * tall + 6 * kept * count * tall, 8 * MIB,
    )

    late, vectors, latent_grad, color_grad = call(
        lambda *refs: pull_kernel(features, step, *refs),
        [
            ((count, dim + spare), BF, VM), ((8, dim), F32, VM), ((count, dim), F32, HBM), ((3, 1, own), F32, HBM),
        ],
        (
            segments, kept_mask, absorbed, lifted, x_in, unit_in, spread_in, weight, stats, in_gain,
            key_weight, query_weight, latent, lat_gain, mixed_grad, sums,
        ),
        (1, 9, 10, 11, 12, 13),
        [
            column, pltpu.VMEM((rows, 2 * count), BF), pltpu.VMEM((count, tall), F32),
            pltpu.VMEM((rows, LANES), F32), pltpu.VMEM((rows, LANES), F32),
            pltpu.VMEM((8, kept + own + LANES), F32), area, wide, area, pltpu.VMEM((3, 1, own), F32),
            pltpu.SemaphoreType.DMA((5,)),
        ],
        16, 2 * count * dim * dim + 2 * count * dim * tall + 8 * kept * count * tall, 8 * MIB,
    )

    block = 256
    turns = dim // block

    def cols(at):
        return pl.BlockSpec((count, block), lambda i: (0, at * turns + i))

    def full(at):
        return pl.BlockSpec((count, dim), lambda i: (0, at))

    def tail(at):
        return pl.BlockSpec((count, spare), lambda i: (0, at * dim // spare))

    strip = pl.BlockSpec((block, dim), lambda i: (i, 0))
    slab = pl.BlockSpec((features, block), lambda i: (0, i))
    line = pl.BlockSpec((block,), lambda i: (i,))
    square = out((dim, dim), F32)
    slab_out = out((features, dim), F32)
    line_out = out((dim,), F32)

    def twice(specs):
        return tuple(spec for spec in specs for _ in range(2))

    early_far = other(early)
    packs_far = other(packs)
    late_far = other(late)
    vectors_far = other(vectors)
    down_weight_grad, down_bias_grad, up_weight_grad, up_bias_grad, value_weight_grad, value_bias_grad = pl.pallas_call(
        lambda *refs: late_kernel(features, dim, *refs),
        grid=(turns,),
        out_shape=(square, line_out, square, line_out, slab_out, line_out),
        in_specs=twice((cols(0), full(2), cols(2), cols(1), full(2), cols(2), tail(4), cols(3))),
        out_specs=(strip, line, strip, line, slab, line),
        compiler_params=pltpu.CompilerParams(vmem_limit_bytes=30 * MIB),
        cost_estimate=pl.CostEstimate(
            flops=8 * count * dim * dim + 4 * count * dim * tall, bytes_accessed=16 * MIB, transcendentals=0
        ),
    )(
        packs, packs_far, early, early_far, early, early_far, packs, packs_far, packs, packs_far, packs, packs_far,
        packs, packs_far, packs, packs_far,
    )

    vector_spec = pl.BlockSpec((8, dim), lambda i: (0, 0))
    full_line = pl.BlockSpec((dim,), lambda i: (0,))
    short_line = pl.BlockSpec((features,), lambda i: (0,))
    short_out = out((features,), F32)
    (
        query_weight_grad, query_bias_grad, key_weight_grad, lat_gain_grad, lat_shift_grad, mlp_gain_grad,
        mlp_shift_grad, in_gain_grad, in_shift_grad,
    ) = pl.pallas_call(
        lambda *refs: last_kernel(features, dim, *refs),
        grid=(turns,),
        out_shape=(square, line_out, slab_out) + (line_out,) * 4 + (short_out,) * 2,
        in_specs=twice((cols(0), full(0), cols(0), tail(1), cols(1), vector_spec)) + (HBM,),
        out_specs=(strip, line, slab) + (full_line,) * 4 + (short_line,) * 2,
        compiler_params=pltpu.CompilerParams(vmem_limit_bytes=20 * MIB),
        cost_estimate=pl.CostEstimate(
            flops=4 * count * dim * dim + 4 * count * dim * tall, bytes_accessed=8 * MIB, transcendentals=0
        ),
    )(
        early, early_far, late, late_far, late, late_far, late, late_far, early, early_far, vectors, vectors_far,
        pltpu.with_memory_space_constraint(value_bias_grad, pltpu.HBM),
    )

    return (
        encoded[None], latent_grad[None], color_grad.transpose(1, 0, 2), lat_gain_grad, lat_shift_grad,
        query_weight_grad, query_bias_grad, in_gain_grad, in_shift_grad, key_weight_grad, value_weight_grad,
        value_bias_grad, mlp_gain_grad, mlp_shift_grad, up_weight_grad, up_bias_grad, down_weight_grad, down_bias_grad,
    )


def in_blocks(
    latents,
    pixels,
    coords,
    kept_mask,
    lat_gain,
    lat_shift,
    query_weight,
    query_bias,
    in_gain,
    in_shift,
    key_weight,
    value_weight,
    value_bias,
    mlp_gain,
    mlp_shift,
    up_weight,
    up_bias,
    down_weight,
    down_bias,
    cotangent,
):
    pix = lax.axis_size("pix")
    mine = lax.axis_index("pix")
    own = pixels.shape[2]
    packed = jnp.concatenate(
        [
            pixels[0].astype(BF),
            coords[0].astype(BF),
            kept_mask.astype(BF),
            jnp.zeros((2, own), BF),
        ],
        axis=0,
    )
    gathered = lax.all_to_all(jnp.broadcast_to(packed[None], (pix,) + packed.shape), "pix", 0, 0)
    every = gathered.transpose(1, 0, 2).reshape(packed.shape[0], pix * own)
    swap = [(0, 1), (1, 0)]

    def other(value):
        return lax.ppermute(value, "img", swap)

    root = math.sqrt(latents.shape[2])
    latent = latents[0].astype(F32)
    lat_unit, lat_spread = norm_stats(latent, 1)
    norm_one = (lat_unit * lat_gain + lat_shift).astype(BF)
    query = (jnp.dot(norm_one, query_weight, preferred_element_type=F32) + query_bias).astype(BF)
    absorbed = (contract(query, key_weight, 1, 1) * (1.0 / root)).astype(BF)

    waves = jnp.asarray(fourier_lookup(), BF)
    places = jnp.arange(GRID, dtype=F32)[:, None]

    def features(part):
        cells = part[3:5].astype(F32)
        position = (cells * (2.0 / (GRID - 1)) - 1.0).astype(BF)
        row_waves = jnp.dot(waves, (cells[0:1] == places).astype(BF), preferred_element_type=F32).astype(BF)
        col_waves = jnp.dot(waves, (cells[1:2] == places).astype(BF), preferred_element_type=F32).astype(BF)
        table = jnp.concatenate(
            [part[0:3], position, row_waves[:BANDS], col_waves[:BANDS], row_waves[BANDS:], col_waves[BANDS:]],
            axis=0,
        ).astype(F32)
        unit, spread = norm_stats(table, 0)
        x_in = (unit * in_gain[:, None] + in_shift[:, None]).astype(BF)
        score = jnp.dot(absorbed, x_in, preferred_element_type=F32)
        return unit, spread, x_in, jnp.where(part[5:6] > 0, score, FLOOR), part[5:6] > 0

    def pool(part, feats):
        unit, spread, x_in, score, live = feats
        top = jnp.max(score, axis=1, keepdims=True)
        weight = jnp.where(live, jnp.exp(score - top), 0.0)
        return top, jnp.sum(weight, axis=1, keepdims=True), contract(weight.astype(BF), x_in, 1, 1)

    blocks = max(1, pix // BLOCK)
    parts = every.reshape(packed.shape[0], blocks, -1).transpose(1, 0, 2)
    if blocks == 1:
        feats = features(parts[0])
        row_top, row_total, pooled = pool(parts[0], feats)
    else:

        def merge(carry, part):
            top, total, sums = pool(part, features(part))
            new_top = jnp.maximum(carry[0], top)
            old_scale, new_scale = jnp.exp(carry[0] - new_top), jnp.exp(top - new_top)
            return (
                new_top,
                carry[1] * old_scale + total * new_scale,
                carry[2] * old_scale + sums * new_scale,
            ), None

        start = (
            jnp.full((latent.shape[0], 1), FLOOR, F32),
            jnp.zeros((latent.shape[0], 1), F32),
            jnp.zeros((latent.shape[0], in_gain.shape[0]), F32),
        )
        row_top, row_total, pooled = lax.scan(merge, start, parts)[0]
    pooled = pooled / row_total
    pooled_low = pooled.astype(BF)
    attn = jnp.dot(pooled_low, value_weight, preferred_element_type=F32) + value_bias
    mixed = latent + attn
    mix_unit, mix_spread = norm_stats(mixed, 1)
    norm_two = (mix_unit * mlp_gain + mlp_shift).astype(BF)
    pre_act = jnp.dot(norm_two, up_weight, preferred_element_type=F32) + up_bias
    half_erf = 0.5 * (1.0 + lax.erf(pre_act * (1.0 / math.sqrt(2.0))))
    hidden = (pre_act * half_erf).astype(BF)
    encoded = (
        mixed + jnp.dot(hidden, down_weight, preferred_element_type=F32) + down_bias
    ).astype(BF)

    out_grad = cotangent[0]
    out_grad_full = out_grad.astype(F32)
    hidden_grad = contract(out_grad, down_weight, 1, 1)
    slope = half_erf + pre_act * jnp.exp(-0.5 * pre_act * pre_act) * (1.0 / math.sqrt(2.0 * math.pi))
    pre_grad = (hidden_grad * slope).astype(BF)
    norm_two_grad = contract(pre_grad, up_weight, 1, 1)
    mixed_grad = out_grad_full + norm_back(norm_two_grad, mlp_gain, mix_unit, mix_spread, 1)
    attn_grad = mixed_grad.astype(BF)

    lifted = contract(attn_grad, value_weight, 1, 1).astype(BF)
    row_delta = jnp.sum(lifted.astype(F32) * pooled, axis=1, keepdims=True)

    def pull(part, feats):
        unit, spread, x_in, score, live = feats
        prob = jnp.where(live, jnp.exp(score - row_top), 0.0) / row_total
        score_grad = (prob * (jnp.dot(lifted, x_in, preferred_element_type=F32) - row_delta)).astype(BF)
        score_pool = contract(score_grad, x_in, 1, 1)
        x_in_grad = contract(absorbed, score_grad, 0, 0) + contract(lifted, prob.astype(BF), 0, 0)
        gain_part = jnp.sum(x_in_grad * unit, axis=1)
        shift_part = jnp.sum(x_in_grad, axis=1)
        colour_part = norm_back(x_in_grad, in_gain[:, None], unit, spread, 0)[:3]
        return score_pool, gain_part, shift_part, colour_part

    if blocks == 1:
        score_pool, in_gain_grad, in_shift_grad, all_colors = pull(parts[0], feats)
    else:

        def gather_up(carry, part):
            found = pull(part, features(part))
            return tuple(kept + new for kept, new in zip(carry, found[:3])), found[3]

        start = (
            jnp.zeros((latent.shape[0], in_gain.shape[0]), F32),
            jnp.zeros_like(in_gain),
            jnp.zeros_like(in_shift),
        )
        (score_pool, in_gain_grad, in_shift_grad), stacked = lax.scan(gather_up, start, parts)
        all_colors = stacked.transpose(1, 0, 2).reshape(3, -1)
    color_grad = lax.dynamic_slice(all_colors, (0, mine * own), (3, own))
    score_pool_low = score_pool.astype(BF)
    query_grad = (
        jnp.dot(score_pool_low, key_weight, preferred_element_type=F32) * (1.0 / root)
    ).astype(BF)
    norm_one_grad = contract(query_grad, query_weight, 1, 1)
    latent_grad = mixed_grad + norm_back(norm_one_grad, lat_gain, lat_unit, lat_spread, 1)

    def both(value):
        return jnp.concatenate([value, other(value)], axis=0)

    out_both = both(out_grad)
    hidden_both = both(hidden)
    two_both = both(norm_two)
    pre_both = both(pre_grad)
    attn_both = both(attn_grad)
    one_both = both(norm_one)
    query_both = both(query)
    query_grad_both = both(query_grad)
    pool_both = both(pooled_low)
    score_both = both(score_pool_low)
    wide = jnp.stack(
        [
            jnp.sum(norm_one_grad * lat_unit, axis=0),
            jnp.sum(norm_one_grad, axis=0),
            jnp.sum(norm_two_grad * mix_unit, axis=0),
            jnp.sum(norm_two_grad, axis=0),
        ]
    )
    narrow = jnp.stack([in_gain_grad, in_shift_grad])
    wide = wide + other(wide)
    narrow = narrow + other(narrow)
    return (
        encoded[None],
        latent_grad[None],
        color_grad[None],
        wide[0],
        wide[1],
        contract(one_both, query_grad_both, 0, 0),
        jnp.sum(query_grad_both.astype(F32), axis=0),
        narrow[0],
        narrow[1],
        contract(score_both, query_both, 0, 0) * (1.0 / root),
        contract(pool_both, attn_both, 0, 0),
        jnp.sum(attn_both.astype(F32), axis=0),
        wide[2],
        wide[3],
        contract(two_both, pre_both, 0, 0),
        jnp.sum(pre_both.astype(F32), axis=0),
        contract(hidden_both, out_both, 0, 0),
        jnp.sum(out_both.astype(F32), axis=0),
    )


def shards(*args):
    pixels = args[1]
    kept = lax.axis_size("pix") * pixels.shape[2] // 2
    fits = kept <= 4096 and pixels.shape[2] % LANES == 0
    return (on_chip if fits else in_blocks)(*args)


def solution(mesh):
    lat = P("img", None, None)
    whole = P()
    return jax.shard_map(
        shards,
        mesh=mesh,
        in_specs=(lat, P("img", None, "pix"), P("img", None, "pix"), P("img", "pix"))
        + (whole,) * 15
        + (lat,),
        out_specs=(lat, lat, P("img", None, "pix")) + (whole,) * 15,
        check_vma=False,
    )
```

```python
import math

import jax
import jax.numpy as jnp
import numpy as np
from jax import lax
from jax.experimental import pallas as pl
from jax.experimental.pallas import tpu as pltpu
from jax.sharding import PartitionSpec as P

BANDS = 64
GRID = 224
EPSILON = 1e-05
FLOOR = -1e30
BLOCK = 16
LANES = 128
BF = jnp.bfloat16
F32 = jnp.float32
VM = pl.BlockSpec(memory_space=pltpu.VMEM)
HBM = pl.BlockSpec(memory_space=pltpu.HBM)
MIB = 1 << 20
MAKE, MAKEU = 256, 6
POOL, POOLU = 256, 6
PULL, PULLU = 1024, 3
STRIP = 256


def fourier_lookup():
    position = np.arange(GRID, dtype=np.float32) * np.float32(2.0 / (GRID - 1)) - np.float32(1.0)
    frequency = np.float32(1.0) + np.arange(BANDS, dtype=np.float32) * np.float32(
        (GRID / 2.0 - 1.0) / (BANDS - 1)
    )
    phases = position[None, :] * (np.float32(math.pi) * frequency)[:, None]
    waves = np.concatenate([np.sin(phases.astype(np.float64)), np.cos(phases.astype(np.float64))])
    return waves.astype(np.float32)


def split_numpy(values):
    parts = []
    for _ in range(3):
        part = values.astype(BF).astype(np.float64)
        parts.append(part)
        values = values - part
    return parts


def lookup_with_sums():
    waves = fourier_lookup().astype(BF).astype(np.float64)
    sums = split_numpy(waves.sum(axis=0)) + split_numpy((waves * waves).sum(axis=0))
    table = np.zeros((2 * BANDS + 16, GRID))
    table[: 2 * BANDS] = waves
    table[2 * BANDS : 2 * BANDS + 6] = np.stack(sums)
    return table


def split(values):
    parts = []
    for _ in range(3):
        part = values.astype(BF)
        parts.append(part)
        values = values - part.astype(F32)
    return parts


def contract(left, right, left_dim, right_dim):
    return lax.dot_general(
        left, right, (((left_dim,), (right_dim,)), ((), ())), preferred_element_type=F32
    )


def norm_stats(values, axis):
    centre = values - jnp.mean(values, axis=axis, keepdims=True)
    spread = lax.rsqrt(jnp.mean(centre * centre, axis=axis, keepdims=True) + EPSILON)
    return centre * spread, spread


def norm_back(upstream, gain, unit, spread, axis):
    inner = upstream * gain
    return spread * (
        inner
        - jnp.mean(inner, axis=axis, keepdims=True)
        - unit * jnp.mean(inner * unit, axis=axis, keepdims=True)
    )


def out(shape, dtype):
    return jax.ShapeDtypeStruct(shape, dtype)


def padded(rows, step):
    return -(-rows // step) * step


def lane_ids(shape):
    return lax.broadcasted_iota(jnp.int32, shape, len(shape) - 1)


def waves_first(values, features):
    width = values.shape[1]
    lead = features - 4 * BANDS
    at = lane_ids(values.shape)
    waves = pltpu.roll(values, width - lead, 1)
    rest = pltpu.roll(values, 4 * BANDS, 1)
    return jnp.where(at < 4 * BANDS, waves, jnp.where(at < features, rest, 0.0))


def waves_last(values, features):
    width = values.shape[1]
    lead = features - 4 * BANDS
    at = lane_ids(values.shape)
    rest = pltpu.roll(values, width - 4 * BANDS, 1)
    waves = pltpu.roll(values, lead, 1)
    return jnp.where(at < lead, rest, jnp.where(at < features, waves, 0.0))


def fold(values):
    total = values[:, :LANES]
    for start in range(LANES, values.shape[1], LANES):
        total = total + values[:, start : start + LANES]
    return total


def fold_max(values):
    total = values[:, :LANES]
    for start in range(LANES, values.shape[1], LANES):
        total = jnp.maximum(total, values[:, start : start + LANES])
    return total


def fold_rows(values):
    total = values[:8]
    for start in range(8, values.shape[0], 8):
        total = total + values[start : start + 8]
    return total


def slot_of(kept_row):
    own = kept_row.shape[1]
    shape = (own, own)
    upper = lax.broadcasted_iota(jnp.int32, shape, 0) <= lax.broadcasted_iota(jnp.int32, shape, 1)
    tall = jnp.broadcast_to(kept_row, (8, own)).astype(BF)
    rank = jnp.dot(tall, jnp.where(upper, 1.0, 0.0).astype(BF), preferred_element_type=F32)[:1]
    slot = jnp.where(kept_row > 0, rank - 1.0, -1.0)
    return slot == lax.broadcasted_iota(jnp.int32, shape, 0).astype(F32)


class Fetch:
    def __init__(self, source, target, sem):
        self.copy = pltpu.make_async_copy(source, target, sem)
        self.target = target
        self.waiting = True

    def start(self):
        self.copy.start()

    def get(self):
        if self.waiting:
            self.copy.wait()
            self.waiting = False
        return self.target


def row_of(fetch):
    return fetch.get()[...].reshape(1, -1)


def pack_kernel(pixels, coords, kept, packed, rows):
    rows[...] = jnp.zeros_like(rows)
    rows[0:3, :] = pixels.get()[:, 0, :]
    rows[3:5, :] = coords.get()[...].astype(F32)
    kept_row = kept.get()[...].astype(F32)
    rows[5:6, :] = kept_row
    slots = jnp.where(slot_of(kept_row), 1.0, 0.0).astype(BF)
    squeezed = contract(rows[...].astype(BF), slots, 1, 1).astype(BF)
    packed[...] = jnp.broadcast_to(squeezed[None], packed.shape)


def pad_rows(target, source):
    rows = source.shape[0]
    whole = rows // LANES * LANES
    target[:whole, :] = source[:whole, :]
    target[whole:, :] = jnp.zeros_like(target[whole:, :])
    target[whole:rows, :] = source[whole:, :]


def turn_blocks(target, source):
    size = source.shape[0]
    for start in range(0, source.shape[1], size):
        span = slice(start, start + size)
        target[:, span] = jnp.transpose(source[:, span].astype(F32)).astype(BF)


def turn_pool(target, pool):
    count, tall = pool.shape
    turned = jnp.transpose(pool).astype(BF)
    target[...] = jnp.zeros_like(target)
    for at, start in enumerate(range(0, tall, count)):
        height = min(count, tall - start)
        target[:height, at * count : (at + 1) * count] = turned[start : start + height]


def query_kernel(
    features, latent, gain, shift, weight, bias, key_raw, in_gain, grad, down, in_shift,
    value_bias, mlp_gain, mlp_shift, up_bias, down_bias, table,
    early, absorbed, scorer, hidden_grad, table_kept, rows, ends, one, key,
):
    latent = latent.get()
    count, dim = latent.shape
    tall = absorbed.shape[1]
    turned, query, kept_grad = (early.at[:, at * dim : (at + 1) * dim] for at in range(3))
    step = 32
    lat_gain, lat_shift = row_of(gain), row_of(shift)
    for start in range(0, count, step):
        unit, _ = norm_stats(latent[start : start + step, :].astype(F32), 1)
        one[start : start + step, :] = (unit * lat_gain + lat_shift).astype(BF)
    bias, weight = row_of(bias), weight.get()
    step = 256
    for start in range(0, dim, step):
        part = jnp.dot(one[...], weight[:, start : start + step], preferred_element_type=F32)
        query[:, start : start + step] = (part + bias[:, start : start + step]).astype(BF)
    turn_blocks(turned, one)
    pad_rows(key, key_raw.get())
    lifted = contract(query[...], key[...], 1, 1) * (1.0 / math.sqrt(dim))
    lifted = waves_first(lifted, features)
    absorbed[...] = lifted
    gains = gain_row(in_gain, tall, features)
    scorer[...] = (lifted * gains * math.log2(math.e)).astype(BF)
    ends[...] = jnp.zeros_like(ends)
    ends[0:1, :] = gains
    ends[1:2, :] = gain_row(in_shift, tall, features)
    grad = grad.get()
    kept_grad[...] = grad[...]
    table_kept[...] = table.get()[...]
    rows[...] = jnp.zeros_like(rows)
    for at, vector in enumerate((value_bias, mlp_gain, mlp_shift, up_bias, down_bias)):
        rows[at : at + 1, :] = row_of(vector)
    rows[5:6, :] = lat_gain
    down = down.get()
    for start in range(0, dim, step):
        hidden_grad[:, start : start + step] = contract(grad[...], down[start : start + step, :], 1, 1)


def gain_row(fetch, width, features):
    row = row_of(fetch)
    wide = jnp.concatenate([row, jnp.zeros((1, width - features), F32)], axis=1)
    return waves_first(jnp.broadcast_to(wide, (8, width)), features)[:1]


def segment_counts(segments, stop):
    return [jnp.sum(segments[index][5:6, :].astype(F32)).astype(jnp.int32) for index in range(stop)]


def forward_kernel(
    features,
    segments, scorer, hidden_grad, early, table, latent, value_raw, up, down, rows, ends,
    encoded_out, packs, mixed_grad, lift_out, puller, unit_out, spread_out, score_out, pool_unit, stats, sums,
    placed, places, top, pooled, mixed, mix_unit, mix_spread, value, hidden, two, pool_low, encoded, out_sem,
):
    pix, _, own = segments.shape
    tall, kept = unit_out.shape
    waves = 4 * BANDS
    ones = slice(features, waves + 8)

    placed[...] = jnp.zeros_like(placed)
    offset = jnp.int32(0)
    for index, found in enumerate(segment_counts(segments, pix)):
        wide = jnp.concatenate([segments[index].astype(F32), jnp.zeros((8, LANES), F32)], axis=1)
        inside = lax.rem(offset, LANES)
        base = pl.multiple_of(jnp.minimum(offset - inside, kept), LANES)
        placed[:, pl.ds(base, own + LANES)] += pltpu.roll(wide, inside, 1)
        offset = offset + found
    places[...] = lax.broadcasted_iota(jnp.int32, places.shape, 0).astype(F32).astype(BF)
    unit_out[waves + 16 :, :] = jnp.zeros((tall - waves - 16, kept), BF)
    top[...] = jnp.full_like(top, FLOOR)

    step = MAKE

    def make(index, carry):
        lanes = pl.ds(pl.multiple_of(index * step, LANES), step)
        raw = placed[:, lanes]
        column = jnp.concatenate([places[...]] * (step // LANES), axis=1)
        one, none = jnp.ones((), BF), jnp.zeros((), BF)
        row_hot = jnp.where(column == raw[3:4].astype(BF), one, none)
        col_hot = jnp.where(column == raw[4:5].astype(BF), one, none)
        row_waves = jnp.dot(table[...], row_hot, preferred_element_type=F32)
        col_waves = jnp.dot(table[...], col_hot, preferred_element_type=F32)
        at = lax.broadcasted_iota(jnp.int32, raw.shape, 0)
        position = (raw * (2.0 / (GRID - 1)) - 1.0).astype(BF).astype(F32)
        extra = jnp.where(at < 3, raw, jnp.where(at < 5, position, 0.0))
        both = row_waves[2 * BANDS :] + col_waves[2 * BANDS :]
        mean = (
            jnp.sum(both[0:3], axis=0, keepdims=True) + jnp.sum(extra, axis=0, keepdims=True)
        ) * (1.0 / features)
        square = (
            jnp.sum(both[3:6], axis=0, keepdims=True) + jnp.sum(extra * extra, axis=0, keepdims=True)
        ) * (1.0 / features)
        spread = lax.rsqrt(jnp.maximum(square - mean * mean, 0.0) + EPSILON)
        centre = mean * spread
        spread_out[:, lanes] = jnp.broadcast_to(spread, (8, step))
        for piece, start in (
            (row_waves[:BANDS], 0),
            (col_waves[:BANDS], BANDS),
            (row_waves[BANDS : 2 * BANDS], 2 * BANDS),
            (col_waves[BANDS : 2 * BANDS], 3 * BANDS),
        ):
            unit_out[start : start + BANDS, lanes] = (piece * spread - centre).astype(BF)
        tail = jnp.where(at < features - waves, extra * spread - centre, 1.0)
        tail = jnp.concatenate([tail, jnp.zeros((8, step), F32)], axis=0)
        unit_out[waves : waves + 16, lanes] = tail.astype(BF)
        score = jnp.dot(scorer[...], unit_out[:, lanes], preferred_element_type=F32)
        score_out[:, lanes] = score
        top[...] = jnp.maximum(top[...], fold_max(score))
        return carry

    lax.fori_loop(0, kept // step, make, 0, unroll=MAKEU)
    peak = jnp.max(top[...], axis=1, keepdims=True)
    top[...] = jnp.broadcast_to(peak, top.shape)
    pooled[...] = jnp.zeros_like(pooled)

    step = POOL

    def pool(index, carry):
        lanes = pl.ds(pl.multiple_of(index * step, LANES), step)
        weight = jnp.exp2(score_out[:, lanes] - top[:, :1])
        pooled[...] += contract(weight.astype(BF), unit_out[:, lanes], 1, 1)
        return carry

    lax.fori_loop(0, kept // step, pool, 0, unroll=POOLU)
    total = pooled[:, features : features + 1]
    pool_unit[...] = pooled[...] * (1.0 / total)
    latent, value_raw, up, down = latent.get(), value_raw.get(), up.get(), down.get()
    gains, shifts = ends[0:1, :], ends[1:2, :]
    count, dim = mixed.shape
    grad = early.at[:, 2 * dim :]
    value_bias, gain, shift, up_bias, down_bias = (rows[at : at + 1, :] for at in range(5))
    hidden_turned, two_turned, pre_grad, attn_grad = (packs.at[:, at * dim : (at + 1) * dim] for at in range(4))
    pool = waves_last(pool_unit[...] * gains + shifts, features)
    pool_low[...] = pool.astype(BF)
    turn_pool(packs.at[:, 4 * dim :], pool)

    pad_rows(value, value_raw)
    wide = 256
    for start in range(0, dim, wide):
        span = slice(start, start + wide)
        attn = jnp.dot(pool_low[...], value[:, span], preferred_element_type=F32) + value_bias[:, span]
        mixed[:, span] = latent[:, span].astype(F32) + attn
    low = 32
    for start in range(0, count, low):
        span = slice(start, start + low)
        unit, spread = norm_stats(mixed[span, :], 1)
        mix_unit[span, :] = unit
        mix_spread[span, :] = jnp.broadcast_to(spread, (low, LANES))
        two[span, :] = (unit * gain + shift).astype(BF)
    turn_blocks(two_turned, two)
    for start in range(0, dim, wide):
        span = slice(start, start + wide)
        act = jnp.dot(two[...], up[:, span], preferred_element_type=F32) + up_bias[:, span]
        half = 0.5 * (1.0 + lax.erf(act * (1.0 / math.sqrt(2.0))))
        active = act * half
        hidden[:, span] = active.astype(BF)
        hidden_turned[:, span] = jnp.transpose(active).astype(BF)
        slope = half + act * jnp.exp(-0.5 * act * act) * (1.0 / math.sqrt(2.0 * math.pi))
        pre_grad[:, span] = (hidden_grad[:, span] * slope).astype(BF)
    for start in range(0, dim, wide):
        span = slice(start, start + wide)
        part = jnp.dot(hidden[...], down[:, span], preferred_element_type=F32)
        encoded[:, span] = (mixed[:, span] + part + down_bias[:, span]).astype(BF)
    leave = pltpu.make_async_copy(encoded, encoded_out, out_sem)
    leave.start()
    for start in range(0, dim, wide):
        span = slice(start, start + wide)
        mixed[:, span] = contract(pre_grad[...], up[span, :], 1, 1)
    gain_sum = jnp.zeros((8, dim), F32)
    shift_sum = jnp.zeros((8, dim), F32)
    for start in range(0, count, low):
        span = slice(start, start + low)
        upstream = mixed[span, :]
        unit = mix_unit[span, :]
        full = grad[span, :].astype(F32) + norm_back(upstream, gain, unit, mix_spread[span, :1], 1)
        mixed_grad[span, :] = full
        attn_grad[span, :] = full.astype(BF)
        gain_sum = gain_sum + fold_rows(upstream * unit)
        shift_sum = shift_sum + fold_rows(upstream)
    sums[0:1, :] = jnp.sum(gain_sum, axis=0, keepdims=True)
    sums[1:2, :] = jnp.sum(shift_sum, axis=0, keepdims=True)
    lifted = waves_first(contract(attn_grad[...], value[...], 1, 1), features)
    lift_out[...] = lifted
    pulled = (lifted * gains).astype(BF)
    at = lane_ids(pulled.shape)
    inside = jnp.where(at < features, pulled.astype(F32) * pool_unit[...], 0.0)
    delta = jnp.sum(inside, axis=1, keepdims=True)
    for lane, part in enumerate(split(-delta)):
        pulled = jnp.where(at == features + lane, part, pulled)
    puller[...] = pulled
    at = lane_ids(stats.shape)
    stats[...] = jnp.where(at == 0, peak + jnp.log2(total), delta)
    leave.wait()


def pull_kernel(
    features,
    segments, kept_row, absorbed, lifted, puller, unit_in, spread_in, score, pool_unit, stats,
    key_raw, sums, ends, query_weight, latent, rows, mixed_grad,
    late, vectors, color_out, latent_out,
    pooled, key, color_grad, back, latent_grad, out_sems,
):
    count, dim = pooled.shape[0], key.shape[1]
    own = segments.shape[2]
    tall, kept = unit_in.shape
    waves = 4 * BANDS
    pooled[...] = jnp.zeros_like(pooled)

    def shares(lanes):
        inner = jnp.dot(puller[...], unit_in[:, lanes], preferred_element_type=F32)
        prob = jnp.exp2(score[:, lanes] - stats[:, :1])
        return inner, prob, (prob * inner).astype(BF)

    step = PULL

    def pull(index, carry):
        lanes = pl.ds(pl.multiple_of(index * step, LANES), step)
        pooled[...] += contract(shares(lanes)[2], unit_in[:, lanes], 1, 1)
        return carry

    lax.fori_loop(0, kept // step, pull, 0, unroll=PULLU)
    gains, shifts = ends[0:1, :], ends[1:2, :]
    kept_row, key_raw, query_weight, latent = kept_row.get(), key_raw.get(), query_weight.get(), latent.get()

    mine = lax.axis_index("pix")
    offset = jnp.int32(0)
    for index, found in enumerate(segment_counts(segments, segments.shape[0])):
        offset = offset + jnp.where(index < mine, found, 0)
    inside = lax.rem(offset, LANES)
    base = pl.multiple_of(jnp.minimum(offset - inside, kept - own - LANES), LANES)
    inside = offset - base
    lanes = pl.ds(base, own + LANES)
    inner, prob, score_grad = shares(lanes)
    tilt = score_grad.astype(F32) * score[:, lanes] * math.log(2.0) + prob * (inner + stats[:, 1:2])
    tilt = jnp.sum(tilt, axis=0, keepdims=True) * (1.0 / features)
    factors = []
    for held in (absorbed, lifted):
        scaled = held[...] * gains
        at = lane_ids((count, LANES))
        corner = jnp.where(at == 3, jnp.sum(scaled, axis=1, keepdims=True), scaled[:, waves : waves + LANES])
        factors.append(jnp.transpose(corner)[:8].astype(BF))
    both = jnp.concatenate([score_grad, prob.astype(BF)], axis=0)
    terms = jnp.dot(jnp.concatenate(factors, axis=1), both, preferred_element_type=F32)
    unit = unit_in[waves : waves + 16, lanes].astype(F32)[:8]
    colors = spread_in[:, lanes] * (terms - terms[3:4] * (1.0 / features) - unit * tilt)
    window = pltpu.roll(colors, own + LANES - inside, 1)[:, :own]
    slots = jnp.where(slot_of(kept_row[...].astype(F32)), 1.0, 0.0)
    spread_back = jnp.dot(window, slots, precision=lax.Precision.HIGHEST, preferred_element_type=F32)
    color_grad[:, 0, :] = spread_back[:3]

    held = pooled[...]
    total = held[:, features : features + 1]
    pool = waves_last(held * gains + shifts * total, features)
    turn_pool(late.at[:, dim:], pool)
    pool = pool.astype(BF)
    pad_rows(key, key_raw)
    gain_sum = absorbed[...] * held + lifted[...] * pool_unit[...]
    shift_sum = absorbed[...] * total + lifted[...]
    vectors[...] = jnp.zeros_like(vectors)
    for at, found in ((4, gain_sum), (5, shift_sum)):
        flat = jnp.sum(fold_rows(found), axis=0, keepdims=True)
        vectors[at : at + 1, :tall] = waves_last(jnp.broadcast_to(flat, (8, tall)), features)[:1]
    wide = 256
    for start in range(0, dim, wide):
        span = slice(start, start + wide)
        part = jnp.dot(pool, key[:, span], preferred_element_type=F32) * (1.0 / math.sqrt(dim))
        late[:, span] = part.astype(BF)
    vectors[2:4, :] = sums[0:2, :]
    for start in range(0, dim, wide):
        span = slice(start, start + wide)
        back[:, span] = contract(late[:, :dim], query_weight[span, :], 1, 1)
    low = 32
    gain = rows[5:6, :]
    gain_sum = jnp.zeros((8, dim), F32)
    shift_sum = jnp.zeros((8, dim), F32)
    for start in range(0, count, low):
        span = slice(start, start + low)
        unit, spread = norm_stats(latent[span, :].astype(F32), 1)
        upstream = back[span, :]
        latent_grad[span, :] = mixed_grad[span, :] + norm_back(upstream, gain, unit, spread, 1)
        gain_sum = gain_sum + fold_rows(upstream * unit)
        shift_sum = shift_sum + fold_rows(upstream)
    vectors[0:1, :] = jnp.sum(gain_sum, axis=0, keepdims=True)
    vectors[1:2, :] = jnp.sum(shift_sum, axis=0, keepdims=True)
    leave = [
        pltpu.make_async_copy(color_grad, color_out, out_sems.at[0]),
        pltpu.make_async_copy(latent_grad, latent_out, out_sems.at[1]),
    ]
    for copy in leave:
        copy.start()
    for copy in leave:
        copy.wait()


class Leaving:
    def __init__(self, buffers, sems):
        self.buffers, self.sems, self.flying, self.turn = buffers, sems, {}, 0

    def free(self):
        slot = self.turn % self.buffers.shape[0]
        if slot in self.flying:
            self.flying[slot].wait()
        return self.buffers.at[slot]

    def send(self, target):
        slot = self.turn % self.buffers.shape[0]
        self.turn += 1
        self.flying[slot] = pltpu.make_async_copy(self.buffers.at[slot], target, self.sems.at[slot])
        self.flying[slot].start()

    def end(self):
        for copy in self.flying.values():
            copy.wait()


def parts_of(ref, dim):
    squares = ref.shape[1] // dim
    parts = [ref.at[:, at * dim : (at + 1) * dim] for at in range(squares)]
    return parts + ([ref.at[:, squares * dim :]] if ref.shape[1] % dim else [])


def products(leaving, left, left_far, right, right_far, target, bias):
    count = left.shape[0]
    size = leaving.buffers.shape[1]
    for start in range(0, left.shape[1], size):
        buffer = leaving.free()
        at, inner = start // count * count, start % count
        rows, lanes = slice(inner, inner + size), slice(at, at + count)
        strip = jnp.concatenate([left[rows, lanes], left_far[rows, lanes]], axis=1)
        if bias is not None and start == 0:
            strip = jnp.concatenate([strip, jnp.ones((16, 2 * count), BF)], axis=0)
        found = jnp.dot(strip, jnp.concatenate([right[...], right_far[...]], axis=0), preferred_element_type=F32)
        buffer[...] = found[:size]
        if bias is not None and start == 0:
            bias[...] = found[size]
        leaving.send(target.at[start : start + size, :])


def short_product(held, left, left_far, right, right_far, bias, scale):
    features, count = held.shape[0], left.shape[0]
    pieces = []
    for at, start in enumerate(range(0, features, count)):
        height = min(count, padded(features - start, 16))
        lanes = slice(at * count, (at + 1) * count)
        pieces.append(jnp.concatenate([left[:height, lanes], left_far[:height, lanes]], axis=1))
    high = sum(piece.shape[0] for piece in pieces)
    pieces.append(jnp.ones((16, 2 * count), BF))
    both = jnp.concatenate([right[...], right_far[...]], axis=0)
    found = jnp.dot(jnp.concatenate(pieces, axis=0), both, preferred_element_type=F32)
    held[...] = found[:features] if scale is None else found[:features] * scale
    if bias is not None:
        bias[...] = found[high]


def late_kernel(
    features,
    packs, packs_far, early, early_far,
    down_out, down_bias, up_out, up_bias, value_out, value_bias,
    buffers, held, sems, held_sem,
):
    dim = down_out.shape[1]
    hidden, two, pre, attn, pool = parts_of(packs, dim)
    hidden_far, two_far, pre_far, attn_far, pool_far = parts_of(packs_far, dim)
    grad, grad_far = parts_of(early, dim)[2], parts_of(early_far, dim)[2]
    leaving = Leaving(buffers, sems)
    products(leaving, hidden, hidden_far, grad, grad_far, down_out, down_bias)
    short_product(held, pool, pool_far, attn, attn_far, value_bias, None)
    leave = pltpu.make_async_copy(held, value_out, held_sem)
    leave.start()
    products(leaving, two, two_far, pre, pre_far, up_out, up_bias)
    leave.wait()
    leaving.end()


def last_kernel(
    features,
    early, early_far, late, late_far, vectors, vectors_far, _,
    query_out, query_bias, key_out, lat_gain, lat_shift, mlp_gain, mlp_shift, in_gain, in_shift,
    buffers, held, sems, held_sem,
):
    dim = query_out.shape[1]
    one, query, _ = parts_of(early, dim)
    one_far, query_far, _ = parts_of(early_far, dim)
    grad, pool = parts_of(late, dim)
    grad_far, pool_far = parts_of(late_far, dim)
    leaving = Leaving(buffers, sems)
    products(leaving, one, one_far, grad, grad_far, query_out, query_bias)
    short_product(held, pool, pool_far, query, query_far, None, 1.0 / math.sqrt(dim))
    short = pltpu.make_async_copy(held, key_out, held_sem)
    short.start()
    sums = vectors[...] + vectors_far[...]
    lat_gain[...] = sums[0]
    lat_shift[...] = sums[1]
    mlp_gain[...] = sums[2]
    mlp_shift[...] = sums[3]
    in_gain[...] = sums[4, :features]
    in_shift[...] = sums[5, :features]
    leaving.end()
    short.wait()


def call(body, outs, args, fetched, scratch, vmem, flops, moved, unread=()):
    places = [at for at in range(len(args)) if at in fetched]
    buffers = [pltpu.VMEM(args[at].shape, args[at].dtype) for at in places]
    shapes = tuple(out(shape, dtype) for shape, dtype, _ in outs)

    def whole(*refs):
        sources, rest = list(refs[: len(args)]), refs[len(args) :]
        targets = ()
        if places:
            targets, sems, rest = rest[-len(buffers) - 1 : -1], rest[-1], rest[: -len(buffers) - 1]
        for slot, (at, target) in enumerate(zip(places, targets)):
            sources[at] = Fetch(sources[at], target, sems.at[slot])
            sources[at].start()
        body(*sources, *rest)
        for at in places:
            sources[at].get()

    return pl.pallas_call(
        whole,
        out_shape=shapes if len(shapes) > 1 else shapes[0],
        in_specs=tuple(HBM if at in fetched or at in unread else VM for at in range(len(args))),
        out_specs=tuple(place for _, _, place in outs) if len(outs) > 1 else outs[0][2],
        scratch_shapes=list(scratch) + buffers + ([pltpu.SemaphoreType.DMA((len(places),))] if places else []),
        compiler_params=pltpu.CompilerParams(vmem_limit_bytes=vmem * MIB),
        cost_estimate=pl.CostEstimate(flops=flops, bytes_accessed=moved, transcendentals=0),
    )(*(pltpu.with_memory_space_constraint(arg, pltpu.HBM) if at in fetched or at in unread else arg for at, arg in enumerate(args)))


def on_chip(
    latents, pixels, coords, kept_mask, lat_gain, lat_shift, query_weight, query_bias, in_gain, in_shift,
    key_weight, value_weight, value_bias, mlp_gain, mlp_shift, up_weight, up_bias, down_weight, down_bias,
    cotangent,
):
    pix = lax.axis_size("pix")
    own = pixels.shape[2]
    kept = pix * own // 2
    _, count, dim = latents.shape
    features = in_gain.shape[0]
    tall = padded(features, LANES)
    latent, out_grad = latents[0], cotangent[0]
    swap = [(0, 1), (1, 0)]

    def other(value):
        return lax.ppermute(value, "img", swap)

    packed = call(
        pack_kernel, [((pix, 8, own), BF, VM)], (pixels.transpose(1, 0, 2), coords[0], kept_mask), (0, 1, 2),
        [pltpu.VMEM((8, own), F32)], 8, 4 * 8 * own * own, 16 * 8 * own,
    )
    segments = lax.all_to_all(packed, "pix", 0, 0)

    table = jnp.asarray(lookup_with_sums(), BF)
    wide = pltpu.VMEM((tall, dim), BF)
    early, absorbed, scorer, hidden_grad, table_kept, rows, ends = call(
        lambda *refs: query_kernel(features, *refs),
        [
            ((count, 3 * dim), BF, VM), ((count, tall), F32, VM), ((count, tall), BF, VM), ((count, dim), F32, VM),
            (table.shape, BF, VM), ((8, dim), F32, VM), ((8, tall), F32, VM),
        ],
        (
            latent, lat_gain, lat_shift, query_weight, query_bias, key_weight, in_gain, out_grad, down_weight,
            in_shift, value_bias, mlp_gain, mlp_shift, up_bias, down_bias, table,
        ),
        tuple(range(16)), [pltpu.VMEM((count, dim), BF), wide],
        14, 4 * count * dim * dim + 2 * count * dim * tall, 8 * MIB,
    )

    narrow = pltpu.VMEM((count, LANES), F32)
    area = pltpu.VMEM((count, dim), F32)
    low = pltpu.VMEM((count, dim), BF)
    spare = 512
    (
        encoded, packs, mixed_grad, lifted, puller, unit_in, spread_in, score, pool_unit, stats, sums,
    ) = call(
        lambda *refs: forward_kernel(features, *refs),
        [
            ((count, dim), BF, HBM), ((count, 4 * dim + spare), BF, VM), ((count, dim), F32, VM),
            ((count, tall), F32, VM), ((count, tall), BF, VM), ((tall, kept), BF, VM), ((8, kept), F32, VM),
            ((count, kept), F32, VM), ((count, tall), F32, VM), ((count, LANES), F32, VM), ((8, dim), F32, VM),
        ],
        (
            segments, scorer, hidden_grad, early, table_kept, latent, value_weight, up_weight, down_weight, rows, ends,
        ),
        (5, 6, 7, 8),
        [
            pltpu.VMEM((8, kept + own + LANES), F32), pltpu.VMEM((GRID, LANES), BF), narrow,
            pltpu.VMEM((count, tall), F32), area, area, narrow, wide, low, low, pltpu.VMEM((count, tall), BF), low,
            pltpu.SemaphoreType.DMA(()),
        ],
        20, 6 * count * dim * dim + 4 * count * dim * tall + 6 * kept * count * tall, 8 * MIB,
    )

    late, vectors, color_grad, latent_grad = call(
        lambda *refs: pull_kernel(features, *refs),
        [((count, dim + spare), BF, VM), ((8, dim), F32, VM), ((3, 1, own), F32, HBM), ((count, dim), F32, HBM)],
        (
            segments, kept_mask, absorbed, lifted, puller, unit_in, spread_in, score, pool_unit, stats, key_weight,
            sums, ends, query_weight, latent, rows, mixed_grad,
        ),
        (1, 10, 13, 14),
        [
            pltpu.VMEM((count, tall), F32), wide, pltpu.VMEM((3, 1, own), F32), area, area,
            pltpu.SemaphoreType.DMA((2,)),
        ],
        16, 2 * count * dim * dim + 4 * kept * count * tall, 8 * MIB,
    )

    early_far = other(early)
    packs_far = other(packs)
    late_far = other(late)
    vectors_far = other(vectors)
    square = ((dim, dim), F32, HBM)
    slab = ((features, dim), F32, HBM)
    line = ((dim,), F32, VM)
    short = ((features,), F32, VM)
    slots = [
        pltpu.VMEM((4, STRIP, dim), F32), pltpu.VMEM((features, dim), F32),
    ]
    sems = [pltpu.SemaphoreType.DMA((4,)), pltpu.SemaphoreType.DMA(())]
    down_weight_grad, down_bias_grad, up_weight_grad, up_bias_grad, value_weight_grad, value_bias_grad = call(
        lambda *refs: late_kernel(features, *refs),
        [square, line, square, line, slab, line], (packs, packs_far, early, early_far), (),
        slots + sems, 12, 8 * count * dim * dim + 4 * count * dim * tall, 10 * MIB,
    )
    (
        query_weight_grad, query_bias_grad, key_weight_grad, lat_gain_grad, lat_shift_grad, mlp_gain_grad,
        mlp_shift_grad, in_gain_grad, in_shift_grad,
    ) = call(
        lambda *refs: last_kernel(features, *refs),
        [square, line, slab, line, line, line, line, short, short],
        (
            early, early_far, late, late_far, vectors, vectors_far, down_weight_grad,
        ),
        (), slots + sems, 12, 4 * count * dim * dim + 4 * count * dim * tall, 6 * MIB, (6,),
    )

    return (
        encoded[None], latent_grad[None], color_grad.transpose(1, 0, 2), lat_gain_grad, lat_shift_grad,
        query_weight_grad, query_bias_grad, in_gain_grad, in_shift_grad, key_weight_grad, value_weight_grad,
        value_bias_grad, mlp_gain_grad, mlp_shift_grad, up_weight_grad, up_bias_grad, down_weight_grad, down_bias_grad,
    )


def in_blocks(
    latents,
    pixels,
    coords,
    kept_mask,
    lat_gain,
    lat_shift,
    query_weight,
    query_bias,
    in_gain,
    in_shift,
    key_weight,
    value_weight,
    value_bias,
    mlp_gain,
    mlp_shift,
    up_weight,
    up_bias,
    down_weight,
    down_bias,
    cotangent,
):
    pix = lax.axis_size("pix")
    mine = lax.axis_index("pix")
    own = pixels.shape[2]
    packed = jnp.concatenate(
        [
            pixels[0].astype(BF),
            coords[0].astype(BF),
            kept_mask.astype(BF),
            jnp.zeros((2, own), BF),
        ],
        axis=0,
    )
    gathered = lax.all_to_all(jnp.broadcast_to(packed[None], (pix,) + packed.shape), "pix", 0, 0)
    every = gathered.transpose(1, 0, 2).reshape(packed.shape[0], pix * own)
    swap = [(0, 1), (1, 0)]

    def other(value):
        return lax.ppermute(value, "img", swap)

    root = math.sqrt(latents.shape[2])
    latent = latents[0].astype(F32)
    lat_unit, lat_spread = norm_stats(latent, 1)
    norm_one = (lat_unit * lat_gain + lat_shift).astype(BF)
    query = (jnp.dot(norm_one, query_weight, preferred_element_type=F32) + query_bias).astype(BF)
    absorbed = (contract(query, key_weight, 1, 1) * (1.0 / root)).astype(BF)

    waves = jnp.asarray(fourier_lookup(), BF)
    places = jnp.arange(GRID, dtype=F32)[:, None]

    def features(part):
        cells = part[3:5].astype(F32)
        position = (cells * (2.0 / (GRID - 1)) - 1.0).astype(BF)
        row_waves = jnp.dot(waves, (cells[0:1] == places).astype(BF), preferred_element_type=F32).astype(BF)
        col_waves = jnp.dot(waves, (cells[1:2] == places).astype(BF), preferred_element_type=F32).astype(BF)
        table = jnp.concatenate(
            [part[0:3], position, row_waves[:BANDS], col_waves[:BANDS], row_waves[BANDS:], col_waves[BANDS:]],
            axis=0,
        ).astype(F32)
        unit, spread = norm_stats(table, 0)
        x_in = (unit * in_gain[:, None] + in_shift[:, None]).astype(BF)
        score = jnp.dot(absorbed, x_in, preferred_element_type=F32)
        return unit, spread, x_in, jnp.where(part[5:6] > 0, score, FLOOR), part[5:6] > 0

    def pool(part, feats):
        unit, spread, x_in, score, live = feats
        top = jnp.max(score, axis=1, keepdims=True)
        weight = jnp.where(live, jnp.exp(score - top), 0.0)
        return top, jnp.sum(weight, axis=1, keepdims=True), contract(weight.astype(BF), x_in, 1, 1)

    blocks = max(1, pix // BLOCK)
    parts = every.reshape(packed.shape[0], blocks, -1).transpose(1, 0, 2)
    if blocks == 1:
        feats = features(parts[0])
        row_top, row_total, pooled = pool(parts[0], feats)
    else:

        def merge(carry, part):
            top, total, sums = pool(part, features(part))
            new_top = jnp.maximum(carry[0], top)
            old_scale, new_scale = jnp.exp(carry[0] - new_top), jnp.exp(top - new_top)
            return (
                new_top,
                carry[1] * old_scale + total * new_scale,
                carry[2] * old_scale + sums * new_scale,
            ), None

        start = (
            jnp.full((latent.shape[0], 1), FLOOR, F32),
            jnp.zeros((latent.shape[0], 1), F32),
            jnp.zeros((latent.shape[0], in_gain.shape[0]), F32),
        )
        row_top, row_total, pooled = lax.scan(merge, start, parts)[0]
    pooled = pooled / row_total
    pooled_low = pooled.astype(BF)
    attn = jnp.dot(pooled_low, value_weight, preferred_element_type=F32) + value_bias
    mixed = latent + attn
    mix_unit, mix_spread = norm_stats(mixed, 1)
    norm_two = (mix_unit * mlp_gain + mlp_shift).astype(BF)
    pre_act = jnp.dot(norm_two, up_weight, preferred_element_type=F32) + up_bias
    half_erf = 0.5 * (1.0 + lax.erf(pre_act * (1.0 / math.sqrt(2.0))))
    hidden = (pre_act * half_erf).astype(BF)
    encoded = (
        mixed + jnp.dot(hidden, down_weight, preferred_element_type=F32) + down_bias
    ).astype(BF)

    out_grad = cotangent[0]
    out_grad_full = out_grad.astype(F32)
    hidden_grad = contract(out_grad, down_weight, 1, 1)
    slope = half_erf + pre_act * jnp.exp(-0.5 * pre_act * pre_act) * (1.0 / math.sqrt(2.0 * math.pi))
    pre_grad = (hidden_grad * slope).astype(BF)
    norm_two_grad = contract(pre_grad, up_weight, 1, 1)
    mixed_grad = out_grad_full + norm_back(norm_two_grad, mlp_gain, mix_unit, mix_spread, 1)
    attn_grad = mixed_grad.astype(BF)

    lifted = contract(attn_grad, value_weight, 1, 1).astype(BF)
    row_delta = jnp.sum(lifted.astype(F32) * pooled, axis=1, keepdims=True)

    def pull(part, feats):
        unit, spread, x_in, score, live = feats
        prob = jnp.where(live, jnp.exp(score - row_top), 0.0) / row_total
        score_grad = (prob * (jnp.dot(lifted, x_in, preferred_element_type=F32) - row_delta)).astype(BF)
        score_pool = contract(score_grad, x_in, 1, 1)
        x_in_grad = contract(absorbed, score_grad, 0, 0) + contract(lifted, prob.astype(BF), 0, 0)
        gain_part = jnp.sum(x_in_grad * unit, axis=1)
        shift_part = jnp.sum(x_in_grad, axis=1)
        colour_part = norm_back(x_in_grad, in_gain[:, None], unit, spread, 0)[:3]
        return score_pool, gain_part, shift_part, colour_part

    if blocks == 1:
        score_pool, in_gain_grad, in_shift_grad, all_colors = pull(parts[0], feats)
    else:

        def gather_up(carry, part):
            found = pull(part, features(part))
            return tuple(kept + new for kept, new in zip(carry, found[:3])), found[3]

        start = (
            jnp.zeros((latent.shape[0], in_gain.shape[0]), F32),
            jnp.zeros_like(in_gain),
            jnp.zeros_like(in_shift),
        )
        (score_pool, in_gain_grad, in_shift_grad), stacked = lax.scan(gather_up, start, parts)
        all_colors = stacked.transpose(1, 0, 2).reshape(3, -1)
    color_grad = lax.dynamic_slice(all_colors, (0, mine * own), (3, own))
    score_pool_low = score_pool.astype(BF)
    query_grad = (
        jnp.dot(score_pool_low, key_weight, preferred_element_type=F32) * (1.0 / root)
    ).astype(BF)
    norm_one_grad = contract(query_grad, query_weight, 1, 1)
    latent_grad = mixed_grad + norm_back(norm_one_grad, lat_gain, lat_unit, lat_spread, 1)

    def both(value):
        return jnp.concatenate([value, other(value)], axis=0)

    out_both = both(out_grad)
    hidden_both = both(hidden)
    two_both = both(norm_two)
    pre_both = both(pre_grad)
    attn_both = both(attn_grad)
    one_both = both(norm_one)
    query_both = both(query)
    query_grad_both = both(query_grad)
    pool_both = both(pooled_low)
    score_both = both(score_pool_low)
    wide = jnp.stack(
        [
            jnp.sum(norm_one_grad * lat_unit, axis=0),
            jnp.sum(norm_one_grad, axis=0),
            jnp.sum(norm_two_grad * mix_unit, axis=0),
            jnp.sum(norm_two_grad, axis=0),
        ]
    )
    narrow = jnp.stack([in_gain_grad, in_shift_grad])
    wide = wide + other(wide)
    narrow = narrow + other(narrow)
    return (
        encoded[None],
        latent_grad[None],
        color_grad[None],
        wide[0],
        wide[1],
        contract(one_both, query_grad_both, 0, 0),
        jnp.sum(query_grad_both.astype(F32), axis=0),
        narrow[0],
        narrow[1],
        contract(score_both, query_both, 0, 0) * (1.0 / root),
        contract(pool_both, attn_both, 0, 0),
        jnp.sum(attn_both.astype(F32), axis=0),
        wide[2],
        wide[3],
        contract(two_both, pre_both, 0, 0),
        jnp.sum(pre_both.astype(F32), axis=0),
        contract(hidden_both, out_both, 0, 0),
        jnp.sum(out_both.astype(F32), axis=0),
    )


def shards(*args):
    pixels = args[1]
    kept = lax.axis_size("pix") * pixels.shape[2] // 2
    fits = kept <= 4096 and kept % (3 * PULL) == 0 and pixels.shape[2] % LANES == 0
    return (on_chip if fits else in_blocks)(*args)


def solution(mesh):
    lat = P("img", None, None)
    whole = P()
    return jax.shard_map(
        shards,
        mesh=mesh,
        in_specs=(lat, P("img", None, "pix"), P("img", None, "pix"), P("img", "pix"))
        + (whole,) * 15
        + (lat,),
        out_specs=(lat, lat, P("img", None, "pix")) + (whole,) * 15,
        check_vma=False,
    )
```

```python
import math

import jax
import jax.numpy as jnp
import numpy as np
from jax import lax
from jax.experimental import pallas as pl
from jax.experimental.pallas import tpu as pltpu
from jax.sharding import PartitionSpec as P

BANDS = 64
GRID = 224
EPSILON = 1e-05
FLOOR = -1e30
BLOCK = 16
LANES = 128
BF = jnp.bfloat16
F32 = jnp.float32
VM = pl.BlockSpec(memory_space=pltpu.VMEM)
HBM = pl.BlockSpec(memory_space=pltpu.HBM)
MIB = 1 << 20
MAKE = 256
SCORE = 1024
POOL = 512
PULL = 1024
WIDE = 256
STRIP = 256


def fourier_lookup():
    position = np.arange(GRID, dtype=np.float32) * np.float32(2.0 / (GRID - 1)) - np.float32(1.0)
    frequency = np.float32(1.0) + np.arange(BANDS, dtype=np.float32) * np.float32(
        (GRID / 2.0 - 1.0) / (BANDS - 1)
    )
    phases = position[None, :] * (np.float32(math.pi) * frequency)[:, None]
    waves = np.concatenate([np.sin(phases.astype(np.float64)), np.cos(phases.astype(np.float64))])
    return waves.astype(np.float32)


def split_numpy(values):
    parts = []
    for _ in range(3):
        part = values.astype(BF).astype(np.float64)
        parts.append(part)
        values = values - part
    return parts


def lookup_with_sums():
    waves = fourier_lookup().astype(BF).astype(np.float64)
    sums = split_numpy(waves.sum(axis=0)) + split_numpy((waves * waves).sum(axis=0))
    table = np.zeros((2 * BANDS + 16, GRID))
    table[: 2 * BANDS] = waves
    table[2 * BANDS : 2 * BANDS + 6] = np.stack(sums)
    return table


def split(values):
    parts = []
    for _ in range(3):
        part = values.astype(BF)
        parts.append(part)
        values = values - part.astype(F32)
    return parts


def contract(left, right, left_dim, right_dim):
    return lax.dot_general(
        left, right, (((left_dim,), (right_dim,)), ((), ())), preferred_element_type=F32
    )


def norm_stats(values, axis):
    centre = values - jnp.mean(values, axis=axis, keepdims=True)
    spread = lax.rsqrt(jnp.mean(centre * centre, axis=axis, keepdims=True) + EPSILON)
    return centre * spread, spread


def norm_back(upstream, gain, unit, spread, axis):
    inner = upstream * gain
    return spread * (
        inner
        - jnp.mean(inner, axis=axis, keepdims=True)
        - unit * jnp.mean(inner * unit, axis=axis, keepdims=True)
    )


def out(shape, dtype):
    return jax.ShapeDtypeStruct(shape, dtype)


def padded(rows, step):
    return -(-rows // step) * step


def lane_ids(shape):
    return lax.broadcasted_iota(jnp.int32, shape, len(shape) - 1)


def waves_first(values, features):
    width = values.shape[1]
    lead = features - 4 * BANDS
    at = lane_ids(values.shape)
    waves = pltpu.roll(values, width - lead, 1)
    rest = pltpu.roll(values, 4 * BANDS, 1)
    return jnp.where(at < 4 * BANDS, waves, jnp.where(at < features, rest, 0.0))


def waves_last(values, features):
    width = values.shape[1]
    lead = features - 4 * BANDS
    at = lane_ids(values.shape)
    rest = pltpu.roll(values, width - 4 * BANDS, 1)
    waves = pltpu.roll(values, lead, 1)
    return jnp.where(at < lead, rest, jnp.where(at < features, waves, 0.0))


def fold(values):
    total = values[:, :LANES]
    for start in range(LANES, values.shape[1], LANES):
        total = total + values[:, start : start + LANES]
    return total


def fold_max(values):
    total = values[:, :LANES]
    for start in range(LANES, values.shape[1], LANES):
        total = jnp.maximum(total, values[:, start : start + LANES])
    return total


def fold_rows(values):
    total = values[:8]
    for start in range(8, values.shape[0], 8):
        total = total + values[start : start + 8]
    return total


def slot_of(kept_row):
    own = kept_row.shape[1]
    shape = (own, own)
    upper = lax.broadcasted_iota(jnp.int32, shape, 0) <= lax.broadcasted_iota(jnp.int32, shape, 1)
    tall = jnp.broadcast_to(kept_row, (8, own)).astype(BF)
    rank = jnp.dot(tall, jnp.where(upper, 1.0, 0.0).astype(BF), preferred_element_type=F32)[:1]
    slot = jnp.where(kept_row > 0, rank - 1.0, -1.0)
    return slot == lax.broadcasted_iota(jnp.int32, shape, 0).astype(F32)


class Fetch:
    def __init__(self, source, target, sem):
        self.copy = pltpu.make_async_copy(source, target, sem)
        self.target = target
        self.waiting = True

    def start(self):
        self.copy.start()

    def get(self):
        if self.waiting:
            self.copy.wait()
            self.waiting = False
        return self.target


def row_of(fetch):
    return fetch.get()[...].reshape(1, -1)


def pack_kernel(pixels, coords, kept, packed, rows):
    rows[...] = jnp.zeros_like(rows)
    rows[0:3, :] = pixels.get()[:, 0, :]
    rows[3:5, :] = coords.get()[...].astype(F32)
    kept_row = kept.get()[...].astype(F32)
    rows[5:6, :] = kept_row
    slots = jnp.where(slot_of(kept_row), 1.0, 0.0).astype(BF)
    squeezed = contract(rows[...].astype(BF), slots, 1, 1).astype(BF)
    packed[...] = jnp.broadcast_to(squeezed[None], packed.shape)


def pad_rows(target, source):
    rows = source.shape[0]
    whole = rows // LANES * LANES
    target[:whole, :] = source[:whole, :]
    target[whole:, :] = jnp.zeros_like(target[whole:, :])
    target[whole:rows, :] = source[whole:, :]


def turn_blocks(target, source):
    size = source.shape[0]
    for start in range(0, source.shape[1], size):
        span = slice(start, start + size)
        target[:, span] = jnp.transpose(source[:, span].astype(F32)).astype(BF)


def turn_pool(target, pool):
    count, tall = pool.shape
    turned = jnp.transpose(pool).astype(BF)
    target[...] = jnp.zeros_like(target)
    for at, start in enumerate(range(0, tall, count)):
        height = min(count, tall - start)
        target[:height, at * count : (at + 1) * count] = turned[start : start + height]


def query_kernel(
    features, latent, gain, shift, weight, bias, key_raw, in_gain, grad, down, in_shift,
    value_bias, mlp_gain, mlp_shift, up_bias, down_bias, table, up_hbm,
    early_out, absorbed_out, scorer, hidden_grad, table_kept, rows, ends, up,
    one, key, early, absorbed, sems,
):
    bring = [pltpu.make_async_copy(up_hbm, up, sems.at[0])]
    latent = latent.get()
    count, dim = latent.shape
    tall = absorbed.shape[1]
    turned, query, kept_grad = (early.at[:, at * dim : (at + 1) * dim] for at in range(3))
    step = 32
    lat_gain, lat_shift = row_of(gain), row_of(shift)
    for start in range(0, count, step):
        unit, _ = norm_stats(latent[start : start + step, :].astype(F32), 1)
        one[start : start + step, :] = (unit * lat_gain + lat_shift).astype(BF)
    bias, weight = row_of(bias), weight.get()
    for copy in bring:
        copy.start()
    step = 256
    for start in range(0, dim, step):
        part = jnp.dot(one[...], weight[:, start : start + step], preferred_element_type=F32)
        query[:, start : start + step] = (part + bias[:, start : start + step]).astype(BF)
    turn_blocks(turned, one)
    pad_rows(key, key_raw.get())
    lifted = contract(query[...], key[...], 1, 1) * (1.0 / math.sqrt(dim))
    lifted = waves_first(lifted, features)
    absorbed[...] = lifted
    gains = gain_row(in_gain, tall, features)
    scorer[...] = (lifted * gains * math.log2(math.e)).astype(BF)
    ends[...] = jnp.zeros_like(ends)
    ends[0:1, :] = gains
    ends[1:2, :] = gain_row(in_shift, tall, features)
    grad = grad.get()
    kept_grad[...] = grad[...]
    leave = [
        pltpu.make_async_copy(early, early_out, sems.at[2]),
        pltpu.make_async_copy(absorbed, absorbed_out, sems.at[3]),
    ]
    for copy in leave:
        copy.start()
    table_kept[...] = table.get()[...]
    rows[...] = jnp.zeros_like(rows)
    for at, vector in enumerate((value_bias, mlp_gain, mlp_shift, up_bias, down_bias)):
        rows[at : at + 1, :] = row_of(vector)
    rows[5:6, :] = lat_gain
    down = down.get()
    for start in range(0, dim, step):
        part = contract(grad[...], down[start : start + step, :], 1, 1)
        hidden_grad[:, start : start + step] = part.astype(BF)
    for copy in bring + leave:
        copy.wait()


def gain_row(fetch, width, features):
    row = row_of(fetch)
    wide = jnp.concatenate([row, jnp.zeros((1, width - features), F32)], axis=1)
    return waves_first(jnp.broadcast_to(wide, (8, width)), features)[:1]


def segment_counts(segments, stop):
    return [jnp.sum(segments[index][5:6, :].astype(F32)).astype(jnp.int32) for index in range(stop)]


def forward_kernel(
    features,
    segments, scorer, hidden_grad, table, latent, value_raw, up, rows, ends, grad,
    hidden, mixed, packs, mixed_grad, lift_out, puller, unit_out, spread_out, score_out, pool_unit, stats, sums,
    placed, places, top, weight, pooled, back, mix_unit, mix_spread, value, two, pool_low,
):
    pix, _, own = segments.shape
    tall, kept = unit_out.shape
    waves = 4 * BANDS
    ones = slice(features, waves + 8)

    placed[...] = jnp.zeros_like(placed)
    offset = jnp.int32(0)
    for index, found in enumerate(segment_counts(segments, pix)):
        wide = jnp.concatenate([segments[index].astype(F32), jnp.zeros((8, LANES), F32)], axis=1)
        inside = lax.rem(offset, LANES)
        base = pl.multiple_of(jnp.minimum(offset - inside, kept), LANES)
        placed[:, pl.ds(base, own + LANES)] += pltpu.roll(wide, inside, 1)
        offset = offset + found
    places[...] = lax.broadcasted_iota(jnp.int32, places.shape, 0).astype(F32).astype(BF)
    unit_out[waves + 16 :, :] = jnp.zeros((tall - waves - 16, kept), BF)
    top[...] = jnp.full_like(top, FLOOR)

    for start in range(0, kept, MAKE):
        step = MAKE
        lanes = slice(start, start + step)
        raw = placed[:, lanes]
        column = jnp.concatenate([places[...]] * (step // LANES), axis=1)
        one, none = jnp.ones((), BF), jnp.zeros((), BF)
        row_hot = jnp.where(column == raw[3:4].astype(BF), one, none)
        col_hot = jnp.where(column == raw[4:5].astype(BF), one, none)
        row_waves = jnp.dot(table[...], row_hot, preferred_element_type=F32)
        col_waves = jnp.dot(table[...], col_hot, preferred_element_type=F32)
        at = lax.broadcasted_iota(jnp.int32, raw.shape, 0)
        position = (raw * (2.0 / (GRID - 1)) - 1.0).astype(BF).astype(F32)
        extra = jnp.where(at < 3, raw, jnp.where(at < 5, position, 0.0))
        both = row_waves[2 * BANDS :] + col_waves[2 * BANDS :]
        mean = (
            jnp.sum(both[0:3], axis=0, keepdims=True) + jnp.sum(extra, axis=0, keepdims=True)
        ) * (1.0 / features)
        square = (
            jnp.sum(both[3:6], axis=0, keepdims=True) + jnp.sum(extra * extra, axis=0, keepdims=True)
        ) * (1.0 / features)
        spread = lax.rsqrt(jnp.maximum(square - mean * mean, 0.0) + EPSILON)
        centre = mean * spread
        spread_out[:, lanes] = jnp.broadcast_to(spread, (8, step))
        for piece, low in (
            (row_waves[:BANDS], 0),
            (col_waves[:BANDS], BANDS),
            (row_waves[BANDS : 2 * BANDS], 2 * BANDS),
            (col_waves[BANDS : 2 * BANDS], 3 * BANDS),
        ):
            unit_out[low : low + BANDS, lanes] = (piece * spread - centre).astype(BF)
        tail = jnp.where(at < features - waves, extra * spread - centre, 1.0)
        tail = jnp.concatenate([tail, jnp.zeros((8, step), F32)], axis=0)
        unit_out[waves : waves + 16, lanes] = tail.astype(BF)
    for start in range(0, kept, SCORE):
        lanes = slice(start, start + SCORE)
        score = jnp.dot(scorer[...], unit_out[:, lanes], preferred_element_type=F32)
        score_out[:, lanes] = score
        top[...] = jnp.maximum(top[...], fold_max(score))
    peak = jnp.max(top[...], axis=1, keepdims=True)
    top[...] = jnp.broadcast_to(peak, top.shape)
    for start in range(0, kept, POOL):
        lanes = slice(start, start + POOL)
        weight[:, lanes] = jnp.exp2(score_out[:, lanes] - top[:, :1]).astype(BF)
    pooled[...] = contract(weight[...], unit_out[...], 1, 1)
    total = pooled[:, features : features + 1]
    pool_unit[...] = pooled[...] * (1.0 / total)
    gains, shifts = ends[0:1, :], ends[1:2, :]
    count, dim = mixed.shape
    value_bias, gain, shift, up_bias = (rows[at : at + 1, :] for at in range(4))
    hidden_turned, two_turned, pre_grad, attn_grad = (packs.at[:, at * dim : (at + 1) * dim] for at in range(4))
    pool = waves_last(pool_unit[...] * gains + shifts, features)
    pool_low[...] = pool.astype(BF)
    turn_pool(packs.at[:, 4 * dim :], pool)

    latent = latent.get()
    pad_rows(value, value_raw.get())
    wide = WIDE
    for start in range(0, dim, wide):
        span = slice(start, start + wide)
        attn = jnp.dot(pool_low[...], value[:, span], preferred_element_type=F32) + value_bias[:, span]
        mixed[:, span] = latent[:, span].astype(F32) + attn
    low = 32
    for start in range(0, count, low):
        span = slice(start, start + low)
        unit, spread = norm_stats(mixed[span, :], 1)
        mix_unit[span, :] = unit
        mix_spread[span, :] = jnp.broadcast_to(spread, (low, LANES))
        two[span, :] = (unit * gain + shift).astype(BF)
    turn_blocks(two_turned, two)
    for start in range(0, dim, wide):
        span = slice(start, start + wide)
        act = jnp.dot(two[...], up[:, span], preferred_element_type=F32) + up_bias[:, span]
        half = 0.5 * (1.0 + lax.erf(act * (1.0 / math.sqrt(2.0))))
        active = act * half
        hidden[:, span] = active.astype(BF)
        hidden_turned[:, span] = jnp.transpose(active).astype(BF)
        slope = half + act * jnp.exp(-0.5 * act * act) * (1.0 / math.sqrt(2.0 * math.pi))
        pre_grad[:, span] = (hidden_grad[:, span].astype(F32) * slope).astype(BF)
    for start in range(0, dim, wide):
        span = slice(start, start + wide)
        back[:, span] = contract(pre_grad[...], up[span, :], 1, 1)
    grad = grad.get()
    gain_sum = jnp.zeros((8, dim), F32)
    shift_sum = jnp.zeros((8, dim), F32)
    for start in range(0, count, low):
        span = slice(start, start + low)
        upstream = back[span, :]
        unit = mix_unit[span, :]
        full = grad[span, :].astype(F32) + norm_back(upstream, gain, unit, mix_spread[span, :1], 1)
        mixed_grad[span, :] = full
        attn_grad[span, :] = full.astype(BF)
        gain_sum = gain_sum + fold_rows(upstream * unit)
        shift_sum = shift_sum + fold_rows(upstream)
    sums[0:1, :] = jnp.sum(gain_sum, axis=0, keepdims=True)
    sums[1:2, :] = jnp.sum(shift_sum, axis=0, keepdims=True)
    lifted = waves_first(contract(attn_grad[...], value[...], 1, 1), features)
    lift_out[...] = lifted
    pulled = (lifted * gains).astype(BF)
    at = lane_ids(pulled.shape)
    inside = jnp.where(at < features, pulled.astype(F32) * pool_unit[...], 0.0)
    delta = jnp.sum(inside, axis=1, keepdims=True)
    for lane, part in enumerate(split(-delta)):
        pulled = jnp.where(at == features + lane, part, pulled)
    puller[...] = pulled
    at = lane_ids(stats.shape)
    stats[...] = jnp.where(at == 0, peak + jnp.log2(total), delta)


def write_vectors(array, lines, vectors):
    width = array.shape[0]
    lines[...] = jnp.zeros_like(lines)
    row = 0
    for vector in vectors:
        for part in split(vector):
            for start in range(0, vector.shape[1], width):
                lines[row : row + 1, :] = part[:, start : start + width].astype(F32)
                row += 1
    array[LANES : LANES + lines.shape[0], array.shape[1] - width :] = lines[...].astype(BF)


def read_vectors(array, dim, number):
    width = array.shape[0]
    turns = dim // width
    high = padded(3 * number * turns, 16)
    lines = array[LANES : LANES + high, array.shape[1] - width :].astype(F32)
    vectors = []
    for at in range(number):
        first = 3 * at * turns
        total = sum(lines[first + part * turns : first + (part + 1) * turns] for part in range(3))
        vectors.append(jnp.concatenate([total[turn : turn + 1] for turn in range(turns)], axis=1))
    return vectors


def pull_kernel(
    features,
    segments, kept_row, absorbed, lifted, puller, unit_in, spread_in, score, pool_unit, stats,
    key_raw, sums, ends, query_weight, latent, rows, mixed_grad,
    late, color_out, latent_out,
    pulls, pooled, key, color_grad, back, latent_grad, lines, out_sems,
):
    count, dim = pooled.shape[0], key.shape[1]
    own = segments.shape[2]
    tall, kept = unit_in.shape
    waves = 4 * BANDS
    def shares(lanes):
        inner = jnp.dot(puller[...], unit_in[:, lanes], preferred_element_type=F32)
        prob = jnp.exp2(score[:, lanes] - stats[:, :1])
        return inner, prob, (prob * inner).astype(BF)

    for start in range(0, kept, PULL):
        lanes = slice(start, start + PULL)
        pulls[:, lanes] = shares(lanes)[2]
    pooled[...] = contract(pulls[...], unit_in[...], 1, 1)
    gains, shifts = ends[0:1, :], ends[1:2, :]
    kept_row, key_raw, query_weight = kept_row.get(), key_raw.get(), query_weight.get()
    latent, absorbed = latent.get(), absorbed.get()

    mine = lax.axis_index("pix")
    offset = jnp.int32(0)
    for index, found in enumerate(segment_counts(segments, segments.shape[0])):
        offset = offset + jnp.where(index < mine, found, 0)
    inside = lax.rem(offset, LANES)
    base = pl.multiple_of(jnp.minimum(offset - inside, kept - own - LANES), LANES)
    inside = offset - base
    lanes = pl.ds(base, own + LANES)
    inner, prob, score_grad = shares(lanes)
    tilt = score_grad.astype(F32) * score[:, lanes] * math.log(2.0) + prob * (inner + stats[:, 1:2])
    tilt = jnp.sum(tilt, axis=0, keepdims=True) * (1.0 / features)
    factors = []
    for held in (absorbed, lifted):
        scaled = held[...] * gains
        at = lane_ids((count, LANES))
        corner = jnp.where(at == 3, jnp.sum(scaled, axis=1, keepdims=True), scaled[:, waves : waves + LANES])
        factors.append(jnp.transpose(corner)[:8].astype(BF))
    both = jnp.concatenate([score_grad, prob.astype(BF)], axis=0)
    terms = jnp.dot(jnp.concatenate(factors, axis=1), both, preferred_element_type=F32)
    unit = unit_in[waves : waves + 16, lanes].astype(F32)[:8]
    colors = spread_in[:, lanes] * (terms - terms[3:4] * (1.0 / features) - unit * tilt)
    window = pltpu.roll(colors, own + LANES - inside, 1)[:, :own]
    slots = jnp.where(slot_of(kept_row[...].astype(F32)), 1.0, 0.0)
    spread_back = jnp.dot(window, slots, precision=lax.Precision.HIGHEST, preferred_element_type=F32)
    color_grad[:, 0, :] = spread_back[:3]

    held = pooled[...]
    total = held[:, features : features + 1]
    pool = waves_last(held * gains + shifts * total, features)
    turn_pool(late.at[:, dim:], pool)
    pool = pool.astype(BF)
    pad_rows(key, key_raw)
    gain_sum = absorbed[...] * held + lifted[...] * pool_unit[...]
    shift_sum = absorbed[...] * total + lifted[...]
    vectors = []
    for found in (gain_sum, shift_sum):
        flat = jnp.sum(fold_rows(found), axis=0, keepdims=True)
        flat = waves_last(jnp.broadcast_to(flat, (8, tall)), features)[:1]
        vectors.append(jnp.concatenate([flat, jnp.zeros((1, dim - tall), F32)], axis=1))
    vectors += [sums[0:1, :], sums[1:2, :]]
    wide = WIDE
    for start in range(0, dim, wide):
        span = slice(start, start + wide)
        part = jnp.dot(pool, key[:, span], preferred_element_type=F32) * (1.0 / math.sqrt(dim))
        late[:, span] = part.astype(BF)
    for start in range(0, dim, wide):
        span = slice(start, start + wide)
        back[:, span] = contract(late[:, :dim], query_weight[span, :], 1, 1)
    low = 32
    gain = rows[5:6, :]
    gain_sum = jnp.zeros((8, dim), F32)
    shift_sum = jnp.zeros((8, dim), F32)
    for start in range(0, count, low):
        span = slice(start, start + low)
        unit, spread = norm_stats(latent[span, :].astype(F32), 1)
        upstream = back[span, :]
        latent_grad[span, :] = mixed_grad[span, :] + norm_back(upstream, gain, unit, spread, 1)
        gain_sum = gain_sum + fold_rows(upstream * unit)
        shift_sum = shift_sum + fold_rows(upstream)
    vectors += [jnp.sum(gain_sum, axis=0, keepdims=True), jnp.sum(shift_sum, axis=0, keepdims=True)]
    write_vectors(late, lines, vectors)
    leave = [
        pltpu.make_async_copy(color_grad, color_out, out_sems.at[0]),
        pltpu.make_async_copy(latent_grad, latent_out, out_sems.at[1]),
    ]
    for copy in leave:
        copy.start()
    for copy in leave:
        copy.wait()


class Leaving:
    def __init__(self, buffers, sems):
        self.buffers, self.sems, self.flying, self.turn = buffers, sems, {}, 0

    def free(self):
        slot = self.turn % self.buffers.shape[0]
        if slot in self.flying:
            self.flying[slot].wait()
        return self.buffers.at[slot]

    def send(self, target):
        slot = self.turn % self.buffers.shape[0]
        self.turn += 1
        self.flying[slot] = pltpu.make_async_copy(self.buffers.at[slot], target, self.sems.at[slot])
        self.flying[slot].start()

    def end(self):
        for copy in self.flying.values():
            copy.wait()


def parts_of(ref, dim):
    squares = ref.shape[1] // dim
    parts = [ref.at[:, at * dim : (at + 1) * dim] for at in range(squares)]
    return parts + ([ref.at[:, squares * dim :]] if ref.shape[1] % dim else [])


def products(leaving, left, left_far, right, right_far, target, bias):
    count = left.shape[0]
    size = leaving.buffers.shape[1]
    for start in range(0, left.shape[1], size):
        buffer = leaving.free()
        at, inner = start // count * count, start % count
        rows, lanes = slice(inner, inner + size), slice(at, at + count)
        strip = jnp.concatenate([left[rows, lanes], left_far[rows, lanes]], axis=1)
        if bias is not None and start == 0:
            strip = jnp.concatenate([strip, jnp.ones((16, 2 * count), BF)], axis=0)
        found = jnp.dot(strip, jnp.concatenate([right[...], right_far[...]], axis=0), preferred_element_type=F32)
        buffer[...] = found[:size]
        if bias is not None and start == 0:
            bias[...] = found[size]
        leaving.send(target.at[start : start + size, :])


def short_product(held, left, left_far, right, right_far, bias, scale):
    features, count = held.shape[0], left.shape[0]
    pieces = []
    for at, start in enumerate(range(0, features, count)):
        height = min(count, padded(features - start, 16))
        lanes = slice(at * count, (at + 1) * count)
        pieces.append(jnp.concatenate([left[:height, lanes], left_far[:height, lanes]], axis=1))
    high = sum(piece.shape[0] for piece in pieces)
    pieces.append(jnp.ones((16, 2 * count), BF))
    both = jnp.concatenate([right[...], right_far[...]], axis=0)
    found = jnp.dot(jnp.concatenate(pieces, axis=0), both, preferred_element_type=F32)
    held[...] = found[:features] if scale is None else found[:features] * scale
    if bias is not None:
        bias[...] = found[high]


def late_kernel(
    features,
    packs, packs_far, early, early_far,
    down_out, down_bias, up_out, up_bias, value_out, value_bias,
    buffers, held, sems, held_sem,
):
    dim = down_out.shape[1]
    hidden, two, pre, attn, pool = parts_of(packs, dim)
    hidden_far, two_far, pre_far, attn_far, pool_far = parts_of(packs_far, dim)
    grad, grad_far = parts_of(early, dim)[2], parts_of(early_far, dim)[2]
    leaving = Leaving(buffers, sems)
    products(leaving, hidden, hidden_far, grad, grad_far, down_out, down_bias)
    short_product(held, pool, pool_far, attn, attn_far, value_bias, None)
    leave = pltpu.make_async_copy(held, value_out, held_sem)
    leave.start()
    products(leaving, two, two_far, pre, pre_far, up_out, up_bias)
    leave.wait()
    leaving.end()


def last_kernel(
    features,
    early, early_far, late, late_far, hidden, mixed, down, rows, _,
    encoded_out, query_out, query_bias, key_out, lat_gain, lat_shift, mlp_gain, mlp_shift, in_gain, in_shift,
    buffers, held, encoded, sems, held_sem, encoded_sem,
):
    dim = query_out.shape[1]
    one, query, _ = parts_of(early, dim)
    one_far, query_far, _ = parts_of(early_far, dim)
    grad, pool = parts_of(late, dim)
    grad_far, pool_far = parts_of(late_far, dim)
    leaving = Leaving(buffers, sems)
    products(leaving, one, one_far, grad, grad_far, query_out, query_bias)
    short_product(held, pool, pool_far, query, query_far, None, 1.0 / math.sqrt(dim))
    short = pltpu.make_async_copy(held, key_out, held_sem)
    short.start()
    for start in range(0, dim, WIDE):
        span = slice(start, start + WIDE)
        part = jnp.dot(hidden[...], down[:, span], preferred_element_type=F32)
        encoded[:, span] = (mixed[:, span] + part + rows[4:5, span]).astype(BF)
    leave = pltpu.make_async_copy(encoded, encoded_out, encoded_sem)
    leave.start()
    pairs = zip(read_vectors(late, dim, 6), read_vectors(late_far, dim, 6))
    places = (in_gain, in_shift, mlp_gain, mlp_shift, lat_gain, lat_shift)
    for place, (own, far) in zip(places, pairs):
        place[...] = (own + far)[0, : place.shape[0]]
    leaving.end()
    short.wait()
    leave.wait()


def call(body, outs, args, fetched, scratch, vmem, flops, moved, unread=()):
    places = [at for at in range(len(args)) if at in fetched]
    buffers = [pltpu.VMEM(args[at].shape, args[at].dtype) for at in places]
    shapes = tuple(pltpu.HBM(shape, dtype) if place is HBM else out(shape, dtype) for shape, dtype, place in outs)

    def whole(*refs):
        sources, rest = list(refs[: len(args)]), refs[len(args) :]
        targets = ()
        if places:
            targets, sems, rest = rest[-len(buffers) - 1 : -1], rest[-1], rest[: -len(buffers) - 1]
        for slot, (at, target) in enumerate(zip(places, targets)):
            sources[at] = Fetch(sources[at], target, sems.at[slot])
            sources[at].start()
        body(*sources, *rest)
        for at in places:
            sources[at].get()

    return pl.pallas_call(
        whole,
        out_shape=shapes if len(shapes) > 1 else shapes[0],
        in_specs=tuple(HBM if at in fetched or at in unread else VM for at in range(len(args))),
        out_specs=tuple(place for _, _, place in outs) if len(outs) > 1 else outs[0][2],
        scratch_shapes=list(scratch) + buffers + ([pltpu.SemaphoreType.DMA((len(places),))] if places else []),
        compiler_params=pltpu.CompilerParams(vmem_limit_bytes=vmem * MIB),
        cost_estimate=pl.CostEstimate(flops=flops, bytes_accessed=moved, transcendentals=0),
    )(*(pltpu.with_memory_space_constraint(arg, pltpu.HBM) if at in fetched or at in unread else arg for at, arg in enumerate(args)))


def on_chip(
    latents, pixels, coords, kept_mask, lat_gain, lat_shift, query_weight, query_bias, in_gain, in_shift,
    key_weight, value_weight, value_bias, mlp_gain, mlp_shift, up_weight, up_bias, down_weight, down_bias,
    cotangent,
):
    pix = lax.axis_size("pix")
    own = pixels.shape[2]
    kept = pix * own // 2
    _, count, dim = latents.shape
    features = in_gain.shape[0]
    tall = padded(features, LANES)
    latent, out_grad = latents[0], cotangent[0]
    swap = [(0, 1), (1, 0)]

    def other(value):
        return lax.ppermute(value, "img", swap)

    packed = call(
        pack_kernel, [((pix, 8, own), BF, VM)], (pixels.transpose(1, 0, 2), coords[0], kept_mask), (0, 1, 2),
        [pltpu.VMEM((8, own), F32)], 8, 4 * 8 * own * own, 16 * 8 * own,
    )
    segments = lax.all_to_all(packed, "pix", 0, 0)

    table = jnp.asarray(lookup_with_sums(), BF)
    wide = pltpu.VMEM((tall, dim), BF)
    early, absorbed, scorer, hidden_grad, table_kept, rows, ends, up_kept = call(
        lambda *refs: query_kernel(features, *refs),
        [
            ((count, 3 * dim), BF, HBM), ((count, tall), F32, HBM), ((count, tall), BF, VM), ((count, dim), BF, VM),
            (table.shape, BF, VM), ((8, dim), F32, VM), ((8, tall), F32, VM), ((dim, dim), BF, VM),
        ],
        (
            latent, lat_gain, lat_shift, query_weight, query_bias, key_weight, in_gain, out_grad, down_weight,
            in_shift, value_bias, mlp_gain, mlp_shift, up_bias, down_bias, table, up_weight,
        ),
        tuple(range(16)),
        [
            pltpu.VMEM((count, dim), BF), wide, pltpu.VMEM((count, 3 * dim), BF), pltpu.VMEM((count, tall), F32),
            pltpu.SemaphoreType.DMA((4,)),
        ],
        16, 4 * count * dim * dim + 2 * count * dim * tall, 8 * MIB, (16,),
    )

    narrow = pltpu.VMEM((count, LANES), F32)
    area = pltpu.VMEM((count, dim), F32)
    low = pltpu.VMEM((count, dim), BF)
    spare = 512
    (
        hidden, mixed, packs, mixed_grad, lifted, puller, unit_in, spread_in, score, pool_unit, stats, sums,
    ) = call(
        lambda *refs: forward_kernel(features, *refs),
        [
            ((count, dim), BF, VM), ((count, dim), F32, VM), ((count, 4 * dim + spare), BF, VM),
            ((count, dim), F32, VM),
            ((count, tall), F32, VM), ((count, tall), BF, VM), ((tall, kept), BF, VM), ((8, kept), F32, VM),
            ((count, kept), F32, VM), ((count, tall), F32, VM), ((count, LANES), F32, VM), ((8, dim), F32, VM),
        ],
        (
            segments, scorer, hidden_grad, table_kept, latent, value_weight, up_kept, rows, ends, out_grad,
        ),
        (4, 5, 9),
        [
            pltpu.VMEM((8, kept + own + LANES), F32), pltpu.VMEM((GRID, LANES), BF), narrow,
            pltpu.VMEM((count, kept), BF), pltpu.VMEM((count, tall), F32), area, area, narrow, wide, low,
            pltpu.VMEM((count, tall), BF),
        ],
        20, 6 * count * dim * dim + 4 * count * dim * tall + 6 * kept * count * tall, 8 * MIB,
    )

    late, color_grad, latent_grad = call(
        lambda *refs: pull_kernel(features, *refs),
        [
            ((count, dim + spare), BF, VM), ((3, 1, own), F32, HBM), ((count, dim), F32, HBM),
        ],
        (
            segments, kept_mask, absorbed, lifted, puller, unit_in, spread_in, score, pool_unit, stats, key_weight,
            sums, ends, query_weight, latent, rows, mixed_grad,
        ),
        (1, 2, 10, 13, 14),
        [
            pltpu.VMEM((count, kept), BF), pltpu.VMEM((count, tall), F32), wide, pltpu.VMEM((3, 1, own), F32), area,
            area, pltpu.VMEM((80, count), F32), pltpu.SemaphoreType.DMA((2,)),
        ],
        16, 2 * count * dim * dim + 4 * kept * count * tall, 8 * MIB,
    )

    early_far = other(early)
    packs_far = other(packs)
    late_far = other(late)
    square = ((dim, dim), F32, HBM)
    slab = ((features, dim), F32, HBM)
    line = ((dim,), F32, VM)
    short = ((features,), F32, VM)
    slots = [
        pltpu.VMEM((4, STRIP, dim), F32), pltpu.VMEM((features, dim), F32),
    ]
    sems = [pltpu.SemaphoreType.DMA((4,)), pltpu.SemaphoreType.DMA(())]
    down_weight_grad, down_bias_grad, up_weight_grad, up_bias_grad, value_weight_grad, value_bias_grad = call(
        lambda *refs: late_kernel(features, *refs),
        [square, line, square, line, slab, line], (packs, packs_far, early, early_far), (),
        slots + sems, 12, 8 * count * dim * dim + 4 * count * dim * tall, 10 * MIB,
    )
    (
        encoded, query_weight_grad, query_bias_grad, key_weight_grad, lat_gain_grad, lat_shift_grad, mlp_gain_grad,
        mlp_shift_grad, in_gain_grad, in_shift_grad,
    ) = call(
        lambda *refs: last_kernel(features, *refs),
        [((count, dim), BF, HBM), square, line, slab, line, line, line, line, short, short],
        (
            early, early_far, late, late_far, hidden, mixed, down_weight, rows,
            down_weight_grad,
        ),
        (), slots + [low] + sems + [pltpu.SemaphoreType.DMA(())], 12, 4 * count * dim * dim + 4 * count * dim * tall, 6 * MIB, (8,),
    )

    return (
        encoded[None], latent_grad[None], color_grad.transpose(1, 0, 2), lat_gain_grad, lat_shift_grad,
        query_weight_grad, query_bias_grad, in_gain_grad, in_shift_grad, key_weight_grad, value_weight_grad,
        value_bias_grad, mlp_gain_grad, mlp_shift_grad, up_weight_grad, up_bias_grad, down_weight_grad, down_bias_grad,
    )


def in_blocks(
    latents,
    pixels,
    coords,
    kept_mask,
    lat_gain,
    lat_shift,
    query_weight,
    query_bias,
    in_gain,
    in_shift,
    key_weight,
    value_weight,
    value_bias,
    mlp_gain,
    mlp_shift,
    up_weight,
    up_bias,
    down_weight,
    down_bias,
    cotangent,
):
    pix = lax.axis_size("pix")
    mine = lax.axis_index("pix")
    own = pixels.shape[2]
    packed = jnp.concatenate(
        [
            pixels[0].astype(BF),
            coords[0].astype(BF),
            kept_mask.astype(BF),
            jnp.zeros((2, own), BF),
        ],
        axis=0,
    )
    gathered = lax.all_to_all(jnp.broadcast_to(packed[None], (pix,) + packed.shape), "pix", 0, 0)
    every = gathered.transpose(1, 0, 2).reshape(packed.shape[0], pix * own)
    swap = [(0, 1), (1, 0)]

    def other(value):
        return lax.ppermute(value, "img", swap)

    root = math.sqrt(latents.shape[2])
    latent = latents[0].astype(F32)
    lat_unit, lat_spread = norm_stats(latent, 1)
    norm_one = (lat_unit * lat_gain + lat_shift).astype(BF)
    query = (jnp.dot(norm_one, query_weight, preferred_element_type=F32) + query_bias).astype(BF)
    absorbed = (contract(query, key_weight, 1, 1) * (1.0 / root)).astype(BF)

    waves = jnp.asarray(fourier_lookup(), BF)
    places = jnp.arange(GRID, dtype=F32)[:, None]

    def features(part):
        cells = part[3:5].astype(F32)
        position = (cells * (2.0 / (GRID - 1)) - 1.0).astype(BF)
        row_waves = jnp.dot(waves, (cells[0:1] == places).astype(BF), preferred_element_type=F32).astype(BF)
        col_waves = jnp.dot(waves, (cells[1:2] == places).astype(BF), preferred_element_type=F32).astype(BF)
        table = jnp.concatenate(
            [part[0:3], position, row_waves[:BANDS], col_waves[:BANDS], row_waves[BANDS:], col_waves[BANDS:]],
            axis=0,
        ).astype(F32)
        unit, spread = norm_stats(table, 0)
        x_in = (unit * in_gain[:, None] + in_shift[:, None]).astype(BF)
        score = jnp.dot(absorbed, x_in, preferred_element_type=F32)
        return unit, spread, x_in, jnp.where(part[5:6] > 0, score, FLOOR), part[5:6] > 0

    def pool(part, feats):
        unit, spread, x_in, score, live = feats
        top = jnp.max(score, axis=1, keepdims=True)
        weight = jnp.where(live, jnp.exp(score - top), 0.0)
        return top, jnp.sum(weight, axis=1, keepdims=True), contract(weight.astype(BF), x_in, 1, 1)

    blocks = max(1, pix // BLOCK)
    parts = every.reshape(packed.shape[0], blocks, -1).transpose(1, 0, 2)
    if blocks == 1:
        feats = features(parts[0])
        row_top, row_total, pooled = pool(parts[0], feats)
    else:

        def merge(carry, part):
            top, total, sums = pool(part, features(part))
            new_top = jnp.maximum(carry[0], top)
            old_scale, new_scale = jnp.exp(carry[0] - new_top), jnp.exp(top - new_top)
            return (
                new_top,
                carry[1] * old_scale + total * new_scale,
                carry[2] * old_scale + sums * new_scale,
            ), None

        start = (
            jnp.full((latent.shape[0], 1), FLOOR, F32),
            jnp.zeros((latent.shape[0], 1), F32),
            jnp.zeros((latent.shape[0], in_gain.shape[0]), F32),
        )
        row_top, row_total, pooled = lax.scan(merge, start, parts)[0]
    pooled = pooled / row_total
    pooled_low = pooled.astype(BF)
    attn = jnp.dot(pooled_low, value_weight, preferred_element_type=F32) + value_bias
    mixed = latent + attn
    mix_unit, mix_spread = norm_stats(mixed, 1)
    norm_two = (mix_unit * mlp_gain + mlp_shift).astype(BF)
    pre_act = jnp.dot(norm_two, up_weight, preferred_element_type=F32) + up_bias
    half_erf = 0.5 * (1.0 + lax.erf(pre_act * (1.0 / math.sqrt(2.0))))
    hidden = (pre_act * half_erf).astype(BF)
    encoded = (
        mixed + jnp.dot(hidden, down_weight, preferred_element_type=F32) + down_bias
    ).astype(BF)

    out_grad = cotangent[0]
    out_grad_full = out_grad.astype(F32)
    hidden_grad = contract(out_grad, down_weight, 1, 1)
    slope = half_erf + pre_act * jnp.exp(-0.5 * pre_act * pre_act) * (1.0 / math.sqrt(2.0 * math.pi))
    pre_grad = (hidden_grad * slope).astype(BF)
    norm_two_grad = contract(pre_grad, up_weight, 1, 1)
    mixed_grad = out_grad_full + norm_back(norm_two_grad, mlp_gain, mix_unit, mix_spread, 1)
    attn_grad = mixed_grad.astype(BF)

    lifted = contract(attn_grad, value_weight, 1, 1).astype(BF)
    row_delta = jnp.sum(lifted.astype(F32) * pooled, axis=1, keepdims=True)

    def pull(part, feats):
        unit, spread, x_in, score, live = feats
        prob = jnp.where(live, jnp.exp(score - row_top), 0.0) / row_total
        score_grad = (prob * (jnp.dot(lifted, x_in, preferred_element_type=F32) - row_delta)).astype(BF)
        score_pool = contract(score_grad, x_in, 1, 1)
        x_in_grad = contract(absorbed, score_grad, 0, 0) + contract(lifted, prob.astype(BF), 0, 0)
        gain_part = jnp.sum(x_in_grad * unit, axis=1)
        shift_part = jnp.sum(x_in_grad, axis=1)
        colour_part = norm_back(x_in_grad, in_gain[:, None], unit, spread, 0)[:3]
        return score_pool, gain_part, shift_part, colour_part

    if blocks == 1:
        score_pool, in_gain_grad, in_shift_grad, all_colors = pull(parts[0], feats)
    else:

        def gather_up(carry, part):
            found = pull(part, features(part))
            return tuple(kept + new for kept, new in zip(carry, found[:3])), found[3]

        start = (
            jnp.zeros((latent.shape[0], in_gain.shape[0]), F32),
            jnp.zeros_like(in_gain),
            jnp.zeros_like(in_shift),
        )
        (score_pool, in_gain_grad, in_shift_grad), stacked = lax.scan(gather_up, start, parts)
        all_colors = stacked.transpose(1, 0, 2).reshape(3, -1)
    color_grad = lax.dynamic_slice(all_colors, (0, mine * own), (3, own))
    score_pool_low = score_pool.astype(BF)
    query_grad = (
        jnp.dot(score_pool_low, key_weight, preferred_element_type=F32) * (1.0 / root)
    ).astype(BF)
    norm_one_grad = contract(query_grad, query_weight, 1, 1)
    latent_grad = mixed_grad + norm_back(norm_one_grad, lat_gain, lat_unit, lat_spread, 1)

    def both(value):
        return jnp.concatenate([value, other(value)], axis=0)

    out_both = both(out_grad)
    hidden_both = both(hidden)
    two_both = both(norm_two)
    pre_both = both(pre_grad)
    attn_both = both(attn_grad)
    one_both = both(norm_one)
    query_both = both(query)
    query_grad_both = both(query_grad)
    pool_both = both(pooled_low)
    score_both = both(score_pool_low)
    wide = jnp.stack(
        [
            jnp.sum(norm_one_grad * lat_unit, axis=0),
            jnp.sum(norm_one_grad, axis=0),
            jnp.sum(norm_two_grad * mix_unit, axis=0),
            jnp.sum(norm_two_grad, axis=0),
        ]
    )
    narrow = jnp.stack([in_gain_grad, in_shift_grad])
    wide = wide + other(wide)
    narrow = narrow + other(narrow)
    return (
        encoded[None],
        latent_grad[None],
        color_grad[None],
        wide[0],
        wide[1],
        contract(one_both, query_grad_both, 0, 0),
        jnp.sum(query_grad_both.astype(F32), axis=0),
        narrow[0],
        narrow[1],
        contract(score_both, query_both, 0, 0) * (1.0 / root),
        contract(pool_both, attn_both, 0, 0),
        jnp.sum(attn_both.astype(F32), axis=0),
        wide[2],
        wide[3],
        contract(two_both, pre_both, 0, 0),
        jnp.sum(pre_both.astype(F32), axis=0),
        contract(hidden_both, out_both, 0, 0),
        jnp.sum(out_both.astype(F32), axis=0),
    )


def shards(*args):
    pixels = args[1]
    kept = lax.axis_size("pix") * pixels.shape[2] // 2
    fits = kept <= 4096 and kept % (3 * PULL) == 0 and pixels.shape[2] % LANES == 0
    return (on_chip if fits else in_blocks)(*args)


def solution(mesh):
    lat = P("img", None, None)
    whole = P()
    return jax.shard_map(
        shards,
        mesh=mesh,
        in_specs=(lat, P("img", None, "pix"), P("img", None, "pix"), P("img", "pix"))
        + (whole,) * 15
        + (lat,),
        out_specs=(lat, lat, P("img", None, "pix")) + (whole,) * 15,
        check_vma=False,
    )
```

```python
import math

import jax
import jax.numpy as jnp
import numpy as np
from jax import lax
from jax.experimental import pallas as pl
from jax.experimental.pallas import tpu as pltpu
from jax.sharding import PartitionSpec as P

BANDS = 64
GRID = 224
EPSILON = 1e-05
FLOOR = -1e30
BLOCK = 16
LANES = 128
BF = jnp.bfloat16
F32 = jnp.float32
VM = pl.BlockSpec(memory_space=pltpu.VMEM)
HBM = pl.BlockSpec(memory_space=pltpu.HBM)
MIB = 1 << 20
MAKE = 256
SCORE = 1024
POOL = 512
PULL = 1024
WIDE = 256
STRIP = 256


def fourier_lookup():
    position = np.arange(GRID, dtype=np.float32) * np.float32(2.0 / (GRID - 1)) - np.float32(1.0)
    frequency = np.float32(1.0) + np.arange(BANDS, dtype=np.float32) * np.float32(
        (GRID / 2.0 - 1.0) / (BANDS - 1)
    )
    phases = position[None, :] * (np.float32(math.pi) * frequency)[:, None]
    waves = np.concatenate([np.sin(phases.astype(np.float64)), np.cos(phases.astype(np.float64))])
    return waves.astype(np.float32)


def split_numpy(values):
    parts = []
    for _ in range(3):
        part = values.astype(BF).astype(np.float64)
        parts.append(part)
        values = values - part
    return parts


def lookup_with_sums():
    waves = fourier_lookup().astype(BF).astype(np.float64)
    sums = split_numpy(waves.sum(axis=0)) + split_numpy((waves * waves).sum(axis=0))
    table = np.zeros((2 * BANDS + 16, GRID))
    table[: 2 * BANDS] = waves
    table[2 * BANDS : 2 * BANDS + 6] = np.stack(sums)
    return table


def split(values):
    parts = []
    for _ in range(3):
        part = values.astype(BF)
        parts.append(part)
        values = values - part.astype(F32)
    return parts


def contract(left, right, left_dim, right_dim):
    return lax.dot_general(
        left, right, (((left_dim,), (right_dim,)), ((), ())), preferred_element_type=F32
    )


def norm_stats(values, axis):
    centre = values - jnp.mean(values, axis=axis, keepdims=True)
    spread = lax.rsqrt(jnp.mean(centre * centre, axis=axis, keepdims=True) + EPSILON)
    return centre * spread, spread


def norm_back(upstream, gain, unit, spread, axis):
    inner = upstream * gain
    return spread * (
        inner
        - jnp.mean(inner, axis=axis, keepdims=True)
        - unit * jnp.mean(inner * unit, axis=axis, keepdims=True)
    )


def out(shape, dtype):
    return jax.ShapeDtypeStruct(shape, dtype)


def padded(rows, step):
    return -(-rows // step) * step


def lane_ids(shape):
    return lax.broadcasted_iota(jnp.int32, shape, len(shape) - 1)


def waves_first(values, features):
    width = values.shape[1]
    lead = features - 4 * BANDS
    at = lane_ids(values.shape)
    waves = pltpu.roll(values, width - lead, 1)
    rest = pltpu.roll(values, 4 * BANDS, 1)
    return jnp.where(at < 4 * BANDS, waves, jnp.where(at < features, rest, 0.0))


def waves_last(values, features):
    width = values.shape[1]
    lead = features - 4 * BANDS
    at = lane_ids(values.shape)
    rest = pltpu.roll(values, width - 4 * BANDS, 1)
    waves = pltpu.roll(values, lead, 1)
    return jnp.where(at < lead, rest, jnp.where(at < features, waves, 0.0))


def fold(values):
    total = values[:, :LANES]
    for start in range(LANES, values.shape[1], LANES):
        total = total + values[:, start : start + LANES]
    return total


def fold_max(values):
    total = values[:, :LANES]
    for start in range(LANES, values.shape[1], LANES):
        total = jnp.maximum(total, values[:, start : start + LANES])
    return total


def fold_rows(values):
    total = values[:8]
    for start in range(8, values.shape[0], 8):
        total = total + values[start : start + 8]
    return total


def slot_of(kept_row):
    own = kept_row.shape[1]
    shape = (own, own)
    upper = lax.broadcasted_iota(jnp.int32, shape, 0) <= lax.broadcasted_iota(jnp.int32, shape, 1)
    tall = jnp.broadcast_to(kept_row, (8, own)).astype(BF)
    rank = jnp.dot(tall, jnp.where(upper, 1.0, 0.0).astype(BF), preferred_element_type=F32)[:1]
    slot = jnp.where(kept_row > 0, rank - 1.0, -1.0)
    return slot == lax.broadcasted_iota(jnp.int32, shape, 0).astype(F32)


class Fetch:
    def __init__(self, source, target, sem):
        self.copy = pltpu.make_async_copy(source, target, sem)
        self.target = target
        self.waiting = True

    def start(self):
        self.copy.start()

    def get(self):
        if self.waiting:
            self.copy.wait()
            self.waiting = False
        return self.target


def row_of(fetch):
    return fetch.get()[...].reshape(1, -1)


def pack_kernel(pixels, coords, kept, packed, rows):
    rows[...] = jnp.zeros_like(rows)
    rows[0:3, :] = pixels.get()[:, 0, :]
    rows[3:5, :] = coords.get()[...].astype(F32)
    kept_row = kept.get()[...].astype(F32)
    rows[5:6, :] = kept_row
    slots = jnp.where(slot_of(kept_row), 1.0, 0.0).astype(BF)
    squeezed = contract(rows[...].astype(BF), slots, 1, 1).astype(BF)
    packed[...] = jnp.broadcast_to(squeezed[None], packed.shape)


def pad_rows(target, source):
    rows = source.shape[0]
    whole = rows // LANES * LANES
    target[:whole, :] = source[:whole, :]
    target[whole:, :] = jnp.zeros_like(target[whole:, :])
    target[whole:rows, :] = source[whole:, :]


def turn_blocks(target, source):
    size = source.shape[0]
    for start in range(0, source.shape[1], size):
        span = slice(start, start + size)
        target[:, span] = jnp.transpose(source[:, span].astype(F32)).astype(BF)


def turn_pool(target, pool):
    count, tall = pool.shape
    turned = jnp.transpose(pool).astype(BF)
    target[...] = jnp.zeros_like(target)
    for at, start in enumerate(range(0, tall, count)):
        height = min(count, tall - start)
        target[:height, at * count : (at + 1) * count] = turned[start : start + height]


def query_kernel(
    features, latent, gain, shift, weight, bias, key_raw, in_gain, grad, down, in_shift,
    value_bias, mlp_gain, mlp_shift, up_bias, down_bias, table, up_hbm,
    early_out, absorbed_out, scorer, hidden_grad, table_kept, rows, ends, up,
    one, key, early, absorbed, sems,
):
    bring = [pltpu.make_async_copy(up_hbm, up, sems.at[0])]
    latent = latent.get()
    count, dim = latent.shape
    tall = absorbed.shape[1]
    turned, query = early.at[:, :dim], early.at[:, dim:]
    step = 32
    lat_gain, lat_shift = row_of(gain), row_of(shift)
    for start in range(0, count, step):
        unit, _ = norm_stats(latent[start : start + step, :].astype(F32), 1)
        one[start : start + step, :] = (unit * lat_gain + lat_shift).astype(BF)
    bias, weight = row_of(bias), weight.get()
    for copy in bring:
        copy.start()
    step = 256
    for start in range(0, dim, step):
        part = jnp.dot(one[...], weight[:, start : start + step], preferred_element_type=F32)
        query[:, start : start + step] = (part + bias[:, start : start + step]).astype(BF)
    turn_blocks(turned, one)
    pad_rows(key, key_raw.get())
    lifted = contract(query[...], key[...], 1, 1) * (1.0 / math.sqrt(dim))
    lifted = waves_first(lifted, features)
    absorbed[...] = lifted
    gains = gain_row(in_gain, tall, features)
    scorer[...] = (lifted * gains * math.log2(math.e)).astype(BF)
    ends[...] = jnp.zeros_like(ends)
    ends[0:1, :] = gains
    ends[1:2, :] = gain_row(in_shift, tall, features)
    grad = grad.get()
    leave = [
        pltpu.make_async_copy(early, early_out, sems.at[2]),
        pltpu.make_async_copy(absorbed, absorbed_out, sems.at[3]),
    ]
    for copy in leave:
        copy.start()
    table_kept[...] = table.get()[...]
    rows[...] = jnp.zeros_like(rows)
    for at, vector in enumerate((value_bias, mlp_gain, mlp_shift, up_bias, down_bias)):
        rows[at : at + 1, :] = row_of(vector)
    rows[5:6, :] = lat_gain
    down = down.get()
    for start in range(0, dim, step):
        part = contract(grad[...], down[start : start + step, :], 1, 1)
        hidden_grad[:, start : start + step] = part.astype(BF)
    for copy in bring + leave:
        copy.wait()


def gain_row(fetch, width, features):
    row = row_of(fetch)
    wide = jnp.concatenate([row, jnp.zeros((1, width - features), F32)], axis=1)
    return waves_first(jnp.broadcast_to(wide, (8, width)), features)[:1]


def segment_counts(segments, stop):
    return [jnp.sum(segments[index][5:6, :].astype(F32)).astype(jnp.int32) for index in range(stop)]


def forward_kernel(
    features,
    segments, scorer, hidden_grad, table, latent, value_raw, up, rows, ends, grad,
    hidden, mixed, packs, mixed_grad, lift_out, puller, unit_out, spread_out, score_out, pool_unit, stats, sums,
    placed, places, top, weight, pooled, back, mix_unit, mix_spread, value, two, pool_low,
):
    pix, _, own = segments.shape
    tall, kept = unit_out.shape
    waves = 4 * BANDS
    ones = slice(features, waves + 8)

    placed[...] = jnp.zeros_like(placed)
    offset = jnp.int32(0)
    for index, found in enumerate(segment_counts(segments, pix)):
        wide = jnp.concatenate([segments[index].astype(F32), jnp.zeros((8, LANES), F32)], axis=1)
        inside = lax.rem(offset, LANES)
        base = pl.multiple_of(jnp.minimum(offset - inside, kept), LANES)
        placed[:, pl.ds(base, own + LANES)] += pltpu.roll(wide, inside, 1)
        offset = offset + found
    places[...] = lax.broadcasted_iota(jnp.int32, places.shape, 0).astype(F32).astype(BF)
    unit_out[waves + 16 :, :] = jnp.zeros((tall - waves - 16, kept), BF)
    top[...] = jnp.full_like(top, FLOOR)

    for start in range(0, kept, MAKE):
        step = MAKE
        lanes = slice(start, start + step)
        raw = placed[:, lanes]
        column = jnp.concatenate([places[...]] * (step // LANES), axis=1)
        one, none = jnp.ones((), BF), jnp.zeros((), BF)
        row_hot = jnp.where(column == raw[3:4].astype(BF), one, none)
        col_hot = jnp.where(column == raw[4:5].astype(BF), one, none)
        row_waves = jnp.dot(table[...], row_hot, preferred_element_type=F32)
        col_waves = jnp.dot(table[...], col_hot, preferred_element_type=F32)
        at = lax.broadcasted_iota(jnp.int32, raw.shape, 0)
        position = (raw * (2.0 / (GRID - 1)) - 1.0).astype(BF).astype(F32)
        extra = jnp.where(at < 3, raw, jnp.where(at < 5, position, 0.0))
        both = row_waves[2 * BANDS :] + col_waves[2 * BANDS :]
        mean = (
            jnp.sum(both[0:3], axis=0, keepdims=True) + jnp.sum(extra, axis=0, keepdims=True)
        ) * (1.0 / features)
        square = (
            jnp.sum(both[3:6], axis=0, keepdims=True) + jnp.sum(extra * extra, axis=0, keepdims=True)
        ) * (1.0 / features)
        spread = lax.rsqrt(jnp.maximum(square - mean * mean, 0.0) + EPSILON)
        centre = mean * spread
        spread_out[:, lanes] = jnp.broadcast_to(spread, (8, step))
        for piece, low in (
            (row_waves[:BANDS], 0),
            (col_waves[:BANDS], BANDS),
            (row_waves[BANDS : 2 * BANDS], 2 * BANDS),
            (col_waves[BANDS : 2 * BANDS], 3 * BANDS),
        ):
            unit_out[low : low + BANDS, lanes] = (piece * spread - centre).astype(BF)
        tail = jnp.where(at < features - waves, extra * spread - centre, 1.0)
        tail = jnp.concatenate([tail, jnp.zeros((8, step), F32)], axis=0)
        unit_out[waves : waves + 16, lanes] = tail.astype(BF)
    for start in range(0, kept, SCORE):
        lanes = slice(start, start + SCORE)
        score = jnp.dot(scorer[...], unit_out[:, lanes], preferred_element_type=F32)
        score_out[:, lanes] = score
        top[...] = jnp.maximum(top[...], fold_max(score))
    peak = jnp.max(top[...], axis=1, keepdims=True)
    top[...] = jnp.broadcast_to(peak, top.shape)
    for start in range(0, kept, POOL):
        lanes = slice(start, start + POOL)
        weight[:, lanes] = jnp.exp2(score_out[:, lanes] - top[:, :1]).astype(BF)
    pooled[...] = contract(weight[...], unit_out[...], 1, 1)
    total = pooled[:, features : features + 1]
    pool_unit[...] = pooled[...] * (1.0 / total)
    gains, shifts = ends[0:1, :], ends[1:2, :]
    count, dim = mixed.shape
    value_bias, gain, shift, up_bias = (rows[at : at + 1, :] for at in range(4))
    hidden_turned, two_turned, pre_grad, attn_grad, kept_grad = (
        packs.at[:, at * dim : (at + 1) * dim] for at in range(5)
    )
    pool = waves_last(pool_unit[...] * gains + shifts, features)
    pool_low[...] = pool.astype(BF)
    turn_pool(packs.at[:, 5 * dim :], pool)

    latent = latent.get()
    pad_rows(value, value_raw.get())
    wide = WIDE
    for start in range(0, dim, wide):
        span = slice(start, start + wide)
        attn = jnp.dot(pool_low[...], value[:, span], preferred_element_type=F32) + value_bias[:, span]
        mixed[:, span] = latent[:, span].astype(F32) + attn
    low = 32
    for start in range(0, count, low):
        span = slice(start, start + low)
        unit, spread = norm_stats(mixed[span, :], 1)
        mix_unit[span, :] = unit
        mix_spread[span, :] = jnp.broadcast_to(spread, (low, LANES))
        two[span, :] = (unit * gain + shift).astype(BF)
    turn_blocks(two_turned, two)
    for start in range(0, dim, wide):
        span = slice(start, start + wide)
        act = jnp.dot(two[...], up[:, span], preferred_element_type=F32) + up_bias[:, span]
        half = 0.5 * (1.0 + lax.erf(act * (1.0 / math.sqrt(2.0))))
        active = act * half
        hidden[:, span] = active.astype(BF)
        hidden_turned[:, span] = jnp.transpose(active).astype(BF)
        slope = half + act * jnp.exp(-0.5 * act * act) * (1.0 / math.sqrt(2.0 * math.pi))
        pre_grad[:, span] = (hidden_grad[:, span].astype(F32) * slope).astype(BF)
    for start in range(0, dim, wide):
        span = slice(start, start + wide)
        back[:, span] = contract(pre_grad[...], up[span, :], 1, 1)
    grad = grad.get()
    kept_grad[...] = grad[...]
    gain_sum = jnp.zeros((8, dim), F32)
    shift_sum = jnp.zeros((8, dim), F32)
    for start in range(0, count, low):
        span = slice(start, start + low)
        upstream = back[span, :]
        unit = mix_unit[span, :]
        full = grad[span, :].astype(F32) + norm_back(upstream, gain, unit, mix_spread[span, :1], 1)
        mixed_grad[span, :] = full
        attn_grad[span, :] = full.astype(BF)
        gain_sum = gain_sum + fold_rows(upstream * unit)
        shift_sum = shift_sum + fold_rows(upstream)
    sums[0:1, :] = jnp.sum(gain_sum, axis=0, keepdims=True)
    sums[1:2, :] = jnp.sum(shift_sum, axis=0, keepdims=True)
    lifted = waves_first(contract(attn_grad[...], value[...], 1, 1), features)
    lift_out[...] = lifted
    pulled = (lifted * gains).astype(BF)
    at = lane_ids(pulled.shape)
    inside = jnp.where(at < features, pulled.astype(F32) * pool_unit[...], 0.0)
    delta = jnp.sum(inside, axis=1, keepdims=True)
    for lane, part in enumerate(split(-delta)):
        pulled = jnp.where(at == features + lane, part, pulled)
    puller[...] = pulled
    at = lane_ids(stats.shape)
    stats[...] = jnp.where(at == 0, peak + jnp.log2(total), delta)


def write_vectors(array, lines, vectors):
    width = array.shape[0]
    lines[...] = jnp.zeros_like(lines)
    row = 0
    for vector in vectors:
        for part in split(vector):
            for start in range(0, vector.shape[1], width):
                lines[row : row + 1, :] = part[:, start : start + width].astype(F32)
                row += 1
    array[LANES : LANES + lines.shape[0], array.shape[1] - width :] = lines[...].astype(BF)


def read_vectors(array, dim, number):
    width = array.shape[0]
    turns = dim // width
    high = padded(3 * number * turns, 16)
    lines = array[LANES : LANES + high, array.shape[1] - width :].astype(F32)
    vectors = []
    for at in range(number):
        first = 3 * at * turns
        total = sum(lines[first + part * turns : first + (part + 1) * turns] for part in range(3))
        vectors.append(jnp.concatenate([total[turn : turn + 1] for turn in range(turns)], axis=1))
    return vectors


def pull_kernel(
    features,
    segments, kept_row, absorbed, lifted, puller, unit_in, spread_in, score, pool_unit, stats,
    key_raw, sums, ends, query_weight, latent, rows, mixed_grad,
    late, color_grad, latent_grad,
    pulls, pooled, key, back, lines,
):
    count, dim = pooled.shape[0], key.shape[1]
    own = segments.shape[2]
    tall, kept = unit_in.shape
    waves = 4 * BANDS
    def shares(lanes):
        inner = jnp.dot(puller[...], unit_in[:, lanes], preferred_element_type=F32)
        prob = jnp.exp2(score[:, lanes] - stats[:, :1])
        return inner, prob, (prob * inner).astype(BF)

    for start in range(0, kept, PULL):
        lanes = slice(start, start + PULL)
        pulls[:, lanes] = shares(lanes)[2]
    pooled[...] = contract(pulls[...], unit_in[...], 1, 1)
    gains, shifts = ends[0:1, :], ends[1:2, :]
    kept_row, key_raw, query_weight = kept_row.get(), key_raw.get(), query_weight.get()
    latent, absorbed = latent.get(), absorbed.get()

    mine = lax.axis_index("pix")
    offset = jnp.int32(0)
    for index, found in enumerate(segment_counts(segments, segments.shape[0])):
        offset = offset + jnp.where(index < mine, found, 0)
    inside = lax.rem(offset, LANES)
    base = pl.multiple_of(jnp.minimum(offset - inside, kept - own - LANES), LANES)
    inside = offset - base
    lanes = pl.ds(base, own + LANES)
    inner, prob, score_grad = shares(lanes)
    tilt = score_grad.astype(F32) * score[:, lanes] * math.log(2.0) + prob * (inner + stats[:, 1:2])
    tilt = jnp.sum(tilt, axis=0, keepdims=True) * (1.0 / features)
    factors = []
    for held in (absorbed, lifted):
        scaled = held[...] * gains
        at = lane_ids((count, LANES))
        corner = jnp.where(at == 3, jnp.sum(scaled, axis=1, keepdims=True), scaled[:, waves : waves + LANES])
        factors.append(jnp.transpose(corner)[:8].astype(BF))
    both = jnp.concatenate([score_grad, prob.astype(BF)], axis=0)
    terms = jnp.dot(jnp.concatenate(factors, axis=1), both, preferred_element_type=F32)
    unit = unit_in[waves : waves + 16, lanes].astype(F32)[:8]
    colors = spread_in[:, lanes] * (terms - terms[3:4] * (1.0 / features) - unit * tilt)
    window = pltpu.roll(colors, own + LANES - inside, 1)[:, :own]
    slots = jnp.where(slot_of(kept_row[...].astype(F32)), 1.0, 0.0)
    spread_back = jnp.dot(window, slots, precision=lax.Precision.HIGHEST, preferred_element_type=F32)
    color_grad[:, 0, :] = spread_back[:3]

    held = pooled[...]
    total = held[:, features : features + 1]
    pool = waves_last(held * gains + shifts * total, features)
    turn_pool(late.at[:, dim:], pool)
    pool = pool.astype(BF)
    pad_rows(key, key_raw)
    gain_sum = absorbed[...] * held + lifted[...] * pool_unit[...]
    shift_sum = absorbed[...] * total + lifted[...]
    vectors = []
    for found in (gain_sum, shift_sum):
        flat = jnp.sum(fold_rows(found), axis=0, keepdims=True)
        flat = waves_last(jnp.broadcast_to(flat, (8, tall)), features)[:1]
        vectors.append(jnp.concatenate([flat, jnp.zeros((1, dim - tall), F32)], axis=1))
    vectors += [sums[0:1, :], sums[1:2, :]]
    wide = WIDE
    for start in range(0, dim, wide):
        span = slice(start, start + wide)
        part = jnp.dot(pool, key[:, span], preferred_element_type=F32) * (1.0 / math.sqrt(dim))
        late[:, span] = part.astype(BF)
    for start in range(0, dim, wide):
        span = slice(start, start + wide)
        back[:, span] = contract(late[:, :dim], query_weight[span, :], 1, 1)
    low = 32
    gain = rows[5:6, :]
    gain_sum = jnp.zeros((8, dim), F32)
    shift_sum = jnp.zeros((8, dim), F32)
    for start in range(0, count, low):
        span = slice(start, start + low)
        unit, spread = norm_stats(latent[span, :].astype(F32), 1)
        upstream = back[span, :]
        latent_grad[span, :] = mixed_grad[span, :] + norm_back(upstream, gain, unit, spread, 1)
        gain_sum = gain_sum + fold_rows(upstream * unit)
        shift_sum = shift_sum + fold_rows(upstream)
    vectors += [jnp.sum(gain_sum, axis=0, keepdims=True), jnp.sum(shift_sum, axis=0, keepdims=True)]
    write_vectors(late, lines, vectors)


class Leaving:
    def __init__(self, buffers, sems):
        self.buffers, self.sems, self.flying, self.turn = buffers, sems, {}, 0

    def free(self):
        slot = self.turn % self.buffers.shape[0]
        if slot in self.flying:
            self.flying[slot].wait()
        return self.buffers.at[slot]

    def send(self, target):
        slot = self.turn % self.buffers.shape[0]
        self.turn += 1
        self.flying[slot] = pltpu.make_async_copy(self.buffers.at[slot], target, self.sems.at[slot])
        self.flying[slot].start()

    def end(self):
        for copy in self.flying.values():
            copy.wait()


def parts_of(ref, dim):
    squares = ref.shape[1] // dim
    parts = [ref.at[:, at * dim : (at + 1) * dim] for at in range(squares)]
    return parts + ([ref.at[:, squares * dim :]] if ref.shape[1] % dim else [])


def products(leaving, left, left_far, right, right_far, target, bias):
    count = left.shape[0]
    size = leaving.buffers.shape[1]
    for start in range(0, left.shape[1], size):
        buffer = leaving.free()
        at, inner = start // count * count, start % count
        rows, lanes = slice(inner, inner + size), slice(at, at + count)
        strip = jnp.concatenate([left[rows, lanes], left_far[rows, lanes]], axis=1)
        if bias is not None and start == 0:
            strip = jnp.concatenate([strip, jnp.ones((16, 2 * count), BF)], axis=0)
        found = jnp.dot(strip, jnp.concatenate([right[...], right_far[...]], axis=0), preferred_element_type=F32)
        buffer[...] = found[:size]
        if bias is not None and start == 0:
            bias[...] = found[size]
        leaving.send(target.at[start : start + size, :])


def short_product(held, left, left_far, right, right_far, bias, scale):
    features, count = held.shape[0], left.shape[0]
    pieces = []
    for at, start in enumerate(range(0, features, count)):
        height = min(count, padded(features - start, 16))
        lanes = slice(at * count, (at + 1) * count)
        pieces.append(jnp.concatenate([left[:height, lanes], left_far[:height, lanes]], axis=1))
    high = sum(piece.shape[0] for piece in pieces)
    pieces.append(jnp.ones((16, 2 * count), BF))
    both = jnp.concatenate([right[...], right_far[...]], axis=0)
    found = jnp.dot(jnp.concatenate(pieces, axis=0), both, preferred_element_type=F32)
    held[...] = found[:features] if scale is None else found[:features] * scale
    if bias is not None:
        bias[...] = found[high]


def late_kernel(
    features,
    packs, packs_far, color_grad, latent_grad,
    color_out, latent_out, down_out, down_bias, up_out, up_bias, value_out, value_bias,
    buffers, held, sems, held_sem, out_sems,
):
    dim = down_out.shape[1]
    hidden, two, pre, attn, grad, pool = parts_of(packs, dim)
    hidden_far, two_far, pre_far, attn_far, grad_far, pool_far = parts_of(packs_far, dim)
    first = [
        pltpu.make_async_copy(latent_grad, latent_out, out_sems.at[0]),
        pltpu.make_async_copy(color_grad, color_out, out_sems.at[1]),
    ]
    for copy in first:
        copy.start()
    leaving = Leaving(buffers, sems)
    products(leaving, hidden, hidden_far, grad, grad_far, down_out, down_bias)
    short_product(held, pool, pool_far, attn, attn_far, value_bias, None)
    leave = pltpu.make_async_copy(held, value_out, held_sem)
    leave.start()
    products(leaving, two, two_far, pre, pre_far, up_out, up_bias)
    for copy in first:
        copy.wait()
    leave.wait()
    leaving.end()


def last_kernel(
    features,
    early, early_far, late, late_far, hidden, mixed, down, rows, _,
    encoded_out, query_out, query_bias, key_out, lat_gain, lat_shift, mlp_gain, mlp_shift, in_gain, in_shift,
    buffers, held, encoded, sems, held_sem, encoded_sem,
):
    dim = query_out.shape[1]
    one, query = parts_of(early, dim)
    one_far, query_far = parts_of(early_far, dim)
    grad, pool = parts_of(late, dim)
    grad_far, pool_far = parts_of(late_far, dim)
    leaving = Leaving(buffers, sems)
    products(leaving, one, one_far, grad, grad_far, query_out, query_bias)
    short_product(held, pool, pool_far, query, query_far, None, 1.0 / math.sqrt(dim))
    short = pltpu.make_async_copy(held, key_out, held_sem)
    short.start()
    for start in range(0, dim, WIDE):
        span = slice(start, start + WIDE)
        part = jnp.dot(hidden[...], down[:, span], preferred_element_type=F32)
        encoded[:, span] = (mixed[:, span] + part + rows[4:5, span]).astype(BF)
    leave = pltpu.make_async_copy(encoded, encoded_out, encoded_sem)
    leave.start()
    pairs = zip(read_vectors(late, dim, 6), read_vectors(late_far, dim, 6))
    places = (in_gain, in_shift, mlp_gain, mlp_shift, lat_gain, lat_shift)
    for place, (own, far) in zip(places, pairs):
        place[...] = (own + far)[0, : place.shape[0]]
    leaving.end()
    short.wait()
    leave.wait()


def call(body, outs, args, fetched, scratch, vmem, flops, moved, unread=()):
    places = [at for at in range(len(args)) if at in fetched]
    buffers = [pltpu.VMEM(args[at].shape, args[at].dtype) for at in places]
    shapes = tuple(pltpu.HBM(shape, dtype) if place is HBM else out(shape, dtype) for shape, dtype, place in outs)

    def whole(*refs):
        sources, rest = list(refs[: len(args)]), refs[len(args) :]
        targets = ()
        if places:
            targets, sems, rest = rest[-len(buffers) - 1 : -1], rest[-1], rest[: -len(buffers) - 1]
        for slot, (at, target) in enumerate(zip(places, targets)):
            sources[at] = Fetch(sources[at], target, sems.at[slot])
            sources[at].start()
        body(*sources, *rest)
        for at in places:
            sources[at].get()

    return pl.pallas_call(
        whole,
        out_shape=shapes if len(shapes) > 1 else shapes[0],
        in_specs=tuple(HBM if at in fetched or at in unread else VM for at in range(len(args))),
        out_specs=tuple(place for _, _, place in outs) if len(outs) > 1 else outs[0][2],
        scratch_shapes=list(scratch) + buffers + ([pltpu.SemaphoreType.DMA((len(places),))] if places else []),
        compiler_params=pltpu.CompilerParams(vmem_limit_bytes=vmem * MIB),
        cost_estimate=pl.CostEstimate(flops=flops, bytes_accessed=moved, transcendentals=0),
    )(*(pltpu.with_memory_space_constraint(arg, pltpu.HBM) if at in fetched or at in unread else arg for at, arg in enumerate(args)))


def on_chip(
    latents, pixels, coords, kept_mask, lat_gain, lat_shift, query_weight, query_bias, in_gain, in_shift,
    key_weight, value_weight, value_bias, mlp_gain, mlp_shift, up_weight, up_bias, down_weight, down_bias,
    cotangent,
):
    pix = lax.axis_size("pix")
    own = pixels.shape[2]
    kept = pix * own // 2
    _, count, dim = latents.shape
    features = in_gain.shape[0]
    tall = padded(features, LANES)
    latent, out_grad = latents[0], cotangent[0]
    swap = [(0, 1), (1, 0)]

    def other(value):
        return lax.ppermute(value, "img", swap)

    packed = call(
        pack_kernel, [((pix, 8, own), BF, VM)], (pixels.transpose(1, 0, 2), coords[0], kept_mask), (0, 1, 2),
        [pltpu.VMEM((8, own), F32)], 8, 4 * 8 * own * own, 16 * 8 * own,
    )
    segments = lax.all_to_all(packed, "pix", 0, 0)

    table = jnp.asarray(lookup_with_sums(), BF)
    wide = pltpu.VMEM((tall, dim), BF)
    early, absorbed, scorer, hidden_grad, table_kept, rows, ends, up_kept = call(
        lambda *refs: query_kernel(features, *refs),
        [
            ((count, 2 * dim), BF, HBM), ((count, tall), F32, HBM), ((count, tall), BF, VM), ((count, dim), BF, VM),
            (table.shape, BF, VM), ((8, dim), F32, VM), ((8, tall), F32, VM), ((dim, dim), BF, VM),
        ],
        (
            latent, lat_gain, lat_shift, query_weight, query_bias, key_weight, in_gain, out_grad, down_weight,
            in_shift, value_bias, mlp_gain, mlp_shift, up_bias, down_bias, table, up_weight,
        ),
        tuple(range(16)),
        [
            pltpu.VMEM((count, dim), BF), wide, pltpu.VMEM((count, 2 * dim), BF), pltpu.VMEM((count, tall), F32),
            pltpu.SemaphoreType.DMA((4,)),
        ],
        16, 4 * count * dim * dim + 2 * count * dim * tall, 8 * MIB, (16,),
    )

    narrow = pltpu.VMEM((count, LANES), F32)
    area = pltpu.VMEM((count, dim), F32)
    low = pltpu.VMEM((count, dim), BF)
    spare = 512
    (
        hidden, mixed, packs, mixed_grad, lifted, puller, unit_in, spread_in, score, pool_unit, stats, sums,
    ) = call(
        lambda *refs: forward_kernel(features, *refs),
        [
            ((count, dim), BF, VM), ((count, dim), F32, VM), ((count, 5 * dim + spare), BF, VM),
            ((count, dim), F32, VM),
            ((count, tall), F32, VM), ((count, tall), BF, VM), ((tall, kept), BF, VM), ((8, kept), F32, VM),
            ((count, kept), F32, VM), ((count, tall), F32, VM), ((count, LANES), F32, VM), ((8, dim), F32, VM),
        ],
        (
            segments, scorer, hidden_grad, table_kept, latent, value_weight, up_kept, rows, ends, out_grad,
        ),
        (4, 5, 9),
        [
            pltpu.VMEM((8, kept + own + LANES), F32), pltpu.VMEM((GRID, LANES), BF), narrow,
            pltpu.VMEM((count, kept), BF), pltpu.VMEM((count, tall), F32), area, area, narrow, wide, low,
            pltpu.VMEM((count, tall), BF),
        ],
        20, 6 * count * dim * dim + 4 * count * dim * tall + 6 * kept * count * tall, 8 * MIB,
    )

    late, color_grad, latent_grad = call(
        lambda *refs: pull_kernel(features, *refs),
        [
            ((count, dim + spare), BF, VM), ((3, 1, own), F32, VM), ((count, dim), F32, VM),
        ],
        (
            segments, kept_mask, absorbed, lifted, puller, unit_in, spread_in, score, pool_unit, stats, key_weight,
            sums, ends, query_weight, latent, rows, mixed_grad,
        ),
        (1, 2, 10, 13, 14),
        [
            pltpu.VMEM((count, kept), BF), pltpu.VMEM((count, tall), F32), wide, area, pltpu.VMEM((80, count), F32),
        ],
        16, 2 * count * dim * dim + 4 * kept * count * tall, 8 * MIB,
    )

    packs_far = other(packs)
    early, late = lax.optimization_barrier((early, late))
    early_far = other(early)
    late_far = other(late)
    square = ((dim, dim), F32, HBM)
    slab = ((features, dim), F32, HBM)
    line = ((dim,), F32, VM)
    short = ((features,), F32, VM)
    slots = [
        pltpu.VMEM((4, STRIP, dim), F32), pltpu.VMEM((features, dim), F32),
    ]
    sems = [pltpu.SemaphoreType.DMA((4,)), pltpu.SemaphoreType.DMA(())]
    (
        color_grad, latent_grad, down_weight_grad, down_bias_grad, up_weight_grad, up_bias_grad, value_weight_grad,
        value_bias_grad,
    ) = call(
        lambda *refs: late_kernel(features, *refs),
        [((3, 1, own), F32, HBM), ((count, dim), F32, HBM), square, line, square, line, slab, line],
        (packs, packs_far, color_grad, latent_grad), (),
        slots + sems + [pltpu.SemaphoreType.DMA((2,))], 12, 8 * count * dim * dim + 4 * count * dim * tall, 10 * MIB,
    )
    (
        encoded, query_weight_grad, query_bias_grad, key_weight_grad, lat_gain_grad, lat_shift_grad, mlp_gain_grad,
        mlp_shift_grad, in_gain_grad, in_shift_grad,
    ) = call(
        lambda *refs: last_kernel(features, *refs),
        [((count, dim), BF, HBM), square, line, slab, line, line, line, line, short, short],
        (
            early, early_far, late, late_far, hidden, mixed, down_weight, rows,
            down_weight_grad,
        ),
        (), slots + [low] + sems + [pltpu.SemaphoreType.DMA(())], 12, 4 * count * dim * dim + 4 * count * dim * tall, 6 * MIB, (8,),
    )

    return (
        encoded[None], latent_grad[None], color_grad.transpose(1, 0, 2), lat_gain_grad, lat_shift_grad,
        query_weight_grad, query_bias_grad, in_gain_grad, in_shift_grad, key_weight_grad, value_weight_grad,
        value_bias_grad, mlp_gain_grad, mlp_shift_grad, up_weight_grad, up_bias_grad, down_weight_grad, down_bias_grad,
    )


def in_blocks(
    latents,
    pixels,
    coords,
    kept_mask,
    lat_gain,
    lat_shift,
    query_weight,
    query_bias,
    in_gain,
    in_shift,
    key_weight,
    value_weight,
    value_bias,
    mlp_gain,
    mlp_shift,
    up_weight,
    up_bias,
    down_weight,
    down_bias,
    cotangent,
):
    pix = lax.axis_size("pix")
    mine = lax.axis_index("pix")
    own = pixels.shape[2]
    packed = jnp.concatenate(
        [
            pixels[0].astype(BF),
            coords[0].astype(BF),
            kept_mask.astype(BF),
            jnp.zeros((2, own), BF),
        ],
        axis=0,
    )
    gathered = lax.all_to_all(jnp.broadcast_to(packed[None], (pix,) + packed.shape), "pix", 0, 0)
    every = gathered.transpose(1, 0, 2).reshape(packed.shape[0], pix * own)
    swap = [(0, 1), (1, 0)]

    def other(value):
        return lax.ppermute(value, "img", swap)

    root = math.sqrt(latents.shape[2])
    latent = latents[0].astype(F32)
    lat_unit, lat_spread = norm_stats(latent, 1)
    norm_one = (lat_unit * lat_gain + lat_shift).astype(BF)
    query = (jnp.dot(norm_one, query_weight, preferred_element_type=F32) + query_bias).astype(BF)
    absorbed = (contract(query, key_weight, 1, 1) * (1.0 / root)).astype(BF)

    waves = jnp.asarray(fourier_lookup(), BF)
    places = jnp.arange(GRID, dtype=F32)[:, None]

    def features(part):
        cells = part[3:5].astype(F32)
        position = (cells * (2.0 / (GRID - 1)) - 1.0).astype(BF)
        row_waves = jnp.dot(waves, (cells[0:1] == places).astype(BF), preferred_element_type=F32).astype(BF)
        col_waves = jnp.dot(waves, (cells[1:2] == places).astype(BF), preferred_element_type=F32).astype(BF)
        table = jnp.concatenate(
            [part[0:3], position, row_waves[:BANDS], col_waves[:BANDS], row_waves[BANDS:], col_waves[BANDS:]],
            axis=0,
        ).astype(F32)
        unit, spread = norm_stats(table, 0)
        x_in = (unit * in_gain[:, None] + in_shift[:, None]).astype(BF)
        score = jnp.dot(absorbed, x_in, preferred_element_type=F32)
        return unit, spread, x_in, jnp.where(part[5:6] > 0, score, FLOOR), part[5:6] > 0

    def pool(part, feats):
        unit, spread, x_in, score, live = feats
        top = jnp.max(score, axis=1, keepdims=True)
        weight = jnp.where(live, jnp.exp(score - top), 0.0)
        return top, jnp.sum(weight, axis=1, keepdims=True), contract(weight.astype(BF), x_in, 1, 1)

    blocks = max(1, pix // BLOCK)
    parts = every.reshape(packed.shape[0], blocks, -1).transpose(1, 0, 2)
    if blocks == 1:
        feats = features(parts[0])
        row_top, row_total, pooled = pool(parts[0], feats)
    else:

        def merge(carry, part):
            top, total, sums = pool(part, features(part))
            new_top = jnp.maximum(carry[0], top)
            old_scale, new_scale = jnp.exp(carry[0] - new_top), jnp.exp(top - new_top)
            return (
                new_top,
                carry[1] * old_scale + total * new_scale,
                carry[2] * old_scale + sums * new_scale,
            ), None

        start = (
            jnp.full((latent.shape[0], 1), FLOOR, F32),
            jnp.zeros((latent.shape[0], 1), F32),
            jnp.zeros((latent.shape[0], in_gain.shape[0]), F32),
        )
        row_top, row_total, pooled = lax.scan(merge, start, parts)[0]
    pooled = pooled / row_total
    pooled_low = pooled.astype(BF)
    attn = jnp.dot(pooled_low, value_weight, preferred_element_type=F32) + value_bias
    mixed = latent + attn
    mix_unit, mix_spread = norm_stats(mixed, 1)
    norm_two = (mix_unit * mlp_gain + mlp_shift).astype(BF)
    pre_act = jnp.dot(norm_two, up_weight, preferred_element_type=F32) + up_bias
    half_erf = 0.5 * (1.0 + lax.erf(pre_act * (1.0 / math.sqrt(2.0))))
    hidden = (pre_act * half_erf).astype(BF)
    encoded = (
        mixed + jnp.dot(hidden, down_weight, preferred_element_type=F32) + down_bias
    ).astype(BF)

    out_grad = cotangent[0]
    out_grad_full = out_grad.astype(F32)
    hidden_grad = contract(out_grad, down_weight, 1, 1)
    slope = half_erf + pre_act * jnp.exp(-0.5 * pre_act * pre_act) * (1.0 / math.sqrt(2.0 * math.pi))
    pre_grad = (hidden_grad * slope).astype(BF)
    norm_two_grad = contract(pre_grad, up_weight, 1, 1)
    mixed_grad = out_grad_full + norm_back(norm_two_grad, mlp_gain, mix_unit, mix_spread, 1)
    attn_grad = mixed_grad.astype(BF)

    lifted = contract(attn_grad, value_weight, 1, 1).astype(BF)
    row_delta = jnp.sum(lifted.astype(F32) * pooled, axis=1, keepdims=True)

    def pull(part, feats):
        unit, spread, x_in, score, live = feats
        prob = jnp.where(live, jnp.exp(score - row_top), 0.0) / row_total
        score_grad = (prob * (jnp.dot(lifted, x_in, preferred_element_type=F32) - row_delta)).astype(BF)
        score_pool = contract(score_grad, x_in, 1, 1)
        x_in_grad = contract(absorbed, score_grad, 0, 0) + contract(lifted, prob.astype(BF), 0, 0)
        gain_part = jnp.sum(x_in_grad * unit, axis=1)
        shift_part = jnp.sum(x_in_grad, axis=1)
        colour_part = norm_back(x_in_grad, in_gain[:, None], unit, spread, 0)[:3]
        return score_pool, gain_part, shift_part, colour_part

    if blocks == 1:
        score_pool, in_gain_grad, in_shift_grad, all_colors = pull(parts[0], feats)
    else:

        def gather_up(carry, part):
            found = pull(part, features(part))
            return tuple(kept + new for kept, new in zip(carry, found[:3])), found[3]

        start = (
            jnp.zeros((latent.shape[0], in_gain.shape[0]), F32),
            jnp.zeros_like(in_gain),
            jnp.zeros_like(in_shift),
        )
        (score_pool, in_gain_grad, in_shift_grad), stacked = lax.scan(gather_up, start, parts)
        all_colors = stacked.transpose(1, 0, 2).reshape(3, -1)
    color_grad = lax.dynamic_slice(all_colors, (0, mine * own), (3, own))
    score_pool_low = score_pool.astype(BF)
    query_grad = (
        jnp.dot(score_pool_low, key_weight, preferred_element_type=F32) * (1.0 / root)
    ).astype(BF)
    norm_one_grad = contract(query_grad, query_weight, 1, 1)
    latent_grad = mixed_grad + norm_back(norm_one_grad, lat_gain, lat_unit, lat_spread, 1)

    def both(value):
        return jnp.concatenate([value, other(value)], axis=0)

    out_both = both(out_grad)
    hidden_both = both(hidden)
    two_both = both(norm_two)
    pre_both = both(pre_grad)
    attn_both = both(attn_grad)
    one_both = both(norm_one)
    query_both = both(query)
    query_grad_both = both(query_grad)
    pool_both = both(pooled_low)
    score_both = both(score_pool_low)
    wide = jnp.stack(
        [
            jnp.sum(norm_one_grad * lat_unit, axis=0),
            jnp.sum(norm_one_grad, axis=0),
            jnp.sum(norm_two_grad * mix_unit, axis=0),
            jnp.sum(norm_two_grad, axis=0),
        ]
    )
    narrow = jnp.stack([in_gain_grad, in_shift_grad])
    wide = wide + other(wide)
    narrow = narrow + other(narrow)
    return (
        encoded[None],
        latent_grad[None],
        color_grad[None],
        wide[0],
        wide[1],
        contract(one_both, query_grad_both, 0, 0),
        jnp.sum(query_grad_both.astype(F32), axis=0),
        narrow[0],
        narrow[1],
        contract(score_both, query_both, 0, 0) * (1.0 / root),
        contract(pool_both, attn_both, 0, 0),
        jnp.sum(attn_both.astype(F32), axis=0),
        wide[2],
        wide[3],
        contract(two_both, pre_both, 0, 0),
        jnp.sum(pre_both.astype(F32), axis=0),
        contract(hidden_both, out_both, 0, 0),
        jnp.sum(out_both.astype(F32), axis=0),
    )


def shards(*args):
    pixels = args[1]
    kept = lax.axis_size("pix") * pixels.shape[2] // 2
    fits = kept <= 4096 and kept % (3 * PULL) == 0 and pixels.shape[2] % LANES == 0
    return (on_chip if fits else in_blocks)(*args)


def solution(mesh):
    lat = P("img", None, None)
    whole = P()
    return jax.shard_map(
        shards,
        mesh=mesh,
        in_specs=(lat, P("img", None, "pix"), P("img", None, "pix"), P("img", "pix"))
        + (whole,) * 15
        + (lat,),
        out_specs=(lat, lat, P("img", None, "pix")) + (whole,) * 15,
        check_vma=False,
    )
```

```python
import math

import jax
import jax.numpy as jnp
import numpy as np
from jax import lax
from jax.experimental import pallas as pl
from jax.experimental.pallas import tpu as pltpu
from jax.sharding import PartitionSpec as P

BANDS = 64
GRID = 224
EPSILON = 1e-05
FLOOR = -1e30
BLOCK = 16
LANES = 128
BF = jnp.bfloat16
F32 = jnp.float32
VM = pl.BlockSpec(memory_space=pltpu.VMEM)
HBM = pl.BlockSpec(memory_space=pltpu.HBM)
MIB = 1 << 20
MAKE = 256
SCORE = 1024
POOL = 512
PULL = 1024
WIDE = 256
STRIP = 256


def fourier_lookup():
    position = np.arange(GRID, dtype=np.float32) * np.float32(2.0 / (GRID - 1)) - np.float32(1.0)
    frequency = np.float32(1.0) + np.arange(BANDS, dtype=np.float32) * np.float32(
        (GRID / 2.0 - 1.0) / (BANDS - 1)
    )
    phases = position[None, :] * (np.float32(math.pi) * frequency)[:, None]
    waves = np.concatenate([np.sin(phases.astype(np.float64)), np.cos(phases.astype(np.float64))])
    return waves.astype(np.float32)


def split_numpy(values):
    parts = []
    for _ in range(3):
        part = values.astype(BF).astype(np.float64)
        parts.append(part)
        values = values - part
    return parts


def lookup_with_sums():
    waves = fourier_lookup().astype(BF).astype(np.float64)
    sums = split_numpy(waves.sum(axis=0)) + split_numpy((waves * waves).sum(axis=0))
    table = np.zeros((2 * BANDS + 16, GRID))
    table[: 2 * BANDS] = waves
    table[2 * BANDS : 2 * BANDS + 6] = np.stack(sums)
    return table


def split(values):
    parts = []
    for _ in range(3):
        part = values.astype(BF)
        parts.append(part)
        values = values - part.astype(F32)
    return parts


def contract(left, right, left_dim, right_dim):
    return lax.dot_general(
        left, right, (((left_dim,), (right_dim,)), ((), ())), preferred_element_type=F32
    )


def norm_stats(values, axis):
    centre = values - jnp.mean(values, axis=axis, keepdims=True)
    spread = lax.rsqrt(jnp.mean(centre * centre, axis=axis, keepdims=True) + EPSILON)
    return centre * spread, spread


def norm_back(upstream, gain, unit, spread, axis):
    inner = upstream * gain
    return spread * (
        inner
        - jnp.mean(inner, axis=axis, keepdims=True)
        - unit * jnp.mean(inner * unit, axis=axis, keepdims=True)
    )


def out(shape, dtype):
    return jax.ShapeDtypeStruct(shape, dtype)


def padded(rows, step):
    return -(-rows // step) * step


def lane_ids(shape):
    return lax.broadcasted_iota(jnp.int32, shape, len(shape) - 1)


def waves_first(values, features):
    width = values.shape[1]
    lead = features - 4 * BANDS
    at = lane_ids(values.shape)
    waves = pltpu.roll(values, width - lead, 1)
    rest = pltpu.roll(values, 4 * BANDS, 1)
    return jnp.where(at < 4 * BANDS, waves, jnp.where(at < features, rest, 0.0))


def waves_last(values, features):
    width = values.shape[1]
    lead = features - 4 * BANDS
    at = lane_ids(values.shape)
    rest = pltpu.roll(values, width - 4 * BANDS, 1)
    waves = pltpu.roll(values, lead, 1)
    return jnp.where(at < lead, rest, jnp.where(at < features, waves, 0.0))


def fold(values):
    total = values[:, :LANES]
    for start in range(LANES, values.shape[1], LANES):
        total = total + values[:, start : start + LANES]
    return total


def fold_max(values):
    total = values[:, :LANES]
    for start in range(LANES, values.shape[1], LANES):
        total = jnp.maximum(total, values[:, start : start + LANES])
    return total


def fold_rows(values):
    total = values[:8]
    for start in range(8, values.shape[0], 8):
        total = total + values[start : start + 8]
    return total


def slot_of(kept_row):
    own = kept_row.shape[1]
    shape = (own, own)
    upper = lax.broadcasted_iota(jnp.int32, shape, 0) <= lax.broadcasted_iota(jnp.int32, shape, 1)
    tall = jnp.broadcast_to(kept_row, (8, own)).astype(BF)
    rank = jnp.dot(tall, jnp.where(upper, 1.0, 0.0).astype(BF), preferred_element_type=F32)[:1]
    slot = jnp.where(kept_row > 0, rank - 1.0, -1.0)
    return slot == lax.broadcasted_iota(jnp.int32, shape, 0).astype(F32)


class Fetch:
    def __init__(self, source, target, sem):
        self.copy = pltpu.make_async_copy(source, target, sem)
        self.target = target
        self.waiting = True

    def start(self):
        self.copy.start()

    def get(self):
        if self.waiting:
            self.copy.wait()
            self.waiting = False
        return self.target


def row_of(fetch):
    return fetch.get()[...].reshape(1, -1)


def pack_kernel(pixels, coords, kept, packed, rows):
    rows[...] = jnp.zeros_like(rows)
    rows[0:3, :] = pixels.get()[:, 0, :]
    rows[3:5, :] = coords.get()[...].astype(F32)
    kept_row = kept.get()[...].astype(F32)
    rows[5:6, :] = kept_row
    slots = jnp.where(slot_of(kept_row), 1.0, 0.0).astype(BF)
    squeezed = contract(rows[...].astype(BF), slots, 1, 1).astype(BF)
    packed[...] = jnp.broadcast_to(squeezed[None], packed.shape)


def pad_rows(target, source):
    rows = source.shape[0]
    whole = rows // LANES * LANES
    target[:whole, :] = source[:whole, :]
    target[whole:, :] = jnp.zeros_like(target[whole:, :])
    target[whole:rows, :] = source[whole:, :]


def turn_blocks(target, source):
    size = source.shape[0]
    for start in range(0, source.shape[1], size):
        span = slice(start, start + size)
        target[:, span] = jnp.transpose(source[:, span].astype(F32)).astype(BF)


def turn_pool(target, pool):
    count, tall = pool.shape
    turned = jnp.transpose(pool).astype(BF)
    target[...] = jnp.zeros_like(target)
    for at, start in enumerate(range(0, tall, count)):
        height = min(count, tall - start)
        target[:height, at * count : (at + 1) * count] = turned[start : start + height]


def query_kernel(
    features, latent, gain, shift, weight, bias, key_raw, in_gain, grad, down, in_shift,
    value_bias, mlp_gain, mlp_shift, up_bias, down_bias, table, up_hbm,
    early_out, absorbed_out, scorer, hidden_grad, table_kept, rows, ends, up,
    one, key, early, absorbed, sems,
):
    bring = [pltpu.make_async_copy(up_hbm, up, sems.at[0])]
    latent = latent.get()
    count, dim = latent.shape
    tall = absorbed.shape[1]
    turned, query = early.at[:, :dim], early.at[:, dim:]
    step = 32
    lat_gain, lat_shift = row_of(gain), row_of(shift)
    for start in range(0, count, step):
        unit, _ = norm_stats(latent[start : start + step, :].astype(F32), 1)
        one[start : start + step, :] = (unit * lat_gain + lat_shift).astype(BF)
    bias, weight = row_of(bias), weight.get()
    for copy in bring:
        copy.start()
    step = 256
    for start in range(0, dim, step):
        part = jnp.dot(one[...], weight[:, start : start + step], preferred_element_type=F32)
        query[:, start : start + step] = (part + bias[:, start : start + step]).astype(BF)
    turn_blocks(turned, one)
    pad_rows(key, key_raw.get())
    lifted = contract(query[...], key[...], 1, 1) * (1.0 / math.sqrt(dim))
    lifted = waves_first(lifted, features)
    absorbed[...] = lifted
    gains = gain_row(in_gain, tall, features)
    scorer[...] = (lifted * gains * math.log2(math.e)).astype(BF)
    ends[...] = jnp.zeros_like(ends)
    ends[0:1, :] = gains
    ends[1:2, :] = gain_row(in_shift, tall, features)
    grad = grad.get()
    leave = [
        pltpu.make_async_copy(early, early_out, sems.at[2]),
        pltpu.make_async_copy(absorbed, absorbed_out, sems.at[3]),
    ]
    for copy in leave:
        copy.start()
    table_kept[...] = table.get()[...]
    rows[...] = jnp.zeros_like(rows)
    for at, vector in enumerate((value_bias, mlp_gain, mlp_shift, up_bias, down_bias)):
        rows[at : at + 1, :] = row_of(vector)
    rows[5:6, :] = lat_gain
    down = down.get()
    for start in range(0, dim, step):
        part = contract(grad[...], down[start : start + step, :], 1, 1)
        hidden_grad[:, start : start + step] = part.astype(BF)
    for copy in bring + leave:
        copy.wait()


def gain_row(fetch, width, features):
    row = row_of(fetch)
    wide = jnp.concatenate([row, jnp.zeros((1, width - features), F32)], axis=1)
    return waves_first(jnp.broadcast_to(wide, (8, width)), features)[:1]


def segment_counts(segments, stop):
    return [jnp.sum(segments[index][5:6, :].astype(F32)).astype(jnp.int32) for index in range(stop)]


def forward_kernel(
    features,
    segments, scorer, hidden_grad, table, latent, value_raw, up, rows, ends, grad,
    hidden, mixed, packs, mixed_grad, lift_out, puller, unit_out, spread_out, score_out, pool_unit, stats, sums,
    placed, places, top, weight, pooled, back, mix_unit, mix_spread, value, two, pool_low,
):
    pix, _, own = segments.shape
    tall, kept = unit_out.shape
    waves = 4 * BANDS
    ones = slice(features, waves + 8)

    placed[...] = jnp.zeros_like(placed)
    offset = jnp.int32(0)
    for index, found in enumerate(segment_counts(segments, pix)):
        wide = jnp.concatenate([segments[index].astype(F32), jnp.zeros((8, LANES), F32)], axis=1)
        inside = lax.rem(offset, LANES)
        base = pl.multiple_of(jnp.minimum(offset - inside, kept), LANES)
        placed[:, pl.ds(base, own + LANES)] += pltpu.roll(wide, inside, 1)
        offset = offset + found
    places[...] = lax.broadcasted_iota(jnp.int32, places.shape, 0).astype(F32).astype(BF)
    unit_out[waves + 16 :, :] = jnp.zeros((tall - waves - 16, kept), BF)
    top[...] = jnp.full_like(top, FLOOR)

    for start in range(0, kept, MAKE):
        step = MAKE
        lanes = slice(start, start + step)
        raw = placed[:, lanes]
        column = jnp.concatenate([places[...]] * (step // LANES), axis=1)
        one, none = jnp.ones((), BF), jnp.zeros((), BF)
        row_hot = jnp.where(column == raw[3:4].astype(BF), one, none)
        col_hot = jnp.where(column == raw[4:5].astype(BF), one, none)
        row_waves = jnp.dot(table[...], row_hot, preferred_element_type=F32)
        col_waves = jnp.dot(table[...], col_hot, preferred_element_type=F32)
        at = lax.broadcasted_iota(jnp.int32, raw.shape, 0)
        position = (raw * (2.0 / (GRID - 1)) - 1.0).astype(BF).astype(F32)
        extra = jnp.where(at < 3, raw, jnp.where(at < 5, position, 0.0))
        both = row_waves[2 * BANDS :] + col_waves[2 * BANDS :]
        mean = (
            jnp.sum(both[0:3], axis=0, keepdims=True) + jnp.sum(extra, axis=0, keepdims=True)
        ) * (1.0 / features)
        square = (
            jnp.sum(both[3:6], axis=0, keepdims=True) + jnp.sum(extra * extra, axis=0, keepdims=True)
        ) * (1.0 / features)
        spread = lax.rsqrt(jnp.maximum(square - mean * mean, 0.0) + EPSILON)
        centre = mean * spread
        spread_out[:, lanes] = jnp.broadcast_to(spread, (8, step))
        for piece, low in (
            (row_waves[:BANDS], 0),
            (col_waves[:BANDS], BANDS),
            (row_waves[BANDS : 2 * BANDS], 2 * BANDS),
            (col_waves[BANDS : 2 * BANDS], 3 * BANDS),
        ):
            unit_out[low : low + BANDS, lanes] = (piece * spread - centre).astype(BF)
        tail = jnp.where(at < features - waves, extra * spread - centre, 1.0)
        tail = jnp.concatenate([tail, jnp.zeros((8, step), F32)], axis=0)
        unit_out[waves : waves + 16, lanes] = tail.astype(BF)
    for start in range(0, kept, SCORE):
        lanes = slice(start, start + SCORE)
        score = jnp.dot(scorer[...], unit_out[:, lanes], preferred_element_type=F32)
        score_out[:, lanes] = score
        top[...] = jnp.maximum(top[...], fold_max(score))
    peak = jnp.max(top[...], axis=1, keepdims=True)
    top[...] = jnp.broadcast_to(peak, top.shape)
    for start in range(0, kept, POOL):
        lanes = slice(start, start + POOL)
        weight[:, lanes] = jnp.exp2(score_out[:, lanes] - top[:, :1]).astype(BF)
    pooled[...] = contract(weight[...], unit_out[...], 1, 1)
    total = pooled[:, features : features + 1]
    pool_unit[...] = pooled[...] * (1.0 / total)
    gains, shifts = ends[0:1, :], ends[1:2, :]
    count, dim = mixed.shape
    value_bias, gain, shift, up_bias = (rows[at : at + 1, :] for at in range(4))
    hidden_turned, two_turned, pre_grad, attn_grad, kept_grad = (
        packs.at[:, at * dim : (at + 1) * dim] for at in range(5)
    )
    pool = waves_last(pool_unit[...] * gains + shifts, features)
    pool_low[...] = pool.astype(BF)
    turn_pool(packs.at[:, 5 * dim :], pool)

    latent = latent.get()
    pad_rows(value, value_raw.get())
    wide = WIDE
    for start in range(0, dim, wide):
        span = slice(start, start + wide)
        attn = jnp.dot(pool_low[...], value[:, span], preferred_element_type=F32) + value_bias[:, span]
        mixed[:, span] = latent[:, span].astype(F32) + attn
    low = 32
    for start in range(0, count, low):
        span = slice(start, start + low)
        unit, spread = norm_stats(mixed[span, :], 1)
        mix_unit[span, :] = unit
        mix_spread[span, :] = jnp.broadcast_to(spread, (low, LANES))
        two[span, :] = (unit * gain + shift).astype(BF)
    turn_blocks(two_turned, two)
    for start in range(0, dim, wide):
        span = slice(start, start + wide)
        act = jnp.dot(two[...], up[:, span], preferred_element_type=F32) + up_bias[:, span]
        half = 0.5 * (1.0 + lax.erf(act * (1.0 / math.sqrt(2.0))))
        active = act * half
        hidden[:, span] = active.astype(BF)
        hidden_turned[:, span] = jnp.transpose(active).astype(BF)
        slope = half + act * jnp.exp(-0.5 * act * act) * (1.0 / math.sqrt(2.0 * math.pi))
        pre_grad[:, span] = (hidden_grad[:, span].astype(F32) * slope).astype(BF)
    for start in range(0, dim, wide):
        span = slice(start, start + wide)
        back[:, span] = contract(pre_grad[...], up[span, :], 1, 1)
    grad = grad.get()
    kept_grad[...] = grad[...]
    gain_sum = jnp.zeros((8, dim), F32)
    shift_sum = jnp.zeros((8, dim), F32)
    for start in range(0, count, low):
        span = slice(start, start + low)
        upstream = back[span, :]
        unit = mix_unit[span, :]
        full = grad[span, :].astype(F32) + norm_back(upstream, gain, unit, mix_spread[span, :1], 1)
        mixed_grad[span, :] = full
        attn_grad[span, :] = full.astype(BF)
        gain_sum = gain_sum + fold_rows(upstream * unit)
        shift_sum = shift_sum + fold_rows(upstream)
    sums[0:1, :] = jnp.sum(gain_sum, axis=0, keepdims=True)
    sums[1:2, :] = jnp.sum(shift_sum, axis=0, keepdims=True)
    lifted = waves_first(contract(attn_grad[...], value[...], 1, 1), features)
    lift_out[...] = lifted
    pulled = (lifted * gains).astype(BF)
    at = lane_ids(pulled.shape)
    inside = jnp.where(at < features, pulled.astype(F32) * pool_unit[...], 0.0)
    delta = jnp.sum(inside, axis=1, keepdims=True)
    for lane, part in enumerate(split(-delta)):
        pulled = jnp.where(at == features + lane, part, pulled)
    puller[...] = pulled
    at = lane_ids(stats.shape)
    stats[...] = jnp.where(at == 0, peak + jnp.log2(total), delta)


def write_vectors(array, lines, vectors):
    width = array.shape[0]
    lines[...] = jnp.zeros_like(lines)
    row = 0
    for vector in vectors:
        for part in split(vector):
            for start in range(0, vector.shape[1], width):
                lines[row : row + 1, :] = part[:, start : start + width].astype(F32)
                row += 1
    array[LANES : LANES + lines.shape[0], array.shape[1] - width :] = lines[...].astype(BF)


def read_vectors(array, dim, number):
    width = array.shape[0]
    turns = dim // width
    high = padded(3 * number * turns, 16)
    lines = array[LANES : LANES + high, array.shape[1] - width :].astype(F32)
    vectors = []
    for at in range(number):
        first = 3 * at * turns
        total = sum(lines[first + part * turns : first + (part + 1) * turns] for part in range(3))
        vectors.append(jnp.concatenate([total[turn : turn + 1] for turn in range(turns)], axis=1))
    return vectors


def pull_kernel(
    features,
    segments, kept_row, absorbed, lifted, puller, unit_in, spread_in, score, pool_unit, stats,
    key_raw, sums, ends, query_weight, latent, rows, mixed_grad, early,
    late, color_grad, latent_grad,
    pulls, pooled, key, back, lines, early_sem,
):
    count, dim = pooled.shape[0], key.shape[1]
    own = segments.shape[2]
    tall, kept = unit_in.shape
    bring = pltpu.make_async_copy(early, late.at[:, dim : 3 * dim], early_sem)
    bring.start()
    waves = 4 * BANDS
    def shares(lanes):
        inner = jnp.dot(puller[...], unit_in[:, lanes], preferred_element_type=F32)
        prob = jnp.exp2(score[:, lanes] - stats[:, :1])
        return inner, prob, (prob * inner).astype(BF)

    for start in range(0, kept, PULL):
        lanes = slice(start, start + PULL)
        pulls[:, lanes] = shares(lanes)[2]
    pooled[...] = contract(pulls[...], unit_in[...], 1, 1)
    gains, shifts = ends[0:1, :], ends[1:2, :]
    kept_row, key_raw, query_weight = kept_row.get(), key_raw.get(), query_weight.get()
    latent, absorbed = latent.get(), absorbed.get()

    mine = lax.axis_index("pix")
    offset = jnp.int32(0)
    for index, found in enumerate(segment_counts(segments, segments.shape[0])):
        offset = offset + jnp.where(index < mine, found, 0)
    inside = lax.rem(offset, LANES)
    base = pl.multiple_of(jnp.minimum(offset - inside, kept - own - LANES), LANES)
    inside = offset - base
    lanes = pl.ds(base, own + LANES)
    inner, prob, score_grad = shares(lanes)
    tilt = score_grad.astype(F32) * score[:, lanes] * math.log(2.0) + prob * (inner + stats[:, 1:2])
    tilt = jnp.sum(tilt, axis=0, keepdims=True) * (1.0 / features)
    factors = []
    for held in (absorbed, lifted):
        scaled = held[...] * gains
        at = lane_ids((count, LANES))
        corner = jnp.where(at == 3, jnp.sum(scaled, axis=1, keepdims=True), scaled[:, waves : waves + LANES])
        factors.append(jnp.transpose(corner)[:8].astype(BF))
    both = jnp.concatenate([score_grad, prob.astype(BF)], axis=0)
    terms = jnp.dot(jnp.concatenate(factors, axis=1), both, preferred_element_type=F32)
    unit = unit_in[waves : waves + 16, lanes].astype(F32)[:8]
    colors = spread_in[:, lanes] * (terms - terms[3:4] * (1.0 / features) - unit * tilt)
    window = pltpu.roll(colors, own + LANES - inside, 1)[:, :own]
    slots = jnp.where(slot_of(kept_row[...].astype(F32)), 1.0, 0.0)
    spread_back = jnp.dot(window, slots, precision=lax.Precision.HIGHEST, preferred_element_type=F32)
    color_grad[:, 0, :] = spread_back[:3]

    held = pooled[...]
    total = held[:, features : features + 1]
    pool = waves_last(held * gains + shifts * total, features)
    turn_pool(late.at[:, 3 * dim :], pool)
    pool = pool.astype(BF)
    pad_rows(key, key_raw)
    gain_sum = absorbed[...] * held + lifted[...] * pool_unit[...]
    shift_sum = absorbed[...] * total + lifted[...]
    vectors = []
    for found in (gain_sum, shift_sum):
        flat = jnp.sum(fold_rows(found), axis=0, keepdims=True)
        flat = waves_last(jnp.broadcast_to(flat, (8, tall)), features)[:1]
        vectors.append(jnp.concatenate([flat, jnp.zeros((1, dim - tall), F32)], axis=1))
    vectors += [sums[0:1, :], sums[1:2, :]]
    wide = WIDE
    for start in range(0, dim, wide):
        span = slice(start, start + wide)
        part = jnp.dot(pool, key[:, span], preferred_element_type=F32) * (1.0 / math.sqrt(dim))
        late[:, span] = part.astype(BF)
    for start in range(0, dim, wide):
        span = slice(start, start + wide)
        back[:, span] = contract(late[:, :dim], query_weight[span, :], 1, 1)
    low = 32
    gain = rows[5:6, :]
    gain_sum = jnp.zeros((8, dim), F32)
    shift_sum = jnp.zeros((8, dim), F32)
    for start in range(0, count, low):
        span = slice(start, start + low)
        unit, spread = norm_stats(latent[span, :].astype(F32), 1)
        upstream = back[span, :]
        latent_grad[span, :] = mixed_grad[span, :] + norm_back(upstream, gain, unit, spread, 1)
        gain_sum = gain_sum + fold_rows(upstream * unit)
        shift_sum = shift_sum + fold_rows(upstream)
    vectors += [jnp.sum(gain_sum, axis=0, keepdims=True), jnp.sum(shift_sum, axis=0, keepdims=True)]
    write_vectors(late, lines, vectors)
    bring.wait()


class Leaving:
    def __init__(self, buffers, sems):
        self.buffers, self.sems, self.flying, self.turn = buffers, sems, {}, 0

    def free(self):
        slot = self.turn % self.buffers.shape[0]
        if slot in self.flying:
            self.flying[slot].wait()
        return self.buffers.at[slot]

    def send(self, target):
        slot = self.turn % self.buffers.shape[0]
        self.turn += 1
        self.flying[slot] = pltpu.make_async_copy(self.buffers.at[slot], target, self.sems.at[slot])
        self.flying[slot].start()

    def end(self):
        for copy in self.flying.values():
            copy.wait()


def parts_of(ref, dim):
    squares = ref.shape[1] // dim
    parts = [ref.at[:, at * dim : (at + 1) * dim] for at in range(squares)]
    return parts + ([ref.at[:, squares * dim :]] if ref.shape[1] % dim else [])


def products(leaving, left, left_far, right, right_far, target, bias):
    count = left.shape[0]
    size = leaving.buffers.shape[1]
    for start in range(0, left.shape[1], size):
        buffer = leaving.free()
        at, inner = start // count * count, start % count
        rows, lanes = slice(inner, inner + size), slice(at, at + count)
        strip = jnp.concatenate([left[rows, lanes], left_far[rows, lanes]], axis=1)
        if bias is not None and start == 0:
            strip = jnp.concatenate([strip, jnp.ones((16, 2 * count), BF)], axis=0)
        found = jnp.dot(strip, jnp.concatenate([right[...], right_far[...]], axis=0), preferred_element_type=F32)
        buffer[...] = found[:size]
        if bias is not None and start == 0:
            bias[...] = found[size]
        leaving.send(target.at[start : start + size, :])


def short_product(held, left, left_far, right, right_far, bias, scale):
    features, count = held.shape[0], left.shape[0]
    pieces = []
    for at, start in enumerate(range(0, features, count)):
        height = min(count, padded(features - start, 16))
        lanes = slice(at * count, (at + 1) * count)
        pieces.append(jnp.concatenate([left[:height, lanes], left_far[:height, lanes]], axis=1))
    high = sum(piece.shape[0] for piece in pieces)
    pieces.append(jnp.ones((16, 2 * count), BF))
    both = jnp.concatenate([right[...], right_far[...]], axis=0)
    found = jnp.dot(jnp.concatenate(pieces, axis=0), both, preferred_element_type=F32)
    held[...] = found[:features] if scale is None else found[:features] * scale
    if bias is not None:
        bias[...] = found[high]


def late_kernel(
    features,
    packs, packs_far, color_grad, latent_grad,
    color_out, latent_out, down_out, down_bias, up_out, up_bias, value_out, value_bias,
    buffers, held, sems, held_sem, out_sems,
):
    dim = down_out.shape[1]
    hidden, two, pre, attn, grad, pool = parts_of(packs, dim)
    hidden_far, two_far, pre_far, attn_far, grad_far, pool_far = parts_of(packs_far, dim)
    first = [
        pltpu.make_async_copy(latent_grad, latent_out, out_sems.at[0]),
        pltpu.make_async_copy(color_grad, color_out, out_sems.at[1]),
    ]
    for copy in first:
        copy.start()
    leaving = Leaving(buffers, sems)
    products(leaving, hidden, hidden_far, grad, grad_far, down_out, down_bias)
    short_product(held, pool, pool_far, attn, attn_far, value_bias, None)
    leave = pltpu.make_async_copy(held, value_out, held_sem)
    leave.start()
    products(leaving, two, two_far, pre, pre_far, up_out, up_bias)
    for copy in first:
        copy.wait()
    leave.wait()
    leaving.end()


def last_kernel(
    features,
    late, late_far, hidden, mixed, down, rows, _,
    encoded_out, query_out, query_bias, key_out, lat_gain, lat_shift, mlp_gain, mlp_shift, in_gain, in_shift,
    buffers, held, encoded, sems, held_sem, encoded_sem,
):
    dim = query_out.shape[1]
    grad, one, query, pool = parts_of(late, dim)
    grad_far, one_far, query_far, pool_far = parts_of(late_far, dim)
    leaving = Leaving(buffers, sems)
    products(leaving, one, one_far, grad, grad_far, query_out, query_bias)
    short_product(held, pool, pool_far, query, query_far, None, 1.0 / math.sqrt(dim))
    short = pltpu.make_async_copy(held, key_out, held_sem)
    short.start()
    for start in range(0, dim, WIDE):
        span = slice(start, start + WIDE)
        part = jnp.dot(hidden[...], down[:, span], preferred_element_type=F32)
        encoded[:, span] = (mixed[:, span] + part + rows[4:5, span]).astype(BF)
    leave = pltpu.make_async_copy(encoded, encoded_out, encoded_sem)
    leave.start()
    pairs = zip(read_vectors(late, dim, 6), read_vectors(late_far, dim, 6))
    places = (in_gain, in_shift, mlp_gain, mlp_shift, lat_gain, lat_shift)
    for place, (own, far) in zip(places, pairs):
        place[...] = (own + far)[0, : place.shape[0]]
    leaving.end()
    short.wait()
    leave.wait()


def call(body, outs, args, fetched, scratch, vmem, flops, moved, unread=()):
    places = [at for at in range(len(args)) if at in fetched]
    buffers = [pltpu.VMEM(args[at].shape, args[at].dtype) for at in places]
    shapes = tuple(pltpu.HBM(shape, dtype) if place is HBM else out(shape, dtype) for shape, dtype, place in outs)

    def whole(*refs):
        sources, rest = list(refs[: len(args)]), refs[len(args) :]
        targets = ()
        if places:
            targets, sems, rest = rest[-len(buffers) - 1 : -1], rest[-1], rest[: -len(buffers) - 1]
        for slot, (at, target) in enumerate(zip(places, targets)):
            sources[at] = Fetch(sources[at], target, sems.at[slot])
            sources[at].start()
        body(*sources, *rest)
        for at in places:
            sources[at].get()

    return pl.pallas_call(
        whole,
        out_shape=shapes if len(shapes) > 1 else shapes[0],
        in_specs=tuple(HBM if at in fetched or at in unread else VM for at in range(len(args))),
        out_specs=tuple(place for _, _, place in outs) if len(outs) > 1 else outs[0][2],
        scratch_shapes=list(scratch) + buffers + ([pltpu.SemaphoreType.DMA((len(places),))] if places else []),
        compiler_params=pltpu.CompilerParams(vmem_limit_bytes=vmem * MIB),
        cost_estimate=pl.CostEstimate(flops=flops, bytes_accessed=moved, transcendentals=0),
    )(*(pltpu.with_memory_space_constraint(arg, pltpu.HBM) if at in fetched or at in unread else arg for at, arg in enumerate(args)))


def on_chip(
    latents, pixels, coords, kept_mask, lat_gain, lat_shift, query_weight, query_bias, in_gain, in_shift,
    key_weight, value_weight, value_bias, mlp_gain, mlp_shift, up_weight, up_bias, down_weight, down_bias,
    cotangent,
):
    pix = lax.axis_size("pix")
    own = pixels.shape[2]
    kept = pix * own // 2
    _, count, dim = latents.shape
    features = in_gain.shape[0]
    tall = padded(features, LANES)
    latent, out_grad = latents[0], cotangent[0]
    swap = [(0, 1), (1, 0)]

    def other(value):
        return lax.ppermute(value, "img", swap)

    packed = call(
        pack_kernel, [((pix, 8, own), BF, VM)], (pixels.transpose(1, 0, 2), coords[0], kept_mask), (0, 1, 2),
        [pltpu.VMEM((8, own), F32)], 8, 4 * 8 * own * own, 16 * 8 * own,
    )
    segments = lax.all_to_all(packed, "pix", 0, 0)

    table = jnp.asarray(lookup_with_sums(), BF)
    wide = pltpu.VMEM((tall, dim), BF)
    early, absorbed, scorer, hidden_grad, table_kept, rows, ends, up_kept = call(
        lambda *refs: query_kernel(features, *refs),
        [
            ((count, 2 * dim), BF, HBM), ((count, tall), F32, HBM), ((count, tall), BF, VM), ((count, dim), BF, VM),
            (table.shape, BF, VM), ((8, dim), F32, VM), ((8, tall), F32, VM), ((dim, dim), BF, VM),
        ],
        (
            latent, lat_gain, lat_shift, query_weight, query_bias, key_weight, in_gain, out_grad, down_weight,
            in_shift, value_bias, mlp_gain, mlp_shift, up_bias, down_bias, table, up_weight,
        ),
        tuple(range(16)),
        [
            pltpu.VMEM((count, dim), BF), wide, pltpu.VMEM((count, 2 * dim), BF), pltpu.VMEM((count, tall), F32),
            pltpu.SemaphoreType.DMA((4,)),
        ],
        16, 4 * count * dim * dim + 2 * count * dim * tall, 8 * MIB, (16,),
    )

    narrow = pltpu.VMEM((count, LANES), F32)
    area = pltpu.VMEM((count, dim), F32)
    low = pltpu.VMEM((count, dim), BF)
    spare = 512
    (
        hidden, mixed, packs, mixed_grad, lifted, puller, unit_in, spread_in, score, pool_unit, stats, sums,
    ) = call(
        lambda *refs: forward_kernel(features, *refs),
        [
            ((count, dim), BF, VM), ((count, dim), F32, VM), ((count, 5 * dim + spare), BF, VM),
            ((count, dim), F32, VM),
            ((count, tall), F32, VM), ((count, tall), BF, VM), ((tall, kept), BF, VM), ((8, kept), F32, VM),
            ((count, kept), F32, VM), ((count, tall), F32, VM), ((count, LANES), F32, VM), ((8, dim), F32, VM),
        ],
        (
            segments, scorer, hidden_grad, table_kept, latent, value_weight, up_kept, rows, ends, out_grad,
        ),
        (4, 5, 9),
        [
            pltpu.VMEM((8, kept + own + LANES), F32), pltpu.VMEM((GRID, LANES), BF), narrow,
            pltpu.VMEM((count, kept), BF), pltpu.VMEM((count, tall), F32), area, area, narrow, wide, low,
            pltpu.VMEM((count, tall), BF),
        ],
        20, 6 * count * dim * dim + 4 * count * dim * tall + 6 * kept * count * tall, 8 * MIB,
    )

    late, color_grad, latent_grad = call(
        lambda *refs: pull_kernel(features, *refs),
        [
            ((count, 3 * dim + spare), BF, VM), ((3, 1, own), F32, VM), ((count, dim), F32, VM),
        ],
        (
            segments, kept_mask, absorbed, lifted, puller, unit_in, spread_in, score, pool_unit, stats, key_weight,
            sums, ends, query_weight, latent, rows, mixed_grad, early,
        ),
        (1, 2, 10, 13, 14),
        [
            pltpu.VMEM((count, kept), BF), pltpu.VMEM((count, tall), F32), wide, area, pltpu.VMEM((80, count), F32),
            pltpu.SemaphoreType.DMA(()),
        ],
        16, 2 * count * dim * dim + 4 * kept * count * tall, 8 * MIB, (17,),
    )

    packs_far = other(packs)
    late_far = other(late)
    square = ((dim, dim), F32, HBM)
    slab = ((features, dim), F32, HBM)
    line = ((dim,), F32, VM)
    short = ((features,), F32, VM)
    slots = [
        pltpu.VMEM((4, STRIP, dim), F32), pltpu.VMEM((features, dim), F32),
    ]
    sems = [pltpu.SemaphoreType.DMA((4,)), pltpu.SemaphoreType.DMA(())]
    (
        color_grad, latent_grad, down_weight_grad, down_bias_grad, up_weight_grad, up_bias_grad, value_weight_grad,
        value_bias_grad,
    ) = call(
        lambda *refs: late_kernel(features, *refs),
        [((3, 1, own), F32, HBM), ((count, dim), F32, HBM), square, line, square, line, slab, line],
        (packs, packs_far, color_grad, latent_grad), (),
        slots + sems + [pltpu.SemaphoreType.DMA((2,))], 12, 8 * count * dim * dim + 4 * count * dim * tall, 10 * MIB,
    )
    (
        encoded, query_weight_grad, query_bias_grad, key_weight_grad, lat_gain_grad, lat_shift_grad, mlp_gain_grad,
        mlp_shift_grad, in_gain_grad, in_shift_grad,
    ) = call(
        lambda *refs: last_kernel(features, *refs),
        [((count, dim), BF, HBM), square, line, slab, line, line, line, line, short, short],
        (
            late, late_far, hidden, mixed, down_weight, rows,
            down_weight_grad,
        ),
        (), slots + [low] + sems + [pltpu.SemaphoreType.DMA(())], 12, 4 * count * dim * dim + 4 * count * dim * tall, 6 * MIB, (6,),
    )

    return (
        encoded[None], latent_grad[None], color_grad.transpose(1, 0, 2), lat_gain_grad, lat_shift_grad,
        query_weight_grad, query_bias_grad, in_gain_grad, in_shift_grad, key_weight_grad, value_weight_grad,
        value_bias_grad, mlp_gain_grad, mlp_shift_grad, up_weight_grad, up_bias_grad, down_weight_grad, down_bias_grad,
    )


def in_blocks(
    latents,
    pixels,
    coords,
    kept_mask,
    lat_gain,
    lat_shift,
    query_weight,
    query_bias,
    in_gain,
    in_shift,
    key_weight,
    value_weight,
    value_bias,
    mlp_gain,
    mlp_shift,
    up_weight,
    up_bias,
    down_weight,
    down_bias,
    cotangent,
):
    pix = lax.axis_size("pix")
    mine = lax.axis_index("pix")
    own = pixels.shape[2]
    packed = jnp.concatenate(
        [
            pixels[0].astype(BF),
            coords[0].astype(BF),
            kept_mask.astype(BF),
            jnp.zeros((2, own), BF),
        ],
        axis=0,
    )
    gathered = lax.all_to_all(jnp.broadcast_to(packed[None], (pix,) + packed.shape), "pix", 0, 0)
    every = gathered.transpose(1, 0, 2).reshape(packed.shape[0], pix * own)
    swap = [(0, 1), (1, 0)]

    def other(value):
        return lax.ppermute(value, "img", swap)

    root = math.sqrt(latents.shape[2])
    latent = latents[0].astype(F32)
    lat_unit, lat_spread = norm_stats(latent, 1)
    norm_one = (lat_unit * lat_gain + lat_shift).astype(BF)
    query = (jnp.dot(norm_one, query_weight, preferred_element_type=F32) + query_bias).astype(BF)
    absorbed = (contract(query, key_weight, 1, 1) * (1.0 / root)).astype(BF)

    waves = jnp.asarray(fourier_lookup(), BF)
    places = jnp.arange(GRID, dtype=F32)[:, None]

    def features(part):
        cells = part[3:5].astype(F32)
        position = (cells * (2.0 / (GRID - 1)) - 1.0).astype(BF)
        row_waves = jnp.dot(waves, (cells[0:1] == places).astype(BF), preferred_element_type=F32).astype(BF)
        col_waves = jnp.dot(waves, (cells[1:2] == places).astype(BF), preferred_element_type=F32).astype(BF)
        table = jnp.concatenate(
            [part[0:3], position, row_waves[:BANDS], col_waves[:BANDS], row_waves[BANDS:], col_waves[BANDS:]],
            axis=0,
        ).astype(F32)
        unit, spread = norm_stats(table, 0)
        x_in = (unit * in_gain[:, None] + in_shift[:, None]).astype(BF)
        score = jnp.dot(absorbed, x_in, preferred_element_type=F32)
        return unit, spread, x_in, jnp.where(part[5:6] > 0, score, FLOOR), part[5:6] > 0

    def pool(part, feats):
        unit, spread, x_in, score, live = feats
        top = jnp.max(score, axis=1, keepdims=True)
        weight = jnp.where(live, jnp.exp(score - top), 0.0)
        return top, jnp.sum(weight, axis=1, keepdims=True), contract(weight.astype(BF), x_in, 1, 1)

    blocks = max(1, pix // BLOCK)
    parts = every.reshape(packed.shape[0], blocks, -1).transpose(1, 0, 2)
    if blocks == 1:
        feats = features(parts[0])
        row_top, row_total, pooled = pool(parts[0], feats)
    else:

        def merge(carry, part):
            top, total, sums = pool(part, features(part))
            new_top = jnp.maximum(carry[0], top)
            old_scale, new_scale = jnp.exp(carry[0] - new_top), jnp.exp(top - new_top)
            return (
                new_top,
                carry[1] * old_scale + total * new_scale,
                carry[2] * old_scale + sums * new_scale,
            ), None

        start = (
            jnp.full((latent.shape[0], 1), FLOOR, F32),
            jnp.zeros((latent.shape[0], 1), F32),
            jnp.zeros((latent.shape[0], in_gain.shape[0]), F32),
        )
        row_top, row_total, pooled = lax.scan(merge, start, parts)[0]
    pooled = pooled / row_total
    pooled_low = pooled.astype(BF)
    attn = jnp.dot(pooled_low, value_weight, preferred_element_type=F32) + value_bias
    mixed = latent + attn
    mix_unit, mix_spread = norm_stats(mixed, 1)
    norm_two = (mix_unit * mlp_gain + mlp_shift).astype(BF)
    pre_act = jnp.dot(norm_two, up_weight, preferred_element_type=F32) + up_bias
    half_erf = 0.5 * (1.0 + lax.erf(pre_act * (1.0 / math.sqrt(2.0))))
    hidden = (pre_act * half_erf).astype(BF)
    encoded = (
        mixed + jnp.dot(hidden, down_weight, preferred_element_type=F32) + down_bias
    ).astype(BF)

    out_grad = cotangent[0]
    out_grad_full = out_grad.astype(F32)
    hidden_grad = contract(out_grad, down_weight, 1, 1)
    slope = half_erf + pre_act * jnp.exp(-0.5 * pre_act * pre_act) * (1.0 / math.sqrt(2.0 * math.pi))
    pre_grad = (hidden_grad * slope).astype(BF)
    norm_two_grad = contract(pre_grad, up_weight, 1, 1)
    mixed_grad = out_grad_full + norm_back(norm_two_grad, mlp_gain, mix_unit, mix_spread, 1)
    attn_grad = mixed_grad.astype(BF)

    lifted = contract(attn_grad, value_weight, 1, 1).astype(BF)
    row_delta = jnp.sum(lifted.astype(F32) * pooled, axis=1, keepdims=True)

    def pull(part, feats):
        unit, spread, x_in, score, live = feats
        prob = jnp.where(live, jnp.exp(score - row_top), 0.0) / row_total
        score_grad = (prob * (jnp.dot(lifted, x_in, preferred_element_type=F32) - row_delta)).astype(BF)
        score_pool = contract(score_grad, x_in, 1, 1)
        x_in_grad = contract(absorbed, score_grad, 0, 0) + contract(lifted, prob.astype(BF), 0, 0)
        gain_part = jnp.sum(x_in_grad * unit, axis=1)
        shift_part = jnp.sum(x_in_grad, axis=1)
        colour_part = norm_back(x_in_grad, in_gain[:, None], unit, spread, 0)[:3]
        return score_pool, gain_part, shift_part, colour_part

    if blocks == 1:
        score_pool, in_gain_grad, in_shift_grad, all_colors = pull(parts[0], feats)
    else:

        def gather_up(carry, part):
            found = pull(part, features(part))
            return tuple(kept + new for kept, new in zip(carry, found[:3])), found[3]

        start = (
            jnp.zeros((latent.shape[0], in_gain.shape[0]), F32),
            jnp.zeros_like(in_gain),
            jnp.zeros_like(in_shift),
        )
        (score_pool, in_gain_grad, in_shift_grad), stacked = lax.scan(gather_up, start, parts)
        all_colors = stacked.transpose(1, 0, 2).reshape(3, -1)
    color_grad = lax.dynamic_slice(all_colors, (0, mine * own), (3, own))
    score_pool_low = score_pool.astype(BF)
    query_grad = (
        jnp.dot(score_pool_low, key_weight, preferred_element_type=F32) * (1.0 / root)
    ).astype(BF)
    norm_one_grad = contract(query_grad, query_weight, 1, 1)
    latent_grad = mixed_grad + norm_back(norm_one_grad, lat_gain, lat_unit, lat_spread, 1)

    def both(value):
        return jnp.concatenate([value, other(value)], axis=0)

    out_both = both(out_grad)
    hidden_both = both(hidden)
    two_both = both(norm_two)
    pre_both = both(pre_grad)
    attn_both = both(attn_grad)
    one_both = both(norm_one)
    query_both = both(query)
    query_grad_both = both(query_grad)
    pool_both = both(pooled_low)
    score_both = both(score_pool_low)
    wide = jnp.stack(
        [
            jnp.sum(norm_one_grad * lat_unit, axis=0),
            jnp.sum(norm_one_grad, axis=0),
            jnp.sum(norm_two_grad * mix_unit, axis=0),
            jnp.sum(norm_two_grad, axis=0),
        ]
    )
    narrow = jnp.stack([in_gain_grad, in_shift_grad])
    wide = wide + other(wide)
    narrow = narrow + other(narrow)
    return (
        encoded[None],
        latent_grad[None],
        color_grad[None],
        wide[0],
        wide[1],
        contract(one_both, query_grad_both, 0, 0),
        jnp.sum(query_grad_both.astype(F32), axis=0),
        narrow[0],
        narrow[1],
        contract(score_both, query_both, 0, 0) * (1.0 / root),
        contract(pool_both, attn_both, 0, 0),
        jnp.sum(attn_both.astype(F32), axis=0),
        wide[2],
        wide[3],
        contract(two_both, pre_both, 0, 0),
        jnp.sum(pre_both.astype(F32), axis=0),
        contract(hidden_both, out_both, 0, 0),
        jnp.sum(out_both.astype(F32), axis=0),
    )


def shards(*args):
    pixels = args[1]
    kept = lax.axis_size("pix") * pixels.shape[2] // 2
    fits = kept <= 4096 and kept % (3 * PULL) == 0 and pixels.shape[2] % LANES == 0
    return (on_chip if fits else in_blocks)(*args)


def solution(mesh):
    lat = P("img", None, None)
    whole = P()
    return jax.shard_map(
        shards,
        mesh=mesh,
        in_specs=(lat, P("img", None, "pix"), P("img", None, "pix"), P("img", "pix"))
        + (whole,) * 15
        + (lat,),
        out_specs=(lat, lat, P("img", None, "pix")) + (whole,) * 15,
        check_vma=False,
    )
```

```python
import math

import jax
import jax.numpy as jnp
import numpy as np
from jax import lax
from jax.experimental import pallas as pl
from jax.experimental.pallas import tpu as pltpu
from jax.sharding import PartitionSpec as P

BANDS = 64
GRID = 224
EPSILON = 1e-05
FLOOR = -1e30
BLOCK = 16
LANES = 128
BF = jnp.bfloat16
F32 = jnp.float32
VM = pl.BlockSpec(memory_space=pltpu.VMEM)
HBM = pl.BlockSpec(memory_space=pltpu.HBM)
MIB = 1 << 20
MAKE = 256
SCORE = 1024
POOL = 256
PULL = 1024
WIDE = 256
STRIP = 256


def fourier_lookup():
    position = np.arange(GRID, dtype=np.float32) * np.float32(2.0 / (GRID - 1)) - np.float32(1.0)
    frequency = np.float32(1.0) + np.arange(BANDS, dtype=np.float32) * np.float32(
        (GRID / 2.0 - 1.0) / (BANDS - 1)
    )
    phases = position[None, :] * (np.float32(math.pi) * frequency)[:, None]
    waves = np.concatenate([np.sin(phases.astype(np.float64)), np.cos(phases.astype(np.float64))])
    return waves.astype(np.float32)


def split_numpy(values):
    parts = []
    for _ in range(3):
        part = values.astype(BF).astype(np.float64)
        parts.append(part)
        values = values - part
    return parts


def lookup_with_sums():
    waves = fourier_lookup().astype(BF).astype(np.float64)
    sums = split_numpy(waves.sum(axis=0)) + split_numpy((waves * waves).sum(axis=0))
    table = np.zeros((2 * BANDS + 16, GRID))
    table[: 2 * BANDS] = waves
    table[2 * BANDS : 2 * BANDS + 6] = np.stack(sums)
    return table


def split(values):
    parts = []
    for _ in range(3):
        part = values.astype(BF)
        parts.append(part)
        values = values - part.astype(F32)
    return parts


def contract(left, right, left_dim, right_dim):
    return lax.dot_general(
        left, right, (((left_dim,), (right_dim,)), ((), ())), preferred_element_type=F32
    )


def norm_stats(values, axis):
    centre = values - jnp.mean(values, axis=axis, keepdims=True)
    spread = lax.rsqrt(jnp.mean(centre * centre, axis=axis, keepdims=True) + EPSILON)
    return centre * spread, spread


def norm_back(upstream, gain, unit, spread, axis):
    inner = upstream * gain
    return spread * (
        inner
        - jnp.mean(inner, axis=axis, keepdims=True)
        - unit * jnp.mean(inner * unit, axis=axis, keepdims=True)
    )


def out(shape, dtype):
    return jax.ShapeDtypeStruct(shape, dtype)


def padded(rows, step):
    return -(-rows // step) * step


def lane_ids(shape):
    return lax.broadcasted_iota(jnp.int32, shape, len(shape) - 1)


def waves_first(values, features):
    width = values.shape[1]
    lead = features - 4 * BANDS
    at = lane_ids(values.shape)
    waves = pltpu.roll(values, width - lead, 1)
    rest = pltpu.roll(values, 4 * BANDS, 1)
    return jnp.where(at < 4 * BANDS, waves, jnp.where(at < features, rest, 0.0))


def waves_last(values, features):
    width = values.shape[1]
    lead = features - 4 * BANDS
    at = lane_ids(values.shape)
    rest = pltpu.roll(values, width - 4 * BANDS, 1)
    waves = pltpu.roll(values, lead, 1)
    return jnp.where(at < lead, rest, jnp.where(at < features, waves, 0.0))


def fold(values):
    total = values[:, :LANES]
    for start in range(LANES, values.shape[1], LANES):
        total = total + values[:, start : start + LANES]
    return total


def fold_max(values):
    total = values[:, :LANES]
    for start in range(LANES, values.shape[1], LANES):
        total = jnp.maximum(total, values[:, start : start + LANES])
    return total


def fold_rows(values):
    total = values[:8]
    for start in range(8, values.shape[0], 8):
        total = total + values[start : start + 8]
    return total


def slot_of(kept_row):
    own = kept_row.shape[1]
    shape = (own, own)
    upper = lax.broadcasted_iota(jnp.int32, shape, 0) <= lax.broadcasted_iota(jnp.int32, shape, 1)
    tall = jnp.broadcast_to(kept_row, (8, own)).astype(BF)
    rank = jnp.dot(tall, jnp.where(upper, 1.0, 0.0).astype(BF), preferred_element_type=F32)[:1]
    slot = jnp.where(kept_row > 0, rank - 1.0, -1.0)
    return slot == lax.broadcasted_iota(jnp.int32, shape, 0).astype(F32)


class Fetch:
    def __init__(self, source, target, sem):
        self.copy = pltpu.make_async_copy(source, target, sem)
        self.target = target
        self.waiting = True

    def start(self):
        self.copy.start()

    def get(self):
        if self.waiting:
            self.copy.wait()
            self.waiting = False
        return self.target


def row_of(fetch):
    return fetch.get()[...].reshape(1, -1)


def pack_kernel(pixels, coords, kept, packed, rows):
    rows[...] = jnp.zeros_like(rows)
    rows[0:3, :] = pixels.get()[:, 0, :]
    rows[3:5, :] = coords.get()[...].astype(F32)
    kept_row = kept.get()[...].astype(F32)
    rows[5:6, :] = kept_row
    slots = jnp.where(slot_of(kept_row), 1.0, 0.0).astype(BF)
    squeezed = contract(rows[...].astype(BF), slots, 1, 1).astype(BF)
    packed[...] = jnp.broadcast_to(squeezed[None], packed.shape)


def pad_rows(target, source):
    rows = source.shape[0]
    whole = rows // LANES * LANES
    target[:whole, :] = source[:whole, :]
    target[whole:, :] = jnp.zeros_like(target[whole:, :])
    target[whole:rows, :] = source[whole:, :]


def turn_blocks(target, source):
    size = source.shape[0]
    for start in range(0, source.shape[1], size):
        span = slice(start, start + size)
        target[:, span] = jnp.transpose(source[:, span])


def turn_pool(target, pool):
    count, tall = pool.shape
    turned = jnp.transpose(pool).astype(BF)
    target[...] = jnp.zeros_like(target)
    for at, start in enumerate(range(0, tall, count)):
        height = min(count, tall - start)
        target[:height, at * count : (at + 1) * count] = turned[start : start + height]


def query_kernel(
    features, latent, gain, shift, weight, bias, key_raw, in_gain, grad, down, in_shift,
    value_bias, mlp_gain, mlp_shift, up_bias, down_bias, table, up_hbm,
    early_out, absorbed_out, scorer, hidden_grad, table_kept, rows, ends, up,
    one, key, early, absorbed, sems,
):
    bring = [pltpu.make_async_copy(up_hbm, up, sems.at[0])]
    latent = latent.get()
    count, dim = latent.shape
    tall = absorbed.shape[1]
    turned, query = early.at[:, :dim], early.at[:, dim:]
    step = 32
    lat_gain, lat_shift = row_of(gain), row_of(shift)
    for start in range(0, count, step):
        unit, _ = norm_stats(latent[start : start + step, :].astype(F32), 1)
        one[start : start + step, :] = (unit * lat_gain + lat_shift).astype(BF)
    bias, weight = row_of(bias), weight.get()
    for copy in bring:
        copy.start()
    step = 256
    for start in range(0, dim, step):
        part = jnp.dot(one[...], weight[:, start : start + step], preferred_element_type=F32)
        query[:, start : start + step] = (part + bias[:, start : start + step]).astype(BF)
    turn_blocks(turned, one)
    pad_rows(key, key_raw.get())
    lifted = contract(query[...], key[...], 1, 1) * (1.0 / math.sqrt(dim))
    lifted = waves_first(lifted, features)
    absorbed[...] = lifted
    gains = gain_row(in_gain, tall, features)
    scorer[...] = (lifted * gains * math.log2(math.e)).astype(BF)
    ends[...] = jnp.zeros_like(ends)
    ends[0:1, :] = gains
    ends[1:2, :] = gain_row(in_shift, tall, features)
    grad = grad.get()
    leave = [
        pltpu.make_async_copy(early, early_out, sems.at[2]),
        pltpu.make_async_copy(absorbed, absorbed_out, sems.at[3]),
    ]
    for copy in leave:
        copy.start()
    table_kept[...] = table.get()[...]
    rows[...] = jnp.zeros_like(rows)
    for at, vector in enumerate((value_bias, mlp_gain, mlp_shift, up_bias, down_bias)):
        rows[at : at + 1, :] = row_of(vector)
    rows[5:6, :] = lat_gain
    down = down.get()
    for start in range(0, dim, step):
        part = contract(grad[...], down[start : start + step, :], 1, 1)
        hidden_grad[:, start : start + step] = part.astype(BF)
    for copy in bring + leave:
        copy.wait()


def gain_row(fetch, width, features):
    row = row_of(fetch)
    wide = jnp.concatenate([row, jnp.zeros((1, width - features), F32)], axis=1)
    return waves_first(jnp.broadcast_to(wide, (8, width)), features)[:1]


def segment_counts(segments, stop):
    return [jnp.sum(segments[index][5:6, :].astype(F32)).astype(jnp.int32) for index in range(stop)]


def forward_kernel(
    features,
    segments, scorer, hidden_grad, table, latent, value_raw, up, rows, ends, grad,
    hidden, mixed, packs, mixed_grad, lift_out, puller, unit_out, spread_out, score_out, pool_unit, stats, sums,
    placed, places, top, weight, pooled, back, mix_unit, mix_spread, value, two, pool_low,
):
    pix, _, own = segments.shape
    tall, kept = unit_out.shape
    waves = 4 * BANDS
    ones = slice(features, waves + 8)

    placed[...] = jnp.zeros_like(placed)
    offset = jnp.int32(0)
    for index, found in enumerate(segment_counts(segments, pix)):
        wide = jnp.concatenate([segments[index].astype(F32), jnp.zeros((8, LANES), F32)], axis=1)
        inside = lax.rem(offset, LANES)
        base = pl.multiple_of(jnp.minimum(offset - inside, kept), LANES)
        placed[:, pl.ds(base, own + LANES)] += pltpu.roll(wide, inside, 1)
        offset = offset + found
    places[...] = lax.broadcasted_iota(jnp.int32, places.shape, 0).astype(F32).astype(BF)
    unit_out[waves + 16 :, :] = jnp.zeros((tall - waves - 16, kept), BF)
    top[...] = jnp.full_like(top, FLOOR)

    for start in range(0, kept, MAKE):
        step = MAKE
        lanes = slice(start, start + step)
        raw = placed[:, lanes]
        column = jnp.concatenate([places[...]] * (step // LANES), axis=1)
        one, none = jnp.ones((), BF), jnp.zeros((), BF)
        row_hot = jnp.where(column == raw[3:4].astype(BF), one, none)
        col_hot = jnp.where(column == raw[4:5].astype(BF), one, none)
        row_waves = jnp.dot(table[...], row_hot, preferred_element_type=F32)
        col_waves = jnp.dot(table[...], col_hot, preferred_element_type=F32)
        at = lax.broadcasted_iota(jnp.int32, raw.shape, 0)
        position = (raw * (2.0 / (GRID - 1)) - 1.0).astype(BF).astype(F32)
        extra = jnp.where(at < 3, raw, jnp.where(at < 5, position, 0.0))
        both = row_waves[2 * BANDS :] + col_waves[2 * BANDS :]
        mean = (
            jnp.sum(both[0:3], axis=0, keepdims=True) + jnp.sum(extra, axis=0, keepdims=True)
        ) * (1.0 / features)
        square = (
            jnp.sum(both[3:6], axis=0, keepdims=True) + jnp.sum(extra * extra, axis=0, keepdims=True)
        ) * (1.0 / features)
        spread = lax.rsqrt(jnp.maximum(square - mean * mean, 0.0) + EPSILON)
        centre = mean * spread
        spread_out[:, lanes] = jnp.broadcast_to(spread, (8, step))
        for piece, low in (
            (row_waves[:BANDS], 0),
            (col_waves[:BANDS], BANDS),
            (row_waves[BANDS : 2 * BANDS], 2 * BANDS),
            (col_waves[BANDS : 2 * BANDS], 3 * BANDS),
        ):
            unit_out[low : low + BANDS, lanes] = (piece * spread - centre).astype(BF)
        tail = jnp.where(at < features - waves, extra * spread - centre, 1.0)
        tail = jnp.concatenate([tail, jnp.zeros((8, step), F32)], axis=0)
        unit_out[waves : waves + 16, lanes] = tail.astype(BF)
    for start in range(0, kept, SCORE):
        lanes = slice(start, start + SCORE)
        score = jnp.dot(scorer[...], unit_out[:, lanes], preferred_element_type=F32)
        score_out[:, lanes] = score
        top[...] = jnp.maximum(top[...], fold_max(score))
    peak = jnp.max(top[...], axis=1, keepdims=True)
    top[...] = jnp.broadcast_to(peak, top.shape)
    for start in range(0, kept, POOL):
        lanes = slice(start, start + POOL)
        weight[:, lanes] = jnp.exp2(score_out[:, lanes] - top[:, :1]).astype(BF)
    pooled[...] = contract(weight[...], unit_out[...], 1, 1)
    total = pooled[:, features : features + 1]
    pool_unit[...] = pooled[...] * (1.0 / total)
    gains, shifts = ends[0:1, :], ends[1:2, :]
    count, dim = mixed.shape
    value_bias, gain, shift, up_bias = (rows[at : at + 1, :] for at in range(4))
    hidden_turned, two_turned, pre_grad, attn_grad, kept_grad = (
        packs.at[:, at * dim : (at + 1) * dim] for at in range(5)
    )
    pool = waves_last(pool_unit[...] * gains + shifts, features)
    pool_low[...] = pool.astype(BF)
    turn_pool(packs.at[:, 5 * dim :], pool)

    latent = latent.get()
    pad_rows(value, value_raw.get())
    wide = WIDE
    for start in range(0, dim, wide):
        span = slice(start, start + wide)
        attn = jnp.dot(pool_low[...], value[:, span], preferred_element_type=F32) + value_bias[:, span]
        mixed[:, span] = latent[:, span].astype(F32) + attn
    low = 32
    for start in range(0, count, low):
        span = slice(start, start + low)
        unit, spread = norm_stats(mixed[span, :], 1)
        mix_unit[span, :] = unit
        mix_spread[span, :] = jnp.broadcast_to(spread, (low, LANES))
        two[span, :] = (unit * gain + shift).astype(BF)
    turn_blocks(two_turned, two)
    for start in range(0, dim, wide):
        span = slice(start, start + wide)
        act = jnp.dot(two[...], up[:, span], preferred_element_type=F32) + up_bias[:, span]
        half = 0.5 * (1.0 + lax.erf(act * (1.0 / math.sqrt(2.0))))
        active = act * half
        active = active.astype(BF)
        hidden[:, span] = active
        hidden_turned[:, span] = jnp.transpose(active)
        slope = half + act * jnp.exp(-0.5 * act * act) * (1.0 / math.sqrt(2.0 * math.pi))
        pre_grad[:, span] = (hidden_grad[:, span].astype(F32) * slope).astype(BF)
    for start in range(0, dim, wide):
        span = slice(start, start + wide)
        back[:, span] = contract(pre_grad[...], up[span, :], 1, 1)
    grad = grad.get()
    kept_grad[...] = grad[...]
    gain_sum = jnp.zeros((8, dim), F32)
    shift_sum = jnp.zeros((8, dim), F32)
    for start in range(0, count, low):
        span = slice(start, start + low)
        upstream = back[span, :]
        unit = mix_unit[span, :]
        full = grad[span, :].astype(F32) + norm_back(upstream, gain, unit, mix_spread[span, :1], 1)
        mixed_grad[span, :] = full
        attn_grad[span, :] = full.astype(BF)
        gain_sum = gain_sum + fold_rows(upstream * unit)
        shift_sum = shift_sum + fold_rows(upstream)
    sums[0:1, :] = jnp.sum(gain_sum, axis=0, keepdims=True)
    sums[1:2, :] = jnp.sum(shift_sum, axis=0, keepdims=True)
    lifted = waves_first(contract(attn_grad[...], value[...], 1, 1), features)
    lift_out[...] = lifted
    pulled = (lifted * gains).astype(BF)
    at = lane_ids(pulled.shape)
    inside = jnp.where(at < features, pulled.astype(F32) * pool_unit[...], 0.0)
    delta = jnp.sum(inside, axis=1, keepdims=True)
    for lane, part in enumerate(split(-delta)):
        pulled = jnp.where(at == features + lane, part, pulled)
    puller[...] = pulled
    at = lane_ids(stats.shape)
    stats[...] = jnp.where(at == 0, peak + jnp.log2(total), delta)


def write_vectors(array, lines, vectors):
    width = array.shape[0]
    lines[...] = jnp.zeros_like(lines)
    row = 0
    for vector in vectors:
        for part in split(vector):
            for start in range(0, vector.shape[1], width):
                lines[row : row + 1, :] = part[:, start : start + width].astype(F32)
                row += 1
    array[LANES : LANES + lines.shape[0], array.shape[1] - width :] = lines[...].astype(BF)


def read_vectors(array, dim, number):
    width = array.shape[0]
    turns = dim // width
    high = padded(3 * number * turns, 16)
    lines = array[LANES : LANES + high, array.shape[1] - width :].astype(F32)
    vectors = []
    for at in range(number):
        first = 3 * at * turns
        total = sum(lines[first + part * turns : first + (part + 1) * turns] for part in range(3))
        vectors.append(jnp.concatenate([total[turn : turn + 1] for turn in range(turns)], axis=1))
    return vectors


def pull_kernel(
    features,
    segments, kept_row, absorbed, lifted, puller, unit_in, spread_in, score, pool_unit, stats,
    key_raw, sums, ends, query_weight, latent, rows, mixed_grad, early,
    late, color_grad, latent_grad,
    pulls, pooled, key, back, lines, early_sem,
):
    count, dim = pooled.shape[0], key.shape[1]
    own = segments.shape[2]
    tall, kept = unit_in.shape
    bring = pltpu.make_async_copy(early, late.at[:, dim : 3 * dim], early_sem)
    bring.start()
    waves = 4 * BANDS
    def shares(lanes):
        inner = jnp.dot(puller[...], unit_in[:, lanes], preferred_element_type=F32)
        prob = jnp.exp2(score[:, lanes] - stats[:, :1])
        return inner, prob, (prob * inner).astype(BF)

    for start in range(0, kept, PULL):
        lanes = slice(start, start + PULL)
        pulls[:, lanes] = shares(lanes)[2]
    pooled[...] = contract(pulls[...], unit_in[...], 1, 1)
    gains, shifts = ends[0:1, :], ends[1:2, :]
    kept_row, key_raw, query_weight = kept_row.get(), key_raw.get(), query_weight.get()
    latent, absorbed = latent.get(), absorbed.get()

    mine = lax.axis_index("pix")
    offset = jnp.int32(0)
    for index, found in enumerate(segment_counts(segments, segments.shape[0])):
        offset = offset + jnp.where(index < mine, found, 0)
    inside = lax.rem(offset, LANES)
    base = pl.multiple_of(jnp.minimum(offset - inside, kept - own - LANES), LANES)
    inside = offset - base
    lanes = pl.ds(base, own + LANES)
    inner, prob, score_grad = shares(lanes)
    tilt = score_grad.astype(F32) * score[:, lanes] * math.log(2.0) + prob * (inner + stats[:, 1:2])
    tilt = jnp.sum(tilt, axis=0, keepdims=True) * (1.0 / features)
    factors = []
    for held in (absorbed, lifted):
        scaled = held[...] * gains
        at = lane_ids((count, LANES))
        corner = jnp.where(at == 3, jnp.sum(scaled, axis=1, keepdims=True), scaled[:, waves : waves + LANES])
        factors.append(jnp.transpose(corner)[:8].astype(BF))
    both = jnp.concatenate([score_grad, prob.astype(BF)], axis=0)
    terms = jnp.dot(jnp.concatenate(factors, axis=1), both, preferred_element_type=F32)
    unit = unit_in[waves : waves + 16, lanes].astype(F32)[:8]
    colors = spread_in[:, lanes] * (terms - terms[3:4] * (1.0 / features) - unit * tilt)
    window = pltpu.roll(colors, own + LANES - inside, 1)[:, :own]
    slots = jnp.where(slot_of(kept_row[...].astype(F32)), 1.0, 0.0)
    spread_back = jnp.dot(window, slots, precision=lax.Precision.HIGHEST, preferred_element_type=F32)
    color_grad[:, 0, :] = spread_back[:3]

    held = pooled[...]
    total = held[:, features : features + 1]
    pool = waves_last(held * gains + shifts * total, features)
    turn_pool(late.at[:, 3 * dim :], pool)
    pool = pool.astype(BF)
    pad_rows(key, key_raw)
    gain_sum = absorbed[...] * held + lifted[...] * pool_unit[...]
    shift_sum = absorbed[...] * total + lifted[...]
    vectors = []
    for found in (gain_sum, shift_sum):
        flat = jnp.sum(fold_rows(found), axis=0, keepdims=True)
        flat = waves_last(jnp.broadcast_to(flat, (8, tall)), features)[:1]
        vectors.append(jnp.concatenate([flat, jnp.zeros((1, dim - tall), F32)], axis=1))
    vectors += [sums[0:1, :], sums[1:2, :]]
    wide = WIDE
    for start in range(0, dim, wide):
        span = slice(start, start + wide)
        part = jnp.dot(pool, key[:, span], preferred_element_type=F32) * (1.0 / math.sqrt(dim))
        late[:, span] = part.astype(BF)
    for start in range(0, dim, wide):
        span = slice(start, start + wide)
        back[:, span] = contract(late[:, :dim], query_weight[span, :], 1, 1)
    low = 32
    gain = rows[5:6, :]
    gain_sum = jnp.zeros((8, dim), F32)
    shift_sum = jnp.zeros((8, dim), F32)
    for start in range(0, count, low):
        span = slice(start, start + low)
        unit, spread = norm_stats(latent[span, :].astype(F32), 1)
        upstream = back[span, :]
        latent_grad[span, :] = mixed_grad[span, :] + norm_back(upstream, gain, unit, spread, 1)
        gain_sum = gain_sum + fold_rows(upstream * unit)
        shift_sum = shift_sum + fold_rows(upstream)
    vectors += [jnp.sum(gain_sum, axis=0, keepdims=True), jnp.sum(shift_sum, axis=0, keepdims=True)]
    write_vectors(late, lines, vectors)
    bring.wait()


class Leaving:
    def __init__(self, buffers, sems):
        self.buffers, self.sems, self.flying, self.turn = buffers, sems, {}, 0

    def free(self):
        slot = self.turn % self.buffers.shape[0]
        if slot in self.flying:
            self.flying[slot].wait()
        return self.buffers.at[slot]

    def send(self, target):
        slot = self.turn % self.buffers.shape[0]
        self.turn += 1
        self.flying[slot] = pltpu.make_async_copy(self.buffers.at[slot], target, self.sems.at[slot])
        self.flying[slot].start()

    def end(self):
        for copy in self.flying.values():
            copy.wait()


def parts_of(ref, dim):
    squares = ref.shape[1] // dim
    parts = [ref.at[:, at * dim : (at + 1) * dim] for at in range(squares)]
    return parts + ([ref.at[:, squares * dim :]] if ref.shape[1] % dim else [])


def products(leaving, left, left_far, right, right_far, target, bias):
    count = left.shape[0]
    size = leaving.buffers.shape[1]
    for start in range(0, left.shape[1], size):
        buffer = leaving.free()
        at, inner = start // count * count, start % count
        rows, lanes = slice(inner, inner + size), slice(at, at + count)
        strip = jnp.concatenate([left[rows, lanes], left_far[rows, lanes]], axis=1)
        if bias is not None and start == 0:
            strip = jnp.concatenate([strip, jnp.ones((16, 2 * count), BF)], axis=0)
        found = jnp.dot(strip, jnp.concatenate([right[...], right_far[...]], axis=0), preferred_element_type=F32)
        buffer[...] = found[:size]
        if bias is not None and start == 0:
            bias[...] = found[size]
        leaving.send(target.at[start : start + size, :])


def short_product(held, left, left_far, right, right_far, bias, scale):
    features, count = held.shape[0], left.shape[0]
    pieces = []
    for at, start in enumerate(range(0, features, count)):
        height = min(count, padded(features - start, 16))
        lanes = slice(at * count, (at + 1) * count)
        pieces.append(jnp.concatenate([left[:height, lanes], left_far[:height, lanes]], axis=1))
    high = sum(piece.shape[0] for piece in pieces)
    pieces.append(jnp.ones((16, 2 * count), BF))
    both = jnp.concatenate([right[...], right_far[...]], axis=0)
    found = jnp.dot(jnp.concatenate(pieces, axis=0), both, preferred_element_type=F32)
    held[...] = found[:features] if scale is None else found[:features] * scale
    if bias is not None:
        bias[...] = found[high]


def late_kernel(
    features,
    packs, packs_far, color_grad, latent_grad,
    color_out, latent_out, down_out, down_bias, up_out, up_bias, value_out, value_bias,
    buffers, held, sems, held_sem, out_sems,
):
    dim = down_out.shape[1]
    hidden, two, pre, attn, grad, pool = parts_of(packs, dim)
    hidden_far, two_far, pre_far, attn_far, grad_far, pool_far = parts_of(packs_far, dim)
    first = [
        pltpu.make_async_copy(latent_grad, latent_out, out_sems.at[0]),
        pltpu.make_async_copy(color_grad, color_out, out_sems.at[1]),
    ]
    for copy in first:
        copy.start()
    leaving = Leaving(buffers, sems)
    products(leaving, hidden, hidden_far, grad, grad_far, down_out, down_bias)
    short_product(held, pool, pool_far, attn, attn_far, value_bias, None)
    leave = pltpu.make_async_copy(held, value_out, held_sem)
    leave.start()
    products(leaving, two, two_far, pre, pre_far, up_out, up_bias)
    for copy in first:
        copy.wait()
    leave.wait()
    leaving.end()


def last_kernel(
    features,
    late, late_far, hidden, mixed, down, rows, _,
    encoded_out, query_out, query_bias, key_out, lat_gain, lat_shift, mlp_gain, mlp_shift, in_gain, in_shift,
    buffers, held, encoded, sems, held_sem, encoded_sem,
):
    dim = query_out.shape[1]
    grad, one, query, pool = parts_of(late, dim)
    grad_far, one_far, query_far, pool_far = parts_of(late_far, dim)
    leaving = Leaving(buffers, sems)
    products(leaving, one, one_far, grad, grad_far, query_out, query_bias)
    short_product(held, pool, pool_far, query, query_far, None, 1.0 / math.sqrt(dim))
    short = pltpu.make_async_copy(held, key_out, held_sem)
    short.start()
    for start in range(0, dim, WIDE):
        span = slice(start, start + WIDE)
        part = jnp.dot(hidden[...], down[:, span], preferred_element_type=F32)
        encoded[:, span] = (mixed[:, span] + part + rows[4:5, span]).astype(BF)
    leave = pltpu.make_async_copy(encoded, encoded_out, encoded_sem)
    leave.start()
    pairs = zip(read_vectors(late, dim, 6), read_vectors(late_far, dim, 6))
    places = (in_gain, in_shift, mlp_gain, mlp_shift, lat_gain, lat_shift)
    for place, (own, far) in zip(places, pairs):
        place[...] = (own + far)[0, : place.shape[0]]
    leaving.end()
    short.wait()
    leave.wait()


def call(body, outs, args, fetched, scratch, vmem, flops, moved, unread=()):
    places = [at for at in range(len(args)) if at in fetched]
    buffers = [pltpu.VMEM(args[at].shape, args[at].dtype) for at in places]
    shapes = tuple(pltpu.HBM(shape, dtype) if place is HBM else out(shape, dtype) for shape, dtype, place in outs)

    def whole(*refs):
        sources, rest = list(refs[: len(args)]), refs[len(args) :]
        targets = ()
        if places:
            targets, sems, rest = rest[-len(buffers) - 1 : -1], rest[-1], rest[: -len(buffers) - 1]
        for slot, (at, target) in enumerate(zip(places, targets)):
            sources[at] = Fetch(sources[at], target, sems.at[slot])
            sources[at].start()
        body(*sources, *rest)
        for at in places:
            sources[at].get()

    return pl.pallas_call(
        whole,
        out_shape=shapes if len(shapes) > 1 else shapes[0],
        in_specs=tuple(HBM if at in fetched or at in unread else VM for at in range(len(args))),
        out_specs=tuple(place for _, _, place in outs) if len(outs) > 1 else outs[0][2],
        scratch_shapes=list(scratch) + buffers + ([pltpu.SemaphoreType.DMA((len(places),))] if places else []),
        compiler_params=pltpu.CompilerParams(vmem_limit_bytes=vmem * MIB),
        cost_estimate=pl.CostEstimate(flops=flops, bytes_accessed=moved, transcendentals=0),
    )(*(pltpu.with_memory_space_constraint(arg, pltpu.HBM) if at in fetched or at in unread else arg for at, arg in enumerate(args)))


def on_chip(
    latents, pixels, coords, kept_mask, lat_gain, lat_shift, query_weight, query_bias, in_gain, in_shift,
    key_weight, value_weight, value_bias, mlp_gain, mlp_shift, up_weight, up_bias, down_weight, down_bias,
    cotangent,
):
    pix = lax.axis_size("pix")
    own = pixels.shape[2]
    kept = pix * own // 2
    _, count, dim = latents.shape
    features = in_gain.shape[0]
    tall = padded(features, LANES)
    latent, out_grad = latents[0], cotangent[0]
    swap = [(0, 1), (1, 0)]

    def other(value):
        return lax.ppermute(value, "img", swap)

    packed = call(
        pack_kernel, [((pix, 8, own), BF, VM)], (pixels.transpose(1, 0, 2), coords[0], kept_mask), (0, 1, 2),
        [pltpu.VMEM((8, own), F32)], 8, 4 * 8 * own * own, 16 * 8 * own,
    )
    segments = lax.all_to_all(packed, "pix", 0, 0)

    table = jnp.asarray(lookup_with_sums(), BF)
    wide = pltpu.VMEM((tall, dim), BF)
    early, absorbed, scorer, hidden_grad, table_kept, rows, ends, up_kept = call(
        lambda *refs: query_kernel(features, *refs),
        [
            ((count, 2 * dim), BF, HBM), ((count, tall), F32, HBM), ((count, tall), BF, VM), ((count, dim), BF, VM),
            (table.shape, BF, VM), ((8, dim), F32, VM), ((8, tall), F32, VM), ((dim, dim), BF, VM),
        ],
        (
            latent, lat_gain, lat_shift, query_weight, query_bias, key_weight, in_gain, out_grad, down_weight,
            in_shift, value_bias, mlp_gain, mlp_shift, up_bias, down_bias, table, up_weight,
        ),
        tuple(range(16)),
        [
            pltpu.VMEM((count, dim), BF), wide, pltpu.VMEM((count, 2 * dim), BF), pltpu.VMEM((count, tall), F32),
            pltpu.SemaphoreType.DMA((4,)),
        ],
        16, 4 * count * dim * dim + 2 * count * dim * tall, 8 * MIB, (16,),
    )

    narrow = pltpu.VMEM((count, LANES), F32)
    area = pltpu.VMEM((count, dim), F32)
    low = pltpu.VMEM((count, dim), BF)
    spare = 512
    (
        hidden, mixed, packs, mixed_grad, lifted, puller, unit_in, spread_in, score, pool_unit, stats, sums,
    ) = call(
        lambda *refs: forward_kernel(features, *refs),
        [
            ((count, dim), BF, VM), ((count, dim), F32, VM), ((count, 5 * dim + spare), BF, VM),
            ((count, dim), F32, VM),
            ((count, tall), F32, VM), ((count, tall), BF, VM), ((tall, kept), BF, VM), ((8, kept), F32, VM),
            ((count, kept), F32, VM), ((count, tall), F32, VM), ((count, LANES), F32, VM), ((8, dim), F32, VM),
        ],
        (
            segments, scorer, hidden_grad, table_kept, latent, value_weight, up_kept, rows, ends, out_grad,
        ),
        (4, 5, 9),
        [
            pltpu.VMEM((8, kept + own + LANES), F32), pltpu.VMEM((GRID, LANES), BF), narrow,
            pltpu.VMEM((count, kept), BF), pltpu.VMEM((count, tall), F32), area, area, narrow, wide, low,
            pltpu.VMEM((count, tall), BF),
        ],
        20, 6 * count * dim * dim + 4 * count * dim * tall + 6 * kept * count * tall, 8 * MIB,
    )

    late, color_grad, latent_grad = call(
        lambda *refs: pull_kernel(features, *refs),
        [
            ((count, 3 * dim + spare), BF, VM), ((3, 1, own), F32, VM), ((count, dim), F32, VM),
        ],
        (
            segments, kept_mask, absorbed, lifted, puller, unit_in, spread_in, score, pool_unit, stats, key_weight,
            sums, ends, query_weight, latent, rows, mixed_grad, early,
        ),
        (1, 2, 10, 13, 14),
        [
            pltpu.VMEM((count, kept), BF), pltpu.VMEM((count, tall), F32), wide, area, pltpu.VMEM((80, count), F32),
            pltpu.SemaphoreType.DMA(()),
        ],
        16, 2 * count * dim * dim + 4 * kept * count * tall, 8 * MIB, (17,),
    )

    packs_far = other(packs)
    late_far = other(late)
    square = ((dim, dim), F32, HBM)
    slab = ((features, dim), F32, HBM)
    line = ((dim,), F32, VM)
    short = ((features,), F32, VM)
    slots = [
        pltpu.VMEM((4, STRIP, dim), F32), pltpu.VMEM((features, dim), F32),
    ]
    sems = [pltpu.SemaphoreType.DMA((4,)), pltpu.SemaphoreType.DMA(())]
    (
        color_grad, latent_grad, down_weight_grad, down_bias_grad, up_weight_grad, up_bias_grad, value_weight_grad,
        value_bias_grad,
    ) = call(
        lambda *refs: late_kernel(features, *refs),
        [((3, 1, own), F32, HBM), ((count, dim), F32, HBM), square, line, square, line, slab, line],
        (packs, packs_far, color_grad, latent_grad), (),
        slots + sems + [pltpu.SemaphoreType.DMA((2,))], 12, 8 * count * dim * dim + 4 * count * dim * tall, 10 * MIB,
    )
    (
        encoded, query_weight_grad, query_bias_grad, key_weight_grad, lat_gain_grad, lat_shift_grad, mlp_gain_grad,
        mlp_shift_grad, in_gain_grad, in_shift_grad,
    ) = call(
        lambda *refs: last_kernel(features, *refs),
        [((count, dim), BF, HBM), square, line, slab, line, line, line, line, short, short],
        (
            late, late_far, hidden, mixed, down_weight, rows,
            down_weight_grad,
        ),
        (), slots + [low] + sems + [pltpu.SemaphoreType.DMA(())], 12, 4 * count * dim * dim + 4 * count * dim * tall, 6 * MIB, (6,),
    )

    return (
        encoded[None], latent_grad[None], color_grad.transpose(1, 0, 2), lat_gain_grad, lat_shift_grad,
        query_weight_grad, query_bias_grad, in_gain_grad, in_shift_grad, key_weight_grad, value_weight_grad,
        value_bias_grad, mlp_gain_grad, mlp_shift_grad, up_weight_grad, up_bias_grad, down_weight_grad, down_bias_grad,
    )


def in_blocks(
    latents,
    pixels,
    coords,
    kept_mask,
    lat_gain,
    lat_shift,
    query_weight,
    query_bias,
    in_gain,
    in_shift,
    key_weight,
    value_weight,
    value_bias,
    mlp_gain,
    mlp_shift,
    up_weight,
    up_bias,
    down_weight,
    down_bias,
    cotangent,
):
    pix = lax.axis_size("pix")
    mine = lax.axis_index("pix")
    own = pixels.shape[2]
    packed = jnp.concatenate(
        [
            pixels[0].astype(BF),
            coords[0].astype(BF),
            kept_mask.astype(BF),
            jnp.zeros((2, own), BF),
        ],
        axis=0,
    )
    gathered = lax.all_to_all(jnp.broadcast_to(packed[None], (pix,) + packed.shape), "pix", 0, 0)
    every = gathered.transpose(1, 0, 2).reshape(packed.shape[0], pix * own)
    swap = [(0, 1), (1, 0)]

    def other(value):
        return lax.ppermute(value, "img", swap)

    root = math.sqrt(latents.shape[2])
    latent = latents[0].astype(F32)
    lat_unit, lat_spread = norm_stats(latent, 1)
    norm_one = (lat_unit * lat_gain + lat_shift).astype(BF)
    query = (jnp.dot(norm_one, query_weight, preferred_element_type=F32) + query_bias).astype(BF)
    absorbed = (contract(query, key_weight, 1, 1) * (1.0 / root)).astype(BF)

    waves = jnp.asarray(fourier_lookup(), BF)
    places = jnp.arange(GRID, dtype=F32)[:, None]

    def features(part):
        cells = part[3:5].astype(F32)
        position = (cells * (2.0 / (GRID - 1)) - 1.0).astype(BF)
        row_waves = jnp.dot(waves, (cells[0:1] == places).astype(BF), preferred_element_type=F32).astype(BF)
        col_waves = jnp.dot(waves, (cells[1:2] == places).astype(BF), preferred_element_type=F32).astype(BF)
        table = jnp.concatenate(
            [part[0:3], position, row_waves[:BANDS], col_waves[:BANDS], row_waves[BANDS:], col_waves[BANDS:]],
            axis=0,
        ).astype(F32)
        unit, spread = norm_stats(table, 0)
        x_in = (unit * in_gain[:, None] + in_shift[:, None]).astype(BF)
        score = jnp.dot(absorbed, x_in, preferred_element_type=F32)
        return unit, spread, x_in, jnp.where(part[5:6] > 0, score, FLOOR), part[5:6] > 0

    def pool(part, feats):
        unit, spread, x_in, score, live = feats
        top = jnp.max(score, axis=1, keepdims=True)
        weight = jnp.where(live, jnp.exp(score - top), 0.0)
        return top, jnp.sum(weight, axis=1, keepdims=True), contract(weight.astype(BF), x_in, 1, 1)

    blocks = max(1, pix // BLOCK)
    parts = every.reshape(packed.shape[0], blocks, -1).transpose(1, 0, 2)
    if blocks == 1:
        feats = features(parts[0])
        row_top, row_total, pooled = pool(parts[0], feats)
    else:

        def merge(carry, part):
            top, total, sums = pool(part, features(part))
            new_top = jnp.maximum(carry[0], top)
            old_scale, new_scale = jnp.exp(carry[0] - new_top), jnp.exp(top - new_top)
            return (
                new_top,
                carry[1] * old_scale + total * new_scale,
                carry[2] * old_scale + sums * new_scale,
            ), None

        start = (
            jnp.full((latent.shape[0], 1), FLOOR, F32),
            jnp.zeros((latent.shape[0], 1), F32),
            jnp.zeros((latent.shape[0], in_gain.shape[0]), F32),
        )
        row_top, row_total, pooled = lax.scan(merge, start, parts)[0]
    pooled = pooled / row_total
    pooled_low = pooled.astype(BF)
    attn = jnp.dot(pooled_low, value_weight, preferred_element_type=F32) + value_bias
    mixed = latent + attn
    mix_unit, mix_spread = norm_stats(mixed, 1)
    norm_two = (mix_unit * mlp_gain + mlp_shift).astype(BF)
    pre_act = jnp.dot(norm_two, up_weight, preferred_element_type=F32) + up_bias
    half_erf = 0.5 * (1.0 + lax.erf(pre_act * (1.0 / math.sqrt(2.0))))
    hidden = (pre_act * half_erf).astype(BF)
    encoded = (
        mixed + jnp.dot(hidden, down_weight, preferred_element_type=F32) + down_bias
    ).astype(BF)

    out_grad = cotangent[0]
    out_grad_full = out_grad.astype(F32)
    hidden_grad = contract(out_grad, down_weight, 1, 1)
    slope = half_erf + pre_act * jnp.exp(-0.5 * pre_act * pre_act) * (1.0 / math.sqrt(2.0 * math.pi))
    pre_grad = (hidden_grad * slope).astype(BF)
    norm_two_grad = contract(pre_grad, up_weight, 1, 1)
    mixed_grad = out_grad_full + norm_back(norm_two_grad, mlp_gain, mix_unit, mix_spread, 1)
    attn_grad = mixed_grad.astype(BF)

    lifted = contract(attn_grad, value_weight, 1, 1).astype(BF)
    row_delta = jnp.sum(lifted.astype(F32) * pooled, axis=1, keepdims=True)

    def pull(part, feats):
        unit, spread, x_in, score, live = feats
        prob = jnp.where(live, jnp.exp(score - row_top), 0.0) / row_total
        score_grad = (prob * (jnp.dot(lifted, x_in, preferred_element_type=F32) - row_delta)).astype(BF)
        score_pool = contract(score_grad, x_in, 1, 1)
        x_in_grad = contract(absorbed, score_grad, 0, 0) + contract(lifted, prob.astype(BF), 0, 0)
        gain_part = jnp.sum(x_in_grad * unit, axis=1)
        shift_part = jnp.sum(x_in_grad, axis=1)
        colour_part = norm_back(x_in_grad, in_gain[:, None], unit, spread, 0)[:3]
        return score_pool, gain_part, shift_part, colour_part

    if blocks == 1:
        score_pool, in_gain_grad, in_shift_grad, all_colors = pull(parts[0], feats)
    else:

        def gather_up(carry, part):
            found = pull(part, features(part))
            return tuple(kept + new for kept, new in zip(carry, found[:3])), found[3]

        start = (
            jnp.zeros((latent.shape[0], in_gain.shape[0]), F32),
            jnp.zeros_like(in_gain),
            jnp.zeros_like(in_shift),
        )
        (score_pool, in_gain_grad, in_shift_grad), stacked = lax.scan(gather_up, start, parts)
        all_colors = stacked.transpose(1, 0, 2).reshape(3, -1)
    color_grad = lax.dynamic_slice(all_colors, (0, mine * own), (3, own))
    score_pool_low = score_pool.astype(BF)
    query_grad = (
        jnp.dot(score_pool_low, key_weight, preferred_element_type=F32) * (1.0 / root)
    ).astype(BF)
    norm_one_grad = contract(query_grad, query_weight, 1, 1)
    latent_grad = mixed_grad + norm_back(norm_one_grad, lat_gain, lat_unit, lat_spread, 1)

    def both(value):
        return jnp.concatenate([value, other(value)], axis=0)

    out_both = both(out_grad)
    hidden_both = both(hidden)
    two_both = both(norm_two)
    pre_both = both(pre_grad)
    attn_both = both(attn_grad)
    one_both = both(norm_one)
    query_both = both(query)
    query_grad_both = both(query_grad)
    pool_both = both(pooled_low)
    score_both = both(score_pool_low)
    wide = jnp.stack(
        [
            jnp.sum(norm_one_grad * lat_unit, axis=0),
            jnp.sum(norm_one_grad, axis=0),
            jnp.sum(norm_two_grad * mix_unit, axis=0),
            jnp.sum(norm_two_grad, axis=0),
        ]
    )
    narrow = jnp.stack([in_gain_grad, in_shift_grad])
    wide = wide + other(wide)
    narrow = narrow + other(narrow)
    return (
        encoded[None],
        latent_grad[None],
        color_grad[None],
        wide[0],
        wide[1],
        contract(one_both, query_grad_both, 0, 0),
        jnp.sum(query_grad_both.astype(F32), axis=0),
        narrow[0],
        narrow[1],
        contract(score_both, query_both, 0, 0) * (1.0 / root),
        contract(pool_both, attn_both, 0, 0),
        jnp.sum(attn_both.astype(F32), axis=0),
        wide[2],
        wide[3],
        contract(two_both, pre_both, 0, 0),
        jnp.sum(pre_both.astype(F32), axis=0),
        contract(hidden_both, out_both, 0, 0),
        jnp.sum(out_both.astype(F32), axis=0),
    )


def shards(*args):
    pixels = args[1]
    kept = lax.axis_size("pix") * pixels.shape[2] // 2
    fits = kept <= 4096 and kept % (3 * PULL) == 0 and pixels.shape[2] % LANES == 0
    return (on_chip if fits else in_blocks)(*args)


def solution(mesh):
    lat = P("img", None, None)
    whole = P()
    return jax.shard_map(
        shards,
        mesh=mesh,
        in_specs=(lat, P("img", None, "pix"), P("img", None, "pix"), P("img", "pix"))
        + (whole,) * 15
        + (lat,),
        out_specs=(lat, lat, P("img", None, "pix")) + (whole,) * 15,
        check_vma=False,
    )
```
